32 devices in a mesh: groups: 2 (over x), tok: 16 (over z, y, core).
Axes of the slice: x: 2, y: 2, z: 4, core: 2. Of those that a mesh axis runs over, the one named last changes fastest.
Arguments:
- latents: bfloat16 [2304, 1536], P(('groups', 'tok')), parts along dimension 0, may hold values from -6 to 6
- fresh_noise: bfloat16 [2304, 1536], P(('groups', 'tok')), parts along dimension 0, may hold values from -6 to 6
- levels: int32 [4], replicated, may hold values from 50 to 996, as said below
- time_weight: bfloat16 [256, 3072], replicated, may hold values from -0.375 to 0.375
- w_query: bfloat16 [1536, 768], replicated, may hold values from -1 to 1
- w_key: bfloat16 [1536, 768], replicated, may hold values from -10 to 10
- w_value: bfloat16 [1536, 768], replicated, may hold values from -0.15625 to 0.15625
- w_out: bfloat16 [768, 1536], replicated, may hold values from -0.21875 to 0.21875
Outputs:
- stepped: bfloat16 [2, 2304, 1536], P(None, ('groups', 'tok')), parts along dimension 1
- velocity: bfloat16 [2, 2304, 1536], P(None, ('groups', 'tok')), parts along dimension 1
The draws below stay inside these ranges and needn't reach their ends.
There are 2 independent parts, one for each index of `groups`. The reference program is written for one: setup_inputs(seed, part) draws one part's arguments, and reference() takes and returns one part's arrays. A program takes and returns all parts, laid end to end along the dimension named above; an argument that names none is the same for every part. Nothing has to cross between parts.
Inputs may be any that keep to these rules, and one draw needn't show every extreme that they name: `levels`: strictly increasing over sections.
All inputs are finite; a program needn't handle non-finite values.
Results may differ from the reference program's by a relative error of at most 0.0095.
Values may be sent and summed in bfloat16 or wider, within the bound.
No kernel may reach another device: no remote copies, remote signals or barrier semaphores. Data moves between devices by JAX's collectives and lax.ppermute only.
A program may use at most 128 MiB of HBM per device.

```python
import math
import jax
import jax.numpy as jnp
from jax import lax

D = 1536
HEADS = 6
HEAD_DIM = 128
TFREQ = 256
SECTIONS = 4
TOKENS = 1152


def query_key_pair(key):
    first_key, second_key = jax.random.split(jax.random.fold_in(key, 17))
    query_part = jax.random.normal(first_key, (D, HEADS * HEAD_DIM), jnp.float32) / math.sqrt(D)
    key_part = jax.random.normal(second_key, (D, HEADS * HEAD_DIM), jnp.float32) / math.sqrt(D)
    return (query_part, key_part)


def draw_w_query(key, part):
    return query_key_pair(key)[0].astype(jnp.bfloat16)


def draw_w_key(key, part):
    return query_key_pair(key)[1].astype(jnp.bfloat16)


def draw_levels(key, part):
    increments = jax.random.randint(jax.random.fold_in(key, 5), (SECTIONS - 1,), 1, 100).astype(jnp.int32)
    running = jnp.cumsum(increments).astype(jnp.int32)
    total_count = running[-1]
    inner = 50 + 946 * running // total_count
    return jnp.concatenate([jnp.full((1,), 50, jnp.int32), inner.astype(jnp.int32)])


def block_levels(key, extent, cuts, smallest, largest):
    def one(axis_at, parts):
        draws = jax.random.uniform(jax.random.fold_in(jax.random.fold_in(key, 6), axis_at), (parts,), jnp.float32, smallest / len(cuts), largest / len(cuts))
        return jnp.repeat(jnp.exp(draws), extent[axis_at] // parts).reshape((-1,) + (1,) * (len(extent) - axis_at - 1))

    gain = one(*cuts[0])
    for cut in cuts[1:]:
        gain = gain * one(*cut)
    return gain


def normal_values(rng, dims, scale, bound, cuts=(), kind=jnp.bfloat16):
    entries = jax.random.normal(rng, dims, jnp.float32) * scale
    if len(cuts) > 0:
        entries = block_levels(rng, dims, cuts, -0.22, 0.18) * entries
    return jnp.clip(entries, min=-bound, max=bound).astype(kind)


def setup_inputs(seed: int = 0, part: int = 0) -> dict:
    key_of = jax.random.split(jax.random.key(seed), 9)
    part_splits = jax.random.split(jax.random.fold_in(key_of[8], part), 9)
    latents = normal_values(part_splits[0], (TOKENS, D), 1.0, 6.0, ((0, 16),))
    fresh_noise = normal_values(part_splits[1], (TOKENS, D), 1.0, 6.0, ((0, 16),))
    levels = draw_levels(jax.random.fold_in(key_of[8], 71), part)
    time_weight = normal_values(key_of[3], (TFREQ, 2 * D), TFREQ ** -0.5, 0.375)
    w_query = draw_w_query(jax.random.fold_in(key_of[8], 71), part)
    w_key = draw_w_key(jax.random.fold_in(key_of[8], 71), part)
    w_value = normal_values(key_of[6], (D, HEADS * HEAD_DIM), D ** -0.5, 0.15625)
    w_out = normal_values(key_of[7], (HEADS * HEAD_DIM, D), (HEADS * HEAD_DIM) ** -0.5, 0.21875)
    return {"latents": latents, "fresh_noise": fresh_noise, "levels": levels, "time_weight": time_weight, "w_query": w_query, "w_key": w_key, "w_value": w_value, "w_out": w_out}


epsilon = 1e-06

def embed_level(level_value, time_weight):
    half_width = TFREQ // 2
    frequency = jnp.exp(-math.log(10000.0) * jnp.arange(half_width, dtype=jnp.float32) / half_width)
    angles = level_value.astype(jnp.float32) * frequency
    embedding = jnp.concatenate([jnp.cos(angles), jnp.sin(angles)])[None, :]
    modulated = jnp.dot(embedding, time_weight.astype(jnp.float32), precision=lax.Precision.HIGHEST)[0]
    return (modulated[:D], modulated[D:])

def denoise(latent_rows, levels, time_weight, w_query, w_key, w_value, w_out):
    span_rows = TOKENS // SECTIONS
    section_of = jnp.arange(TOKENS, dtype=jnp.int32) // span_rows
    shift_all, scale_all = jax.vmap(lambda value: embed_level(value, time_weight))(levels)
    previous = jnp.concatenate([jnp.zeros((1,), jnp.int32), levels[:-1]])
    step_sizes = (previous - levels).astype(jnp.float32) / 1000.0
    rows_f = latent_rows.astype(jnp.float32)
    normed = rows_f * lax.rsqrt(lax.optimization_barrier(jnp.mean(rows_f * rows_f, axis=-1, keepdims=True)) + epsilon)
    hidden = (normed * (1.0 + scale_all[section_of]) + shift_all[section_of]).astype(jnp.bfloat16)
    queries = jnp.dot(hidden, w_query, preferred_element_type=jnp.float32).astype(jnp.bfloat16)
    keys_all = jnp.dot(hidden, w_key, preferred_element_type=jnp.float32).astype(jnp.bfloat16)
    values_all = jnp.dot(hidden, w_value, preferred_element_type=jnp.float32).astype(jnp.bfloat16)
    allowed = section_of[:, None] >= section_of[None, :]

    def one_head(head_index):

        def take(matrix):
            return lax.dynamic_slice_in_dim(matrix, head_index * HEAD_DIM, HEAD_DIM, 1)
        scores = jnp.dot(take(queries), take(keys_all).T, preferred_element_type=jnp.float32) / math.sqrt(HEAD_DIM)
        scores = jnp.where(allowed, scores, -1e+30)
        top_score = lax.optimization_barrier(jnp.max(scores, axis=-1, keepdims=True))
        weights = jnp.where(allowed, jnp.exp(scores - top_score), 0.0)
        denominator = lax.optimization_barrier(jnp.sum(weights, axis=-1, keepdims=True))
        mixed = jnp.dot(weights.astype(jnp.bfloat16), take(values_all), preferred_element_type=jnp.float32) / denominator
        return mixed.astype(jnp.bfloat16)
    heads_out = lax.map(one_head, jnp.arange(HEADS, dtype=jnp.int32))
    attended = heads_out.transpose(1, 0, 2).reshape(TOKENS, HEADS * HEAD_DIM)
    moving = jnp.dot(attended, w_out, preferred_element_type=jnp.float32)
    stepped = (rows_f + step_sizes[section_of][:, None] * moving).astype(jnp.bfloat16)
    return (stepped, moving.astype(jnp.bfloat16))

def reference(latents, fresh_noise, levels, time_weight, w_query, w_key, w_value, w_out):
    span_rows = TOKENS // SECTIONS
    first, first_moving = denoise(latents, levels, time_weight, w_query, w_key, w_value, w_out)
    second_input = jnp.concatenate([first[span_rows:], fresh_noise[TOKENS - span_rows:]], axis=0)
    second, second_moving = denoise(second_input, levels, time_weight, w_query, w_key, w_value, w_out)
    return (jnp.stack([first, second]), jnp.stack([first_moving, second_moving]))
```

```python
import functools
import math

import jax
import jax.numpy as jnp
from jax import lax
from jax.experimental import pallas as pl
from jax.experimental.pallas import tpu as pltpu
from jax.sharding import PartitionSpec as P

HEAD_DIM = 128
SECTIONS = 4
CORES = 2

epsilon = 1e-06


def permuted(block, axis, move):
    devices = range(lax.axis_size(axis))
    route = [(i, move(i)) for i in devices if move(i) is not None and move(i) in devices]
    return lax.ppermute(block, axis, route)


def embed_levels(levels, time_weight):
    half_width = time_weight.shape[0] // 2
    frequency = jnp.exp(-math.log(10000.0) * jnp.arange(half_width, dtype=jnp.float32) / half_width)
    angles = levels.astype(jnp.float32)[:, None] * frequency[None, :]
    embedding = jnp.concatenate([jnp.cos(angles), jnp.sin(angles)], axis=1)
    modulated = jnp.dot(
        embedding, time_weight.astype(jnp.float32), precision=lax.Precision.HIGHEST
    )
    width = time_weight.shape[1] // 2
    return modulated[:, :width], modulated[:, width:]


def level_steps(levels):
    previous = jnp.concatenate([jnp.zeros((1,), jnp.int32), levels[:-1]])
    return (previous - levels).astype(jnp.float32) / 1000.0


def gathered_body(latents, fresh_noise, levels, time_weight, w_query, w_key, w_value, w_out):
    local_rows = latents.shape[0]
    heads = w_query.shape[1] // HEAD_DIM
    per_section = lax.axis_size("tok") // SECTIONS
    span_rows = local_rows * per_section
    my_block = lax.axis_index("tok") // per_section
    section_ids = jnp.arange(SECTIONS, dtype=jnp.int32)
    shift_all, scale_all = embed_levels(levels, time_weight)
    chosen = section_ids == my_block
    shift_vec = jnp.sum(jnp.where(chosen[:, None], shift_all, 0.0), axis=0)
    scale_vec = jnp.sum(jnp.where(chosen[:, None], scale_all, 0.0), axis=0)
    step_size = jnp.sum(jnp.where(chosen, level_steps(levels), 0.0))

    def denoise_local(rows):
        rows_f = rows.astype(jnp.float32)
        normed = rows_f * lax.rsqrt(jnp.mean(rows_f * rows_f, axis=-1, keepdims=True) + epsilon)
        hidden = (normed * (1.0 + scale_vec) + shift_vec).astype(jnp.bfloat16)

        def project(weight):
            return jnp.dot(hidden, weight, preferred_element_type=jnp.float32).astype(jnp.bfloat16)

        queries = project(w_query).reshape(local_rows, heads, HEAD_DIM)
        keys = lax.all_gather(project(w_key), "tok", axis=0, tiled=True)
        values = lax.all_gather(project(w_value), "tok", axis=0, tiled=True)
        count = keys.shape[0]
        allowed = (jnp.arange(count, dtype=jnp.int32) // span_rows <= my_block)[None, None, :]
        scores = jnp.einsum(
            "rhd,phd->hrp",
            queries,
            keys.reshape(count, heads, HEAD_DIM),
            preferred_element_type=jnp.float32,
        ) / math.sqrt(HEAD_DIM)
        scores = jnp.where(allowed, scores, -1e30)
        best = jnp.max(scores, axis=-1)
        weights = jnp.where(allowed, jnp.exp(scores - best[..., None]), 0.0)
        denominator = jnp.sum(weights, axis=-1)
        summed = jnp.einsum(
            "hrp,phd->hrd",
            weights.astype(jnp.bfloat16),
            values.reshape(count, heads, HEAD_DIM),
            preferred_element_type=jnp.float32,
        )
        attended = (summed / denominator[..., None]).astype(jnp.bfloat16)
        attended = attended.transpose(1, 0, 2).reshape(local_rows, heads * HEAD_DIM)
        moving = jnp.dot(attended, w_out, preferred_element_type=jnp.float32)
        stepped = (rows_f + step_size * moving).astype(jnp.bfloat16)
        return (stepped, moving.astype(jnp.bfloat16))

    first, first_moving = denoise_local(latents)
    incoming = permuted(first, "tok", lambda i: i - per_section)
    second_input = jnp.where(my_block == SECTIONS - 1, fresh_noise, incoming)
    second, second_moving = denoise_local(second_input)
    return (jnp.stack([first, second]), jnp.stack([first_moving, second_moving]))


def modulate(rows_f, scale_row, shift_row):
    normed = rows_f * lax.rsqrt(jnp.mean(rows_f * rows_f, axis=-1, keepdims=True) + epsilon)
    return (normed * (1.0 + scale_row) + shift_row).astype(jnp.bfloat16)


def attend(queries, keys, values):
    scores = lax.dot_general(
        queries, keys, (((1,), (1,)), ((), ())), preferred_element_type=jnp.float32
    )
    top = jnp.max(scores, axis=-1, keepdims=True)
    weights = jnp.exp2((scores - top) * (math.log2(math.e) / math.sqrt(HEAD_DIM)))
    total = jnp.sum(weights, axis=-1, keepdims=True)
    summed = jnp.dot(weights.astype(jnp.bfloat16), values, preferred_element_type=jnp.float32)
    return summed / total


def whole(shape):
    return pl.BlockSpec(shape, lambda *_: (0,) * len(shape))


def project_kernel(info, *refs, pieces, aliased):
    parts = refs[:pieces]
    shift_ref, scale_ref, wq_ref, wk_ref, wv_ref = refs[pieces : pieces + 5]
    refs = refs[pieces + 5 + aliased :]
    out_ref, rows_ref, gather_ref = refs
    local = parts[0].shape[0]
    for i in range(pieces):
        gather_ref[i * local : (i + 1) * local, :] = parts[i][...].astype(jnp.float32)
    rows_f = gather_ref[...]
    rows_ref[...] = rows_f.astype(rows_ref.dtype)
    section = info[0]
    hidden = modulate(rows_f, scale_ref[pl.ds(section, 1), :], shift_ref[pl.ds(section, 1), :])
    width = wq_ref.shape[1]
    for i, w_ref in enumerate((wq_ref, wk_ref, wv_ref)):
        out_ref[:, i * width : (i + 1) * width] = jnp.dot(
            hidden, w_ref[...], preferred_element_type=jnp.float32
        ).astype(out_ref.dtype)


def project(info, parts, mods, weights, carried):
    pieces = len(parts)
    local, depth = parts[0].shape
    span = pieces * local
    width = weights[0].shape[1] // CORES
    blocks = SECTIONS + 1
    w_spec = pl.BlockSpec((depth, width), lambda g, info: (0, info[2]))
    in_specs = [whole(p.shape) for p in parts] + [whole(m.shape) for m in mods] + [w_spec] * 3
    args = list(parts) + list(mods) + list(weights)
    aliases = {}
    if carried is not None:
        for i, c in enumerate(carried):
            aliases[1 + len(args)] = i
            args.append(c)
            in_specs.append(pl.BlockSpec(memory_space=pl.ANY))
    return pl.pallas_call(
        functools.partial(project_kernel, pieces=pieces, aliased=len(aliases)),
        out_shape=(
            jax.ShapeDtypeStruct((blocks * span, 3 * width), jnp.bfloat16),
            jax.ShapeDtypeStruct((blocks * span, depth), jnp.bfloat16),
        ),
        grid_spec=pltpu.PrefetchScalarGridSpec(
            num_scalar_prefetch=1,
            grid=(1,),
            in_specs=in_specs,
            out_specs=(
                pl.BlockSpec((span, 3 * width), lambda g, info: (info[1], 0)),
                pl.BlockSpec((span, depth), lambda g, info: (info[1], 0)),
            ),
            scratch_shapes=[pltpu.VMEM((span, depth), jnp.float32)],
        ),
        input_output_aliases=aliases,
        cost_estimate=pl.CostEstimate(
            flops=2 * span * depth * 3 * width, bytes_accessed=8 << 20, transcendentals=0
        ),
        name="project",
    )(info, *args)


def first_attend_kernel(info, qkv_ref, mine_ref, send_ref, *, span, local, width):
    chip = CORES * local

    def columns(part, head):
        return slice(part * width + head * HEAD_DIM, part * width + (head + 1) * HEAD_DIM)

    def run(section, rows):
        base = section * span
        seen = base + span
        for head in range(width // HEAD_DIM):
            yield head, attend(
                qkv_ref[base : base + rows, columns(0, head)],
                qkv_ref[0:seen, columns(1, head)],
                qkv_ref[0:seen, columns(2, head)],
            )

    for section in range(1, SECTIONS):
        low = (section - 1) * span
        for head, out in run(section, span):
            cols = slice(head * HEAD_DIM, (head + 1) * HEAD_DIM)
            mine_ref[low : low + span, cols] = out.astype(mine_ref.dtype)
            swapped = []
            for i in range(span // local):
                other = i ^ 1
                swapped.append(out[other * local : (other + 1) * local])
            send_ref[low : low + span, cols] = jnp.concatenate(swapped).astype(send_ref.dtype)
    low = (SECTIONS - 1) * span

    @pl.when(info[0] == 0)
    def _():
        for head, out in run(0, chip):
            cols = slice(head * HEAD_DIM, (head + 1) * HEAD_DIM)
            mine_ref[low : low + local, cols] = out[:local].astype(mine_ref.dtype)
            send_ref[low : low + local, cols] = out[local:].astype(send_ref.dtype)


def first_attend(info, qkv, span, local):
    width = qkv.shape[1] // 3
    rows = (SECTIONS - 1) * span + local
    shape = jax.ShapeDtypeStruct((rows, width), jnp.bfloat16)
    return pl.pallas_call(
        functools.partial(first_attend_kernel, span=span, local=local, width=width),
        out_shape=(shape, shape),
        grid_spec=pltpu.PrefetchScalarGridSpec(
            num_scalar_prefetch=1,
            grid=(1,),
            in_specs=[whole(qkv.shape)],
            out_specs=(whole(shape.shape), whole(shape.shape)),
        ),
        cost_estimate=pl.CostEstimate(
            flops=4 * 9 * span * span * width, bytes_accessed=4 << 20, transcendentals=0
        ),
        name="first_attend",
    )(info, qkv)


def middle_kernel(
    info, steps, mine_ref, theirs_ref, rows_ref, fresh_ref, fresh_rows_ref, shift_ref, scale_ref,
    wq_ref, wk_ref, wv_ref, wo_mine_ref, wo_theirs_ref,
    stepped_ref, velocity_ref, next_ref, out_ref, send_ref,
    kv_ref, q_ref, *, span, local,
):
    section = info[0]
    width = wq_ref.shape[1]
    chip = CORES * local

    def moved(low, count):
        return jnp.dot(
            mine_ref[low : low + count, :], wo_mine_ref[...], preferred_element_type=jnp.float32
        ) + jnp.dot(
            theirs_ref[low : low + count, :], wo_theirs_ref[...], preferred_element_type=jnp.float32
        )

    def emit(moving, stepped):
        velocity_ref[0] = moving.astype(velocity_ref.dtype)
        stepped_ref[0] = stepped

    @pl.when(section == 0)
    def _():
        moving = moved((SECTIONS - 1) * span, local)
        old = rows_ref[0:local, :].astype(jnp.float32)
        emit(moving, (old + steps[0] * moving).astype(stepped_ref.dtype))

    for s in range(1, SECTIONS):
        moving = moved((s - 1) * span, span)
        old = rows_ref[s * span : (s + 1) * span, :].astype(jnp.float32)
        stepped = (old + steps[s] * moving).astype(jnp.bfloat16)

        @pl.when(section == s)
        def _():
            emit(moving[:local], stepped[:local])

        t = s - 1
        hidden = modulate(stepped.astype(jnp.float32), scale_ref[t : t + 1, :], shift_ref[t : t + 1, :])
        for i, w_ref in enumerate((wk_ref, wv_ref)):
            kv_ref[t * span : (t + 1) * span, i * width : (i + 1) * width] = jnp.dot(
                hidden, w_ref[...], preferred_element_type=jnp.float32
            ).astype(kv_ref.dtype)

        @pl.when(section == t)
        def _():
            next_ref[...] = stepped[:local]
            q_ref[...] = jnp.dot(
                hidden[:chip], wq_ref[...], preferred_element_type=jnp.float32
            ).astype(q_ref.dtype)

    last = SECTIONS - 1

    @pl.when(section == last)
    def _():
        next_ref[...] = fresh_rows_ref[...]
        q_ref[...] = fresh_ref[0:chip, 0:width]
        kv_ref[last * span : SECTIONS * span, :] = fresh_ref[:, width:]

    for s in range(SECTIONS):

        @pl.when(section == s)
        def _():
            seen = (s + 1) * span
            for head in range(width // HEAD_DIM):
                cols = slice(head * HEAD_DIM, (head + 1) * HEAD_DIM)
                out = attend(
                    q_ref[:, cols],
                    kv_ref[0:seen, cols],
                    kv_ref[0:seen, width + head * HEAD_DIM : width + (head + 1) * HEAD_DIM],
                )
                out_ref[:, cols] = out[:local].astype(out_ref.dtype)
                send_ref[:, cols] = out[local:].astype(send_ref.dtype)


def middle(info, steps, mine, theirs, rows, fresh_qkv, fresh_rows, mods, weights, w_out, span):
    local, depth = fresh_rows.shape
    width = weights[0].shape[1] // CORES
    w_spec = pl.BlockSpec((depth, width), lambda g, info: (0, info[1]))
    wo_mine = pl.BlockSpec((width, depth), lambda g, info: (info[1], 0))
    wo_theirs = pl.BlockSpec((width, depth), lambda g, info: (1 - info[1], 0))
    pair = jax.ShapeDtypeStruct((2, local, depth), jnp.bfloat16)
    pair_spec = pl.BlockSpec((1, local, depth), lambda *_: (0, 0, 0))
    one = jax.ShapeDtypeStruct((local, depth), jnp.bfloat16)
    part = jax.ShapeDtypeStruct((local, width), jnp.bfloat16)
    return pl.pallas_call(
        functools.partial(middle_kernel, span=span, local=local),
        out_shape=(pair, pair, one, part, part),
        grid_spec=pltpu.PrefetchScalarGridSpec(
            num_scalar_prefetch=1,
            grid=(1,),
            in_specs=[
                pl.BlockSpec(memory_space=pltpu.SMEM),
                whole(mine.shape),
                whole(theirs.shape),
                pl.BlockSpec((SECTIONS * span, depth), lambda *_: (0, 0)),
                pl.BlockSpec((span, 3 * width), lambda *_: (SECTIONS - 1, 0)),
                whole(fresh_rows.shape),
                whole(mods[0].shape),
                whole(mods[1].shape),
                w_spec, w_spec, w_spec, wo_mine, wo_theirs,
            ],
            out_specs=(pair_spec, pair_spec, whole(one.shape), whole(part.shape), whole(part.shape)),
            scratch_shapes=[
                pltpu.VMEM((SECTIONS * span, 2 * width), jnp.bfloat16),
                pltpu.VMEM((CORES * local, width), jnp.bfloat16),
            ],
        ),
        cost_estimate=pl.CostEstimate(
            flops=2 * 3 * span * depth * 4 * width, bytes_accessed=16 << 20, transcendentals=0
        ),
        name="middle",
    )(info, steps, mine, theirs, rows, fresh_qkv, fresh_rows, *mods, *weights, w_out, w_out)


def last_kernel(info, steps, mine_ref, theirs_ref, old_ref, wo_mine_ref, wo_theirs_ref, _s, _v, stepped_ref, velocity_ref):
    moving = jnp.dot(
        mine_ref[...], wo_mine_ref[...], preferred_element_type=jnp.float32
    ) + jnp.dot(theirs_ref[...], wo_theirs_ref[...], preferred_element_type=jnp.float32)
    old = old_ref[...].astype(jnp.float32)
    velocity_ref[0] = moving.astype(velocity_ref.dtype)
    stepped_ref[0] = (old + steps[info[0]] * moving).astype(stepped_ref.dtype)


def last(info, steps, mine, theirs, old, w_out, stepped, velocity):
    local, depth = old.shape
    width = mine.shape[1]
    pair_spec = pl.BlockSpec((1, local, depth), lambda *_: (1, 0, 0))
    pair = jax.ShapeDtypeStruct(stepped.shape, stepped.dtype)
    return pl.pallas_call(
        last_kernel,
        out_shape=(pair, pair),
        grid_spec=pltpu.PrefetchScalarGridSpec(
            num_scalar_prefetch=1,
            grid=(1,),
            in_specs=[
                pl.BlockSpec(memory_space=pltpu.SMEM),
                whole(mine.shape),
                whole(theirs.shape),
                whole(old.shape),
                pl.BlockSpec((width, depth), lambda g, info: (info[1], 0)),
                pl.BlockSpec((width, depth), lambda g, info: (1 - info[1], 0)),
                pl.BlockSpec(memory_space=pl.ANY),
                pl.BlockSpec(memory_space=pl.ANY),
            ],
            out_specs=(pair_spec, pair_spec),
        ),
        input_output_aliases={7: 0, 8: 1},
        cost_estimate=pl.CostEstimate(
            flops=4 * local * depth * width, bytes_accessed=4 << 20, transcendentals=0
        ),
        name="last",
    )(info, steps, mine, theirs, old, w_out, w_out, stepped, velocity)


def chip_body(latents, fresh_noise, levels, time_weight, w_query, w_key, w_value, w_out):
    local = latents.shape[0]
    per_section = lax.axis_size("tok") // SECTIONS
    span = local * per_section
    index = lax.axis_index("tok")
    section = (index // per_section).astype(jnp.int32)
    core = (index % CORES).astype(jnp.int32)
    mods = embed_levels(levels, time_weight)
    steps = level_steps(levels)
    weights = (w_query, w_key, w_value)

    def shift(block, distance):
        return permuted(block, "tok", lambda i: i + distance * per_section)

    def chip_swap(block, low=0, high=SECTIONS - 1):
        return permuted(block, "tok", lambda i: i ^ CORES if low <= i // per_section <= high else None)

    def core_swap(block, low=0, high=SECTIONS - 1):
        return permuted(block, "tok", lambda i: i ^ 1 if low <= i // per_section <= high else None)

    def spread(block, low=0, high=SECTIONS - 1):
        across = chip_swap(block, low, high)
        return (block, core_swap(block, low, high), across, core_swap(across, low, high))

    up1 = shift(latents, 1)
    down = shift(latents, -1)
    up2 = shift(up1, 1)
    up3 = shift(up2, 1)
    arrivals = [
        (0, spread(latents)),
        (-1, spread(down, 0, SECTIONS - 2)),
        (1, spread(up1, 1)),
        (2, spread(up2, 2)),
        (3, spread(up3, 3)),
    ]
    carried = None
    for back, parts in arrivals:
        holds = section - back
        valid = (holds >= 0) & (holds < SECTIONS)
        info = jnp.stack([
            jnp.where(valid, holds, 0), jnp.where(valid, holds, SECTIONS), core
        ]).astype(jnp.int32)
        carried = project(info, parts, mods, weights, carried)
    qkv, rows = carried
    top = jnp.int32(SECTIONS - 1)
    fresh_qkv, _ = project(
        jnp.stack([top, top, core]).astype(jnp.int32),
        spread(fresh_noise, SECTIONS - 1), mods, weights, None,
    )
    info = jnp.stack([section, core])
    mine, send = first_attend(info, qkv, span, local)
    theirs = core_swap(send)
    stepped, velocity, old, mine, send = middle(
        info, steps, mine, theirs, rows, fresh_qkv, fresh_noise, mods, weights, w_out, span
    )
    theirs = core_swap(send)
    return last(info, steps, mine, theirs, old, w_out, stepped, velocity)


def solution(mesh):
    per_section = mesh.shape["tok"] // SECTIONS
    body = chip_body if per_section == 2 * CORES else gathered_body
    rows = P(("groups", "tok"), None)
    return jax.shard_map(
        body,
        mesh=mesh,
        in_specs=(rows, rows, P(), P(), P(), P(), P(), P()),
        out_specs=(P(None, ("groups", "tok"), None), P(None, ("groups", "tok"), None)),
        check_vma=False,
    )
```

```python
import functools
import math

import jax
import jax.numpy as jnp
from jax import lax
from jax.experimental import pallas as pl
from jax.experimental.pallas import tpu as pltpu
from jax.sharding import PartitionSpec as P

HEAD_DIM = 128
SECTIONS = 4
CORES = 2

epsilon = 1e-06


def permuted(block, axis, move):
    devices = range(lax.axis_size(axis))
    route = [(i, move(i)) for i in devices if move(i) is not None and move(i) in devices]
    return lax.ppermute(block, axis, route)


def embed_levels(levels, time_weight):
    half_width = time_weight.shape[0] // 2
    frequency = jnp.exp(-math.log(10000.0) * jnp.arange(half_width, dtype=jnp.float32) / half_width)
    angles = levels.astype(jnp.float32)[:, None] * frequency[None, :]
    embedding = jnp.concatenate([jnp.cos(angles), jnp.sin(angles)], axis=1)
    modulated = jnp.dot(
        embedding, time_weight.astype(jnp.float32), precision=lax.Precision.HIGHEST
    )
    width = time_weight.shape[1] // 2
    return modulated[:, :width], modulated[:, width:]


def level_steps(levels):
    previous = jnp.concatenate([jnp.zeros((1,), jnp.int32), levels[:-1]])
    return (previous - levels).astype(jnp.float32) / 1000.0


def gathered_body(latents, fresh_noise, levels, time_weight, w_query, w_key, w_value, w_out):
    local_rows = latents.shape[0]
    heads = w_query.shape[1] // HEAD_DIM
    per_section = lax.axis_size("tok") // SECTIONS
    span_rows = local_rows * per_section
    my_block = lax.axis_index("tok") // per_section
    section_ids = jnp.arange(SECTIONS, dtype=jnp.int32)
    shift_all, scale_all = embed_levels(levels, time_weight)
    chosen = section_ids == my_block
    shift_vec = jnp.sum(jnp.where(chosen[:, None], shift_all, 0.0), axis=0)
    scale_vec = jnp.sum(jnp.where(chosen[:, None], scale_all, 0.0), axis=0)
    step_size = jnp.sum(jnp.where(chosen, level_steps(levels), 0.0))

    def denoise_local(rows):
        rows_f = rows.astype(jnp.float32)
        normed = rows_f * lax.rsqrt(jnp.mean(rows_f * rows_f, axis=-1, keepdims=True) + epsilon)
        hidden = (normed * (1.0 + scale_vec) + shift_vec).astype(jnp.bfloat16)

        def project(weight):
            return jnp.dot(hidden, weight, preferred_element_type=jnp.float32).astype(jnp.bfloat16)

        queries = project(w_query).reshape(local_rows, heads, HEAD_DIM)
        keys = lax.all_gather(project(w_key), "tok", axis=0, tiled=True)
        values = lax.all_gather(project(w_value), "tok", axis=0, tiled=True)
        count = keys.shape[0]
        allowed = (jnp.arange(count, dtype=jnp.int32) // span_rows <= my_block)[None, None, :]
        scores = jnp.einsum(
            "rhd,phd->hrp",
            queries,
            keys.reshape(count, heads, HEAD_DIM),
            preferred_element_type=jnp.float32,
        ) / math.sqrt(HEAD_DIM)
        scores = jnp.where(allowed, scores, -1e30)
        best = jnp.max(scores, axis=-1)
        weights = jnp.where(allowed, jnp.exp(scores - best[..., None]), 0.0)
        denominator = jnp.sum(weights, axis=-1)
        summed = jnp.einsum(
            "hrp,phd->hrd",
            weights.astype(jnp.bfloat16),
            values.reshape(count, heads, HEAD_DIM),
            preferred_element_type=jnp.float32,
        )
        attended = (summed / denominator[..., None]).astype(jnp.bfloat16)
        attended = attended.transpose(1, 0, 2).reshape(local_rows, heads * HEAD_DIM)
        moving = jnp.dot(attended, w_out, preferred_element_type=jnp.float32)
        stepped = (rows_f + step_size * moving).astype(jnp.bfloat16)
        return (stepped, moving.astype(jnp.bfloat16))

    first, first_moving = denoise_local(latents)
    incoming = permuted(first, "tok", lambda i: i - per_section)
    second_input = jnp.where(my_block == SECTIONS - 1, fresh_noise, incoming)
    second, second_moving = denoise_local(second_input)
    return (jnp.stack([first, second]), jnp.stack([first_moving, second_moving]))


VMEM = pl.BlockSpec(memory_space=pltpu.VMEM)
SMEM = pl.BlockSpec(memory_space=pltpu.SMEM)
HBM = pl.BlockSpec(memory_space=pltpu.HBM)
LAST = SECTIONS - 1


def modulate(rows_f, scale_row, shift_row):
    normed = rows_f * lax.rsqrt(jnp.mean(rows_f * rows_f, axis=-1, keepdims=True) + epsilon)
    return (normed * (1.0 + scale_row) + shift_row).astype(jnp.bfloat16)


def dot(a, b):
    return jnp.dot(a, b, preferred_element_type=jnp.float32)


def attend(queries, pairs):
    scores = [
        lax.dot_general(queries, keys, (((1,), (1,)), ((), ())), preferred_element_type=jnp.float32)
        for keys, _ in pairs
    ]
    top = functools.reduce(jnp.maximum, [jnp.max(s, axis=-1, keepdims=True) for s in scores])
    total, summed = 0.0, 0.0
    for score, (_, values) in zip(scores, pairs):
        weights = jnp.exp2((score - top) * (math.log2(math.e) / math.sqrt(HEAD_DIM)))
        total = total + jnp.sum(weights, axis=-1, keepdims=True)
        summed = summed + dot(weights.astype(jnp.bfloat16), values)
    return summed / total


def head_columns(width):
    for head in range(width // HEAD_DIM):
        yield slice(head * HEAD_DIM, (head + 1) * HEAD_DIM), slice(
            width + head * HEAD_DIM, width + (head + 1) * HEAD_DIM
        )


def fetch_kernel(*refs):
    count = len(refs) // 2
    sem = refs[-1]
    copies = [pltpu.make_async_copy(refs[i], refs[count + i], sem.at[i]) for i in range(count)]
    for c in copies:
        c.start()
    for c in copies:
        c.wait()


def fetch(arrays):
    return pl.pallas_call(
        fetch_kernel,
        out_shape=[jax.ShapeDtypeStruct(a.shape, a.dtype) for a in arrays],
        in_specs=[HBM] * len(arrays),
        out_specs=[VMEM] * len(arrays),
        scratch_shapes=[pltpu.SemaphoreType.DMA((len(arrays),))],
        compiler_params=pltpu.CompilerParams(vmem_limit_bytes=1 << 20),
        cost_estimate=pl.CostEstimate(
            flops=0, bytes_accessed=sum(a.size * 2 for a in arrays), transcendentals=0
        ),
        name="fetch",
    )(*[pltpu.with_memory_space_constraint(a, pltpu.HBM) for a in arrays])


def project_kernel(where, own_ref, across_ref, shift_ref, scale_ref, wk_ref, wv_ref, wq_ref, *outs, back):
    rows_f = jnp.concatenate([own_ref[...].astype(jnp.float32), across_ref[...].astype(jnp.float32)])
    if back is None:
        section = LAST
    else:
        section = jnp.clip(where[0] - back, 0, LAST)
    hidden = modulate(rows_f, scale_ref[pl.ds(section, 1), :], shift_ref[pl.ds(section, 1), :])
    width = wk_ref.shape[1]
    outs[0][:, :width] = dot(hidden, wk_ref[...]).astype(jnp.bfloat16)
    outs[0][:, width:] = dot(hidden, wv_ref[...]).astype(jnp.bfloat16)
    if len(outs) > 1:
        outs[1][...] = dot(hidden, wq_ref[...]).astype(jnp.bfloat16)


def project(where, own, across, mods, weights, back, with_queries):
    local, depth = own.shape
    width = weights[0].shape[1]
    shapes = [jax.ShapeDtypeStruct((2 * local, 2 * width), jnp.bfloat16)]
    if with_queries:
        shapes.append(jax.ShapeDtypeStruct((2 * local, width), jnp.bfloat16))
    return pl.pallas_call(
        functools.partial(project_kernel, back=back),
        out_shape=shapes,
        in_specs=[SMEM] + [VMEM] * 7,
        out_specs=[VMEM] * len(shapes),
        compiler_params=pltpu.CompilerParams(vmem_limit_bytes=12 << 20),
        cost_estimate=pl.CostEstimate(
            flops=12 * local * depth * width, bytes_accessed=2 << 20, transcendentals=0
        ),
        name="project",
    )(where, own, across, *mods, *weights)


def first_kernel(where, steps, *refs, slots, query_slots):
    refs = list(refs)
    take = lambda n: [refs.pop(0) for _ in range(n)]
    kv_mine, kv_theirs = take(len(slots)), take(len(slots))
    q_in, own_in, across_in = take(len(query_slots)), take(len(query_slots)), take(len(query_slots))
    shift_ref, scale_ref, wk_ref, wv_ref, wq_ref, wo_ref = take(6)
    stepped_hbm, velocity_hbm, kv2_ref, q2_ref, next_ref = take(5)
    kv_ref, q_ref, x_ref, o_ref, v_ref, st_ref, hid_ref, sem = refs
    local = own_in[0].shape[0]
    half = 2 * local
    span = 2 * half
    width = wk_ref.shape[1]
    section = where[0]

    def place(back):
        holds = section - back
        return jnp.where((holds >= 0) & (holds <= LAST), holds, SECTIONS)

    for i, back in enumerate(slots):
        base = pl.multiple_of(place(back) * span, span)
        kv_ref[pl.ds(base, half), :] = kv_mine[i][...]
        kv_ref[pl.ds(base + half, half), :] = kv_theirs[i][...]
    for i, back in enumerate(query_slots):
        base = pl.multiple_of(place(back) * half, half)
        q_ref[pl.ds(base, half), :] = q_in[i][...]
        x_ref[pl.ds(base, local), :] = own_in[i][...].astype(jnp.float32)
        x_ref[pl.ds(base + local, local), :] = across_in[i][...].astype(jnp.float32)

    def attend_rows(low, count, seen, into):
        for cols, v_cols in head_columns(width):
            out = attend(q_ref[low : low + count, cols], [(kv_ref[0:seen, cols], kv_ref[0:seen, v_cols])])
            o_ref[into : into + count, cols] = out.astype(jnp.bfloat16)

    for s in range(1, SECTIONS):
        attend_rows(s * half, half, (s + 1) * span, (s - 1) * half)
    v_ref[...] = dot(o_ref[0 : LAST * half, :], wo_ref[...])
    for s in range(1, SECTIONS):
        rows = slice((s - 1) * half, s * half)
        stepped = (x_ref[s * half : (s + 1) * half, :] + steps[s] * v_ref[rows, :]).astype(jnp.bfloat16)
        st_ref[rows, :] = stepped
        hid_ref[rows, :] = modulate(
            stepped.astype(jnp.float32), scale_ref[s - 1 : s, :], shift_ref[s - 1 : s, :]
        )
    kv2_ref[:, :width] = dot(hid_ref[...], wk_ref[...]).astype(jnp.bfloat16)
    kv2_ref[:, width:] = dot(hid_ref[...], wv_ref[...]).astype(jnp.bfloat16)

    @pl.when(section < LAST)
    def _():
        base = pl.multiple_of(section * half, half)
        q2_ref[...] = dot(hid_ref[pl.ds(base, half), :][:local], wq_ref[...]).astype(jnp.bfloat16)
        next_ref[...] = st_ref[pl.ds(base, half), :][:local]

    @pl.when(section == 0)
    def _():
        attend_rows(0, local, span, 0)
        moving = dot(o_ref[0:local, :], wo_ref[...])
        hid_ref[0:local, :] = moving.astype(jnp.bfloat16)
        st_ref[0:local, :] = (x_ref[0:local, :] + steps[0] * moving).astype(jnp.bfloat16)

    @pl.when(section > 0)
    def _():
        base = pl.multiple_of((section - 1) * half, half)
        hid_ref[0:local, :] = v_ref[pl.ds(base, half), :][:local].astype(jnp.bfloat16)
        st_ref[0:local, :] = st_ref[pl.ds(base, half), :][:local]

    copies = [
        pltpu.make_async_copy(st_ref.at[0:local, :], stepped_hbm.at[0], sem.at[0]),
        pltpu.make_async_copy(hid_ref.at[0:local, :], velocity_hbm.at[0], sem.at[1]),
    ]
    for c in copies:
        c.start()
    for c in copies:
        c.wait()


def first_round(where, steps, slots, kv_mine, kv_theirs, query_slots, q_in, own_in, across_in, mods, weights, w_out):
    local, depth = own_in[0].shape
    width = weights[0].shape[1]
    half, span = 2 * local, 4 * local
    pair = jax.ShapeDtypeStruct((2, local, depth), jnp.bfloat16)
    args = [*kv_mine, *kv_theirs, *q_in, *own_in, *across_in, *mods, *weights, w_out]
    blocks = SECTIONS + 1
    return pl.pallas_call(
        functools.partial(first_kernel, slots=slots, query_slots=query_slots),
        out_shape=(
            pair,
            pair,
            jax.ShapeDtypeStruct((LAST * half, 2 * width), jnp.bfloat16),
            jax.ShapeDtypeStruct((local, width), jnp.bfloat16),
            jax.ShapeDtypeStruct((local, depth), jnp.bfloat16),
        ),
        in_specs=[SMEM, SMEM] + [VMEM] * len(args),
        out_specs=(HBM, HBM, VMEM, VMEM, VMEM),
        scratch_shapes=[
            pltpu.VMEM((blocks * span, 2 * width), jnp.bfloat16),
            pltpu.VMEM((blocks * half, width), jnp.bfloat16),
            pltpu.VMEM((blocks * half, depth), jnp.float32),
            pltpu.VMEM((LAST * half, width), jnp.bfloat16),
            pltpu.VMEM((LAST * half, depth), jnp.float32),
            pltpu.VMEM((LAST * half, depth), jnp.bfloat16),
            pltpu.VMEM((LAST * half, depth), jnp.bfloat16),
            pltpu.SemaphoreType.DMA((2,)),
        ],
        compiler_params=pltpu.CompilerParams(vmem_limit_bytes=28 << 20),
        cost_estimate=pl.CostEstimate(
            flops=12 * LAST * half * depth * width, bytes_accessed=4 << 20, transcendentals=0
        ),
        name="first_round",
    )(where, steps, *args)


def second_kernel(
    where, steps, q_ref, old_ref, mine_ref, theirs_ref, fresh_q_ref, fresh_ref, fresh_mine_ref, fresh_theirs_ref,
    wo_ref, _s, _v, stepped_hbm, velocity_hbm, o_ref, st_ref, v_ref, x_ref, sem,
):
    local, width = q_ref.shape
    section = where[0]
    for s in range(SECTIONS):

        @pl.when(section == s)
        def _():
            if s < LAST:
                seen = [(mine_ref, (s + 1) * 2 * local), (theirs_ref, (s + 1) * 2 * local)]
                queries = q_ref
                x_ref[...] = old_ref[...]
            else:
                seen = [(r, r.shape[0]) for r in (mine_ref, theirs_ref, fresh_mine_ref, fresh_theirs_ref)]
                queries = fresh_q_ref.at[0:local]
                x_ref[...] = fresh_ref[...]
            for cols, v_cols in head_columns(width):
                out = attend(queries[:, cols], [(r[0:n, cols], r[0:n, v_cols]) for r, n in seen])
                o_ref[:, cols] = out.astype(jnp.bfloat16)

    moving = dot(o_ref[...], wo_ref[...])
    v_ref[...] = moving.astype(jnp.bfloat16)
    st_ref[...] = (x_ref[...].astype(jnp.float32) + steps[section] * moving).astype(jnp.bfloat16)
    copies = [
        pltpu.make_async_copy(st_ref, stepped_hbm.at[1], sem.at[0]),
        pltpu.make_async_copy(v_ref, velocity_hbm.at[1], sem.at[1]),
    ]
    for c in copies:
        c.start()
    for c in copies:
        c.wait()


def second_round(where, steps, q, old, mine, theirs, fresh_q, fresh, fresh_mine, fresh_theirs, w_out, stepped, velocity):
    local, width = q.shape
    pair = jax.ShapeDtypeStruct(stepped.shape, stepped.dtype)
    return pl.pallas_call(
        second_kernel,
        out_shape=(pair, pair),
        in_specs=[SMEM, SMEM] + [VMEM] * 9 + [HBM, HBM],
        out_specs=(HBM, HBM),
        scratch_shapes=[
            pltpu.VMEM((local, width), jnp.bfloat16),
            pltpu.VMEM(old.shape, jnp.bfloat16),
            pltpu.VMEM(old.shape, jnp.bfloat16),
            pltpu.VMEM(old.shape, jnp.bfloat16),
            pltpu.SemaphoreType.DMA((2,)),
        ],
        input_output_aliases={11: 0, 12: 1},
        compiler_params=pltpu.CompilerParams(vmem_limit_bytes=12 << 20),
        cost_estimate=pl.CostEstimate(
            flops=4 * local * old.shape[1] * width, bytes_accessed=4 << 20, transcendentals=0
        ),
        name="second_round",
    )(where, steps, q, old, mine, theirs, fresh_q, fresh, fresh_mine, fresh_theirs, w_out, stepped, velocity)


def chip_body(latents, fresh_noise, levels, time_weight, w_query, w_key, w_value, w_out):
    per_section = lax.axis_size("tok") // SECTIONS
    where = (lax.axis_index("tok") // per_section).astype(jnp.int32).reshape(1)

    def shift(block, distance):
        return permuted(block, "tok", lambda i: i + distance * per_section)

    def chip_swap(block, low=0, high=LAST):
        return permuted(block, "tok", lambda i: i ^ CORES if low <= i // per_section <= high else None)

    def core_swap(block, low=0, high=LAST):
        return permuted(block, "tok", lambda i: i ^ 1 if low <= i // per_section <= high else None)

    def after(value, *others):
        return lax.optimization_barrier((value, *others))[0]

    w_key, w_value, w_query, w_out = fetch((w_key, w_value, w_query, w_out))
    weights = (w_key, w_value, w_query)
    own, across, kv, theirs, q = {}, {}, {}, {}, {}

    def work(back, low=0, high=LAST):
        kv[back], q[back] = project(where, own[back], across[back], mods, weights, back, True)
        theirs[back] = core_swap(kv[back], low, high)

    own[0] = latents
    own[1] = shift(latents, 1)
    across[0] = chip_swap(latents)
    own[-1] = shift(latents, -1)
    fresh_across = chip_swap(fresh_noise, LAST)
    levels = after(levels, own[1], w_key)
    mods, steps = lax.optimization_barrier((embed_levels(levels, time_weight), level_steps(levels)))
    own[2] = shift(own[1], 1)
    across[1] = chip_swap(own[1], 1)
    across[-1] = chip_swap(own[-1], 0, LAST - 1)
    work(0)
    fresh_mine, fresh_q = project(where, fresh_noise, fresh_across, mods, weights, None, True)
    fresh_theirs = core_swap(fresh_mine, LAST)
    own[3] = shift(after(own[2], kv[0], fresh_mine), 1)
    across[2] = chip_swap(own[2], 2)
    work(1, 1)
    work(-1, 0, LAST - 1)
    across[3] = chip_swap(after(own[3], kv[1], kv[-1]), 3)
    work(2, 2)
    ready = lax.optimization_barrier((across[3], kv[2], fresh_theirs, theirs[0], theirs[1], theirs[-1]))
    across[3], kv[2], fresh_theirs, theirs[0], theirs[1], theirs[-1] = ready
    kv[3], = project(where, own[3], across[3], mods, weights, 3, False)
    theirs[3] = core_swap(kv[3], 3)
    slots, query_slots = (0, 1, -1, 2, 3), (0, 1, -1, 2)
    pick = lambda d, names: [d[n] for n in names]
    stepped, velocity, mine2, q2, old = first_round(
        where, steps, slots, pick(kv, slots), pick(theirs, slots), query_slots, pick(q, query_slots),
        pick(own, query_slots), pick(across, query_slots), mods, weights, w_out,
    )
    theirs2 = core_swap(mine2)
    return second_round(
        where, steps, q2, old, mine2, theirs2, fresh_q, fresh_noise, fresh_mine, fresh_theirs, w_out,
        stepped, velocity,
    )


def solution(mesh):
    per_section = mesh.shape["tok"] // SECTIONS
    body = chip_body if per_section == 2 * CORES else gathered_body
    rows = P(("groups", "tok"), None)
    return jax.shard_map(
        body,
        mesh=mesh,
        in_specs=(rows, rows, P(), P(), P(), P(), P(), P()),
        out_specs=(P(None, ("groups", "tok"), None), P(None, ("groups", "tok"), None)),
        check_vma=False,
    )
```

```python
import functools
import math

import jax
import jax.numpy as jnp
from jax import lax
from jax.experimental import pallas as pl
from jax.experimental.pallas import tpu as pltpu
from jax.sharding import PartitionSpec as P


HEAD_DIM = 128
SECTIONS = 4
CORES = 2

epsilon = 1e-06


def permuted(block, axis, move):
    devices = range(lax.axis_size(axis))
    route = [(i, move(i)) for i in devices if move(i) is not None and move(i) in devices]
    return lax.ppermute(block, axis, route)


def level_embedding(levels, half_width):
    frequency = jnp.exp(-math.log(10000.0) * jnp.arange(half_width, dtype=jnp.float32) / half_width)
    angles = levels.astype(jnp.float32)[:, None] * frequency[None, :]
    return jnp.concatenate([jnp.cos(angles), jnp.sin(angles)], axis=1)


def embed_levels(levels, time_weight):
    return jnp.dot(
        level_embedding(levels, time_weight.shape[0] // 2),
        time_weight.astype(jnp.float32),
        precision=lax.Precision.HIGHEST,
    )


def level_steps(levels):
    previous = jnp.concatenate([jnp.zeros((1,), jnp.int32), levels[:-1]])
    return (previous - levels).astype(jnp.float32) / 1000.0


def gathered_body(latents, fresh_noise, levels, time_weight, w_query, w_key, w_value, w_out):
    local_rows = latents.shape[0]
    heads = w_query.shape[1] // HEAD_DIM
    per_section = lax.axis_size("tok") // SECTIONS
    span_rows = local_rows * per_section
    my_block = lax.axis_index("tok") // per_section
    section_ids = jnp.arange(SECTIONS, dtype=jnp.int32)
    mods = embed_levels(levels, time_weight)
    width = mods.shape[1] // 2
    shift_all, scale_all = mods[:, :width], mods[:, width:]
    chosen = section_ids == my_block
    shift_vec = jnp.sum(jnp.where(chosen[:, None], shift_all, 0.0), axis=0)
    scale_vec = jnp.sum(jnp.where(chosen[:, None], scale_all, 0.0), axis=0)
    step_size = jnp.sum(jnp.where(chosen, level_steps(levels), 0.0))

    def denoise_local(rows):
        rows_f = rows.astype(jnp.float32)
        normed = rows_f * lax.rsqrt(jnp.mean(rows_f * rows_f, axis=-1, keepdims=True) + epsilon)
        hidden = (normed * (1.0 + scale_vec) + shift_vec).astype(jnp.bfloat16)

        def project(weight):
            return jnp.dot(hidden, weight, preferred_element_type=jnp.float32).astype(jnp.bfloat16)

        queries = project(w_query).reshape(local_rows, heads, HEAD_DIM)
        keys = lax.all_gather(project(w_key), "tok", axis=0, tiled=True)
        values = lax.all_gather(project(w_value), "tok", axis=0, tiled=True)
        count = keys.shape[0]
        allowed = (jnp.arange(count, dtype=jnp.int32) // span_rows <= my_block)[None, None, :]
        scores = jnp.einsum(
            "rhd,phd->hrp",
            queries,
            keys.reshape(count, heads, HEAD_DIM),
            preferred_element_type=jnp.float32,
        ) / math.sqrt(HEAD_DIM)
        scores = jnp.where(allowed, scores, -1e30)
        best = jnp.max(scores, axis=-1)
        weights = jnp.where(allowed, jnp.exp(scores - best[..., None]), 0.0)
        denominator = jnp.sum(weights, axis=-1)
        summed = jnp.einsum(
            "hrp,phd->hrd",
            weights.astype(jnp.bfloat16),
            values.reshape(count, heads, HEAD_DIM),
            preferred_element_type=jnp.float32,
        )
        attended = (summed / denominator[..., None]).astype(jnp.bfloat16)
        attended = attended.transpose(1, 0, 2).reshape(local_rows, heads * HEAD_DIM)
        moving = jnp.dot(attended, w_out, preferred_element_type=jnp.float32)
        stepped = (rows_f + step_size * moving).astype(jnp.bfloat16)
        return (stepped, moving.astype(jnp.bfloat16))

    first, first_moving = denoise_local(latents)
    incoming = permuted(first, "tok", lambda i: i - per_section)
    second_input = jnp.where(my_block == SECTIONS - 1, fresh_noise, incoming)
    second, second_moving = denoise_local(second_input)
    return (jnp.stack([first, second]), jnp.stack([first_moving, second_moving]))


VMEM = pl.BlockSpec(memory_space=pltpu.VMEM)
SMEM = pl.BlockSpec(memory_space=pltpu.SMEM)
HBM = pl.BlockSpec(memory_space=pltpu.HBM)
LAST = SECTIONS - 1


def modulate(rows_f, scale_row, shift_row):
    normed = rows_f * lax.rsqrt(jnp.mean(rows_f * rows_f, axis=-1, keepdims=True) + epsilon)
    return (normed * (1.0 + scale_row) + shift_row).astype(jnp.bfloat16)


def dot(a, b):
    return jnp.dot(a, b, preferred_element_type=jnp.float32)


def attend(queries, pairs):
    scores = [
        lax.dot_general(queries, keys, (((1,), (1,)), ((), ())), preferred_element_type=jnp.float32)
        for keys, _ in pairs
    ]
    top = functools.reduce(jnp.maximum, [jnp.max(s, axis=-1, keepdims=True) for s in scores])
    total, summed = 0.0, 0.0
    for score, (_, values) in zip(scores, pairs):
        weights = jnp.exp2((score - top) * (math.log2(math.e) / math.sqrt(HEAD_DIM)))
        total = total + jnp.sum(weights, axis=-1, keepdims=True)
        summed = summed + dot(weights.astype(jnp.bfloat16), values)
    return summed / total


def head_columns(width):
    for head in range(width // HEAD_DIM):
        yield slice(head * HEAD_DIM, (head + 1) * HEAD_DIM), slice(
            width + head * HEAD_DIM, width + (head + 1) * HEAD_DIM
        )


def fetch_kernel(*refs, count):
    sources, embedding_ref, time_hbm = refs[:count], refs[count], refs[count + 1]
    outs, mods_ref = refs[count + 2 : 2 * count + 2], refs[2 * count + 2]
    time_ref, sem = refs[2 * count + 3 :]
    time_copy = pltpu.make_async_copy(time_hbm, time_ref, sem.at[count])
    time_copy.start()
    copies = [pltpu.make_async_copy(sources[i], outs[i], sem.at[i]) for i in range(count)]
    for c in copies:
        c.start()
    rest = embedding_ref[...]
    modulated = None
    time_copy.wait()
    for _ in range(3):
        term = rest.astype(jnp.bfloat16)
        rest = rest - term.astype(jnp.float32)
        product = dot(term, time_ref[...])
        modulated = product if modulated is None else modulated + product
    mods_ref[...] = modulated
    for c in copies:
        c.wait()


def fetch(arrays, embedding, time_weight):
    in_hbm = [pltpu.with_memory_space_constraint(a, pltpu.HBM) for a in (*arrays, time_weight)]
    return pl.pallas_call(
        functools.partial(fetch_kernel, count=len(arrays)),
        out_shape=[jax.ShapeDtypeStruct(a.shape, a.dtype) for a in arrays]
        + [jax.ShapeDtypeStruct((embedding.shape[0], time_weight.shape[1]), jnp.float32)],
        in_specs=[HBM] * len(arrays) + [VMEM, HBM],
        out_specs=[VMEM] * (len(arrays) + 1),
        scratch_shapes=[
            pltpu.VMEM(time_weight.shape, time_weight.dtype),
            pltpu.SemaphoreType.DMA((len(arrays) + 1,)),
        ],
        compiler_params=pltpu.CompilerParams(vmem_limit_bytes=6 << 20),
        cost_estimate=pl.CostEstimate(
            flops=0, bytes_accessed=sum(a.size * 2 for a in arrays), transcendentals=0
        ),
        name="fetch",
    )(*in_hbm[:-1], embedding, in_hbm[-1])


def project_kernel(where, *refs, slots):
    refs = list(refs)
    own = [refs.pop(0) for _ in slots]
    across = [refs.pop(0) for _ in slots]
    mods_ref, wk_ref, wv_ref, wq_ref, kv_ref, q_ref = refs
    depth, width = wk_ref.shape
    hidden = []
    for i, slot in enumerate(slots):
        rows_f = jnp.concatenate([own[i][...].astype(jnp.float32), across[i][...].astype(jnp.float32)])
        section = LAST if slot is None else where[0] ^ slot
        row = mods_ref[pl.ds(section, 1), :]
        hidden.append(modulate(rows_f, row[:, depth:], row[:, :depth]))
    hidden = jnp.concatenate(hidden)
    kv_ref[:, :width] = dot(hidden, wk_ref[...]).astype(jnp.bfloat16)
    kv_ref[:, width:] = dot(hidden, wv_ref[...]).astype(jnp.bfloat16)
    q_ref[...] = dot(hidden, wq_ref[...]).astype(jnp.bfloat16)


def project(where, slots, own, across, mods, weights):
    local, depth = own[0].shape
    width = weights[0].shape[1]
    rows = 2 * local * len(slots)
    return pl.pallas_call(
        functools.partial(project_kernel, slots=slots),
        out_shape=(
            jax.ShapeDtypeStruct((rows, 2 * width), jnp.bfloat16),
            jax.ShapeDtypeStruct((rows, width), jnp.bfloat16),
        ),
        in_specs=[SMEM] + [VMEM] * (2 * len(slots) + 4),
        out_specs=(VMEM, VMEM),
        compiler_params=pltpu.CompilerParams(vmem_limit_bytes=12 << 20),
        cost_estimate=pl.CostEstimate(
            flops=6 * rows * depth * width, bytes_accessed=2 << 20, transcendentals=0
        ),
        name="project",
    )(where, *own, *across, mods, *weights)


def first_kernel(where, steps, *refs, groups):
    refs = list(refs)
    take = lambda n: [refs.pop(0) for _ in range(n)]
    slots = [slot for group in groups for slot in group if slot is not None]
    kv_mine, kv_theirs, q_in = take(len(groups)), take(len(groups)), take(len(groups))
    own_in, across_in = take(len(slots)), take(len(slots))
    mods_ref, wk_ref, wv_ref, wq_ref, wo_ref = take(5)
    stepped_hbm, velocity_hbm, kv2_ref, q2_ref, next_ref = take(5)
    kv_ref, q_ref, x_ref, o_ref, v_ref, st_ref, hid_ref, sem = refs
    local = own_in[0].shape[0]
    half = 2 * local
    span = 2 * half
    depth, width = wk_ref.shape
    section = where[0]

    for g, group in enumerate(groups):
        for i, slot in enumerate(group):
            if slot is None:
                continue
            rows = slice(i * half, (i + 1) * half)
            base = pl.multiple_of((section ^ slot) * span, span)
            kv_ref[pl.ds(base, half), :] = kv_mine[g][rows, :]
            kv_ref[pl.ds(base + half, half), :] = kv_theirs[g][rows, :]
            base = pl.multiple_of((section ^ slot) * half, half)
            q_ref[pl.ds(base, half), :] = q_in[g][rows, :]
            n = slots.index(slot)
            x_ref[pl.ds(base, local), :] = own_in[n][...].astype(jnp.float32)
            x_ref[pl.ds(base + local, local), :] = across_in[n][...].astype(jnp.float32)

    def attend_rows(low, count, seen, into):
        for cols, v_cols in head_columns(width):
            out = attend(q_ref[low : low + count, cols], [(kv_ref[0:seen, cols], kv_ref[0:seen, v_cols])])
            o_ref[into : into + count, cols] = out.astype(jnp.bfloat16)

    for s in range(1, SECTIONS):
        attend_rows(s * half, half, (s + 1) * span, (s - 1) * half)
    v_ref[...] = dot(o_ref[0 : LAST * half, :], wo_ref[...])
    for s in range(1, SECTIONS):
        rows = slice((s - 1) * half, s * half)
        stepped = (x_ref[s * half : (s + 1) * half, :] + steps[s] * v_ref[rows, :]).astype(jnp.bfloat16)
        st_ref[rows, :] = stepped
        hid_ref[rows, :] = modulate(
            stepped.astype(jnp.float32), mods_ref[s - 1 : s, depth:], mods_ref[s - 1 : s, :depth]
        )
    kv2_ref[:, :width] = dot(hid_ref[...], wk_ref[...]).astype(jnp.bfloat16)
    kv2_ref[:, width:] = dot(hid_ref[...], wv_ref[...]).astype(jnp.bfloat16)

    @pl.when(section < LAST)
    def _():
        base = pl.multiple_of(section * half, half)
        q2_ref[...] = dot(hid_ref[pl.ds(base, half), :][:local], wq_ref[...]).astype(jnp.bfloat16)
        next_ref[...] = st_ref[pl.ds(base, half), :][:local]

    @pl.when(section == 0)
    def _():
        attend_rows(0, local, span, 0)
        moving = dot(o_ref[0:local, :], wo_ref[...])
        hid_ref[0:local, :] = moving.astype(jnp.bfloat16)
        st_ref[0:local, :] = (x_ref[0:local, :] + steps[0] * moving).astype(jnp.bfloat16)

    @pl.when(section > 0)
    def _():
        base = pl.multiple_of((section - 1) * half, half)
        hid_ref[0:local, :] = v_ref[pl.ds(base, half), :][:local].astype(jnp.bfloat16)
        st_ref[0:local, :] = st_ref[pl.ds(base, half), :][:local]

    copies = [
        pltpu.make_async_copy(st_ref.at[0:local, :], stepped_hbm.at[0], sem.at[0]),
        pltpu.make_async_copy(hid_ref.at[0:local, :], velocity_hbm.at[0], sem.at[1]),
    ]
    for c in copies:
        c.start()
    for c in copies:
        c.wait()


def first_round(where, steps, groups, kv_mine, kv_theirs, q, own, across, mods, weights, w_out):
    local, depth = own[0].shape
    width = weights[0].shape[1]
    half, span = 2 * local, 4 * local
    pair = jax.ShapeDtypeStruct((2, local, depth), jnp.bfloat16)
    args = [*kv_mine, *kv_theirs, *q, *own, *across, mods, *weights, w_out]
    blocks = SECTIONS
    return pl.pallas_call(
        functools.partial(first_kernel, groups=groups),
        out_shape=(
            pair,
            pair,
            jax.ShapeDtypeStruct((LAST * half, 2 * width), jnp.bfloat16),
            jax.ShapeDtypeStruct((local, width), jnp.bfloat16),
            jax.ShapeDtypeStruct((local, depth), jnp.bfloat16),
        ),
        in_specs=[SMEM, SMEM] + [VMEM] * len(args),
        out_specs=(HBM, HBM, VMEM, VMEM, VMEM),
        scratch_shapes=[
            pltpu.VMEM((blocks * span, 2 * width), jnp.bfloat16),
            pltpu.VMEM((blocks * half, width), jnp.bfloat16),
            pltpu.VMEM((blocks * half, depth), jnp.float32),
            pltpu.VMEM((LAST * half, width), jnp.bfloat16),
            pltpu.VMEM((LAST * half, depth), jnp.float32),
            pltpu.VMEM((LAST * half, depth), jnp.bfloat16),
            pltpu.VMEM((LAST * half, depth), jnp.bfloat16),
            pltpu.SemaphoreType.DMA((2,)),
        ],
        compiler_params=pltpu.CompilerParams(vmem_limit_bytes=28 << 20),
        cost_estimate=pl.CostEstimate(
            flops=12 * LAST * half * depth * width, bytes_accessed=4 << 20, transcendentals=0
        ),
        name="first_round",
    )(where, steps, *args)


def second_kernel(
    where, steps, q_ref, old_ref, mine_ref, theirs_ref, fresh_ref, fresh_q_ref, fresh_mine_ref, fresh_theirs_ref,
    wo_ref, _s, _v, stepped_hbm, velocity_hbm, o_ref, st_ref, v_ref, x_ref, sem, *, fresh_row,
):
    local, width = q_ref.shape
    section = where[0]
    for s in range(SECTIONS):

        @pl.when(section == s)
        def _():
            if s < LAST:
                seen = [(mine_ref, (s + 1) * 2 * local), (theirs_ref, (s + 1) * 2 * local)]
                queries = q_ref
                x_ref[...] = old_ref[...]
            else:
                fresh_rows = slice(fresh_row, fresh_row + 2 * local)
                seen = [(r, r.shape[0]) for r in (mine_ref, theirs_ref)]
                seen += [(r.at[fresh_rows], 2 * local) for r in (fresh_mine_ref, fresh_theirs_ref)]
                queries = fresh_q_ref.at[fresh_row : fresh_row + local]
                x_ref[...] = fresh_ref[...]
            for cols, v_cols in head_columns(width):
                out = attend(queries[:, cols], [(r[0:n, cols], r[0:n, v_cols]) for r, n in seen])
                o_ref[:, cols] = out.astype(jnp.bfloat16)

    moving = dot(o_ref[...], wo_ref[...])
    v_ref[...] = moving.astype(jnp.bfloat16)
    st_ref[...] = (x_ref[...].astype(jnp.float32) + steps[section] * moving).astype(jnp.bfloat16)
    copies = [
        pltpu.make_async_copy(st_ref, stepped_hbm.at[1], sem.at[0]),
        pltpu.make_async_copy(v_ref, velocity_hbm.at[1], sem.at[1]),
    ]
    for c in copies:
        c.start()
    for c in copies:
        c.wait()


def second_round(where, steps, q, old, mine, theirs, fresh, fresh_q, fresh_mine, fresh_theirs, fresh_row, w_out, stepped, velocity):
    local, width = q.shape
    pair = jax.ShapeDtypeStruct(stepped.shape, stepped.dtype)
    return pl.pallas_call(
        functools.partial(second_kernel, fresh_row=fresh_row),
        out_shape=(pair, pair),
        in_specs=[SMEM, SMEM] + [VMEM] * 9 + [HBM, HBM],
        out_specs=(HBM, HBM),
        scratch_shapes=[
            pltpu.VMEM((local, width), jnp.bfloat16),
            pltpu.VMEM(old.shape, jnp.bfloat16),
            pltpu.VMEM(old.shape, jnp.bfloat16),
            pltpu.VMEM(old.shape, jnp.bfloat16),
            pltpu.SemaphoreType.DMA((2,)),
        ],
        input_output_aliases={11: 0, 12: 1},
        compiler_params=pltpu.CompilerParams(vmem_limit_bytes=12 << 20),
        cost_estimate=pl.CostEstimate(
            flops=4 * local * old.shape[1] * width, bytes_accessed=4 << 20, transcendentals=0
        ),
        name="second_round",
    )(where, steps, q, old, mine, theirs, fresh, fresh_q, fresh_mine, fresh_theirs, w_out, stepped, velocity)


def chip_body(latents, fresh_noise, levels, time_weight, w_query, w_key, w_value, w_out):
    per_section = lax.axis_size("tok") // SECTIONS
    where = (lax.axis_index("tok") // per_section).astype(jnp.int32).reshape(1)

    def needs(section, source):
        return source <= section + 1

    def from_section(block, slot):
        def move(i):
            section, within = i // per_section, i % per_section
            target = section ^ slot
            return target * per_section + within if needs(target, section) else None

        return permuted(block, "tok", move)

    def chip_swap(block, slot):
        def move(i):
            section = i // per_section
            if slot is None:
                return i ^ CORES if section == LAST else None
            return i ^ CORES if needs(section, section ^ slot) else None

        return permuted(block, "tok", move)

    def core_swap(block):
        return permuted(block, "tok", lambda i: i ^ 1)

    def after(value, *others):
        return lax.optimization_barrier((value, *others))[0]

    embedding, steps = lax.optimization_barrier(
        (level_embedding(levels, time_weight.shape[0] // 2), level_steps(levels))
    )
    w_key, w_value, w_query, w_out, mods = fetch(
        (w_key, w_value, w_query, w_out), embedding, time_weight
    )
    weights = (w_key, w_value, w_query)

    groups = ((0, None), (1, 3), (2,))
    own = {0: latents, None: fresh_noise}
    for slot in (3, 1, 2):
        own[slot] = from_section(latents, slot)
    across = {slot: chip_swap(own[slot], slot) for slot in (0, None, 1, 3)}
    mine, theirs, q = {}, {}, {}

    def work(group):
        mine[group], q[group] = project(
            where, group, [own[x] for x in group], [across[x] for x in group], mods, weights
        )
        theirs[group] = core_swap(mine[group])

    work(groups[0])
    own[2] = after(own[2], own[3], mine[groups[0]])
    across[2] = chip_swap(own[2], 2)
    work(groups[1])
    across[2] = after(across[2], theirs[groups[0]], mine[groups[1]])
    work(groups[2])
    slots = [x for group in groups for x in group if x is not None]
    stepped, velocity, mine2, q2, old = first_round(
        where, steps, groups, [mine[g] for g in groups], [theirs[g] for g in groups], [q[g] for g in groups],
        [own[x] for x in slots], [across[x] for x in slots], mods, weights, w_out,
    )
    theirs2 = core_swap(mine2)
    first = groups[0]
    return second_round(
        where, steps, q2, old, mine2, theirs2, fresh_noise, q[first], mine[first], theirs[first],
        first.index(None) * 2 * latents.shape[0], w_out, stepped, velocity,
    )


def solution(mesh):
    per_section = mesh.shape["tok"] // SECTIONS
    on_chips = per_section == 2 * CORES
    rows = P(("groups", "tok"), None)
    return jax.shard_map(
        chip_body if on_chips else gathered_body,
        mesh=mesh,
        in_specs=(rows, rows, P(), P(), P(), P(), P(), P()),
        out_specs=(P(None, ("groups", "tok"), None), P(None, ("groups", "tok"), None)),
        check_vma=False,
    )
```

```python
import functools
import math

import jax
import jax.numpy as jnp
from jax import lax
from jax.experimental import pallas as pl
from jax.experimental.pallas import tpu as pltpu
from jax.sharding import PartitionSpec as P


HEAD_DIM = 128
SECTIONS = 4
CORES = 2

epsilon = 1e-06


def permuted(block, axis, move):
    devices = range(lax.axis_size(axis))
    route = [(i, move(i)) for i in devices if move(i) is not None and move(i) in devices]
    return lax.ppermute(block, axis, route)


def level_embedding(levels, half_width):
    frequency = jnp.exp(-math.log(10000.0) * jnp.arange(half_width, dtype=jnp.float32) / half_width)
    angles = levels.astype(jnp.float32)[:, None] * frequency[None, :]
    return jnp.concatenate([jnp.cos(angles), jnp.sin(angles)], axis=1)


def embed_levels(levels, time_weight):
    return jnp.dot(
        level_embedding(levels, time_weight.shape[0] // 2),
        time_weight.astype(jnp.float32),
        precision=lax.Precision.HIGHEST,
    )


def level_steps(levels):
    previous = jnp.concatenate([jnp.zeros((1,), jnp.int32), levels[:-1]])
    return (previous - levels).astype(jnp.float32) / 1000.0


def gathered_body(latents, fresh_noise, levels, time_weight, w_query, w_key, w_value, w_out):
    local_rows = latents.shape[0]
    heads = w_query.shape[1] // HEAD_DIM
    per_section = lax.axis_size("tok") // SECTIONS
    span_rows = local_rows * per_section
    my_block = lax.axis_index("tok") // per_section
    section_ids = jnp.arange(SECTIONS, dtype=jnp.int32)
    mods = embed_levels(levels, time_weight)
    width = mods.shape[1] // 2
    shift_all, scale_all = mods[:, :width], mods[:, width:]
    chosen = section_ids == my_block
    shift_vec = jnp.sum(jnp.where(chosen[:, None], shift_all, 0.0), axis=0)
    scale_vec = jnp.sum(jnp.where(chosen[:, None], scale_all, 0.0), axis=0)
    step_size = jnp.sum(jnp.where(chosen, level_steps(levels), 0.0))

    def denoise_local(rows):
        rows_f = rows.astype(jnp.float32)
        normed = rows_f * lax.rsqrt(jnp.mean(rows_f * rows_f, axis=-1, keepdims=True) + epsilon)
        hidden = (normed * (1.0 + scale_vec) + shift_vec).astype(jnp.bfloat16)

        def project(weight):
            return jnp.dot(hidden, weight, preferred_element_type=jnp.float32).astype(jnp.bfloat16)

        queries = project(w_query).reshape(local_rows, heads, HEAD_DIM)
        keys = lax.all_gather(project(w_key), "tok", axis=0, tiled=True)
        values = lax.all_gather(project(w_value), "tok", axis=0, tiled=True)
        count = keys.shape[0]
        allowed = (jnp.arange(count, dtype=jnp.int32) // span_rows <= my_block)[None, None, :]
        scores = jnp.einsum(
            "rhd,phd->hrp",
            queries,
            keys.reshape(count, heads, HEAD_DIM),
            preferred_element_type=jnp.float32,
        ) / math.sqrt(HEAD_DIM)
        scores = jnp.where(allowed, scores, -1e30)
        best = jnp.max(scores, axis=-1)
        weights = jnp.where(allowed, jnp.exp(scores - best[..., None]), 0.0)
        denominator = jnp.sum(weights, axis=-1)
        summed = jnp.einsum(
            "hrp,phd->hrd",
            weights.astype(jnp.bfloat16),
            values.reshape(count, heads, HEAD_DIM),
            preferred_element_type=jnp.float32,
        )
        attended = (summed / denominator[..., None]).astype(jnp.bfloat16)
        attended = attended.transpose(1, 0, 2).reshape(local_rows, heads * HEAD_DIM)
        moving = jnp.dot(attended, w_out, preferred_element_type=jnp.float32)
        stepped = (rows_f + step_size * moving).astype(jnp.bfloat16)
        return (stepped, moving.astype(jnp.bfloat16))

    first, first_moving = denoise_local(latents)
    incoming = permuted(first, "tok", lambda i: i - per_section)
    second_input = jnp.where(my_block == SECTIONS - 1, fresh_noise, incoming)
    second, second_moving = denoise_local(second_input)
    return (jnp.stack([first, second]), jnp.stack([first_moving, second_moving]))


VMEM = pl.BlockSpec(memory_space=pltpu.VMEM)
SMEM = pl.BlockSpec(memory_space=pltpu.SMEM)
HBM = pl.BlockSpec(memory_space=pltpu.HBM)
LAST = SECTIONS - 1


def modulate(rows_f, scale_row, shift_row):
    normed = rows_f * lax.rsqrt(jnp.mean(rows_f * rows_f, axis=-1, keepdims=True) + epsilon)
    return (normed * (1.0 + scale_row) + shift_row).astype(jnp.bfloat16)


def dot(a, b):
    return jnp.dot(a, b, preferred_element_type=jnp.float32)


SHARPNESS = math.log2(math.e) / math.sqrt(HEAD_DIM)


def attend(queries, pairs, state=None):
    scores = [
        lax.dot_general(queries, keys, (((1,), (1,)), ((), ())), preferred_element_type=jnp.float32)
        for keys, _ in pairs
    ]
    top = functools.reduce(jnp.maximum, [jnp.max(s, axis=-1, keepdims=True) for s in scores])
    total, summed = 0.0, 0.0
    if state is not None:
        old_top, old_total, old_summed = state
        top = jnp.maximum(top, old_top)
        fade = jnp.exp2((old_top - top) * SHARPNESS)
        total, summed = old_total * fade, old_summed * fade
    for score, (_, values) in zip(scores, pairs):
        weights = jnp.exp2((score - top) * SHARPNESS)
        total = total + jnp.sum(weights, axis=-1, keepdims=True)
        summed = summed + dot(weights.astype(jnp.bfloat16), values)
    return top, total, summed


def head_columns(width):
    for head in range(width // HEAD_DIM):
        yield slice(head * HEAD_DIM, (head + 1) * HEAD_DIM), slice(
            width + head * HEAD_DIM, width + (head + 1) * HEAD_DIM
        )


def fetch_kernel(*refs, count):
    sources, embedding_ref, time_hbm = refs[:count], refs[count], refs[count + 1]
    outs, mods_ref = refs[count + 2 : 2 * count + 2], refs[2 * count + 2]
    time_ref, sem = refs[2 * count + 3 :]
    time_copy = pltpu.make_async_copy(time_hbm, time_ref, sem.at[count])
    time_copy.start()
    copies = [pltpu.make_async_copy(sources[i], outs[i], sem.at[i]) for i in range(count)]
    for c in copies:
        c.start()
    rest = embedding_ref[...]
    modulated = None
    time_copy.wait()
    for _ in range(3):
        term = rest.astype(jnp.bfloat16)
        rest = rest - term.astype(jnp.float32)
        product = dot(term, time_ref[...])
        modulated = product if modulated is None else modulated + product
    mods_ref[...] = modulated
    for c in copies:
        c.wait()


def fetch(arrays, embedding, time_weight):
    in_hbm = [pltpu.with_memory_space_constraint(a, pltpu.HBM) for a in (*arrays, time_weight)]
    return pl.pallas_call(
        functools.partial(fetch_kernel, count=len(arrays)),
        out_shape=[jax.ShapeDtypeStruct(a.shape, a.dtype) for a in arrays]
        + [jax.ShapeDtypeStruct((embedding.shape[0], time_weight.shape[1]), jnp.float32)],
        in_specs=[HBM] * len(arrays) + [VMEM, HBM],
        out_specs=[VMEM] * (len(arrays) + 1),
        scratch_shapes=[
            pltpu.VMEM(time_weight.shape, time_weight.dtype),
            pltpu.SemaphoreType.DMA((len(arrays) + 1,)),
        ],
        compiler_params=pltpu.CompilerParams(vmem_limit_bytes=6 << 20),
        cost_estimate=pl.CostEstimate(
            flops=0, bytes_accessed=sum(a.size * 2 for a in arrays), transcendentals=0
        ),
        name="fetch",
    )(*in_hbm[:-1], embedding, in_hbm[-1])


def project_kernel(where, *refs, slots):
    refs = list(refs)
    own = [refs.pop(0) for _ in slots]
    across = [refs.pop(0) for _ in slots]
    mods_ref, wk_ref, wv_ref, wq_ref, kv_ref, q_ref = refs
    depth, width = wk_ref.shape
    hidden = []
    for i, slot in enumerate(slots):
        rows_f = jnp.concatenate([own[i][...].astype(jnp.float32), across[i][...].astype(jnp.float32)])
        section = LAST if slot is None else where[0] ^ slot
        row = mods_ref[pl.ds(section, 1), :]
        hidden.append(modulate(rows_f, row[:, depth:], row[:, :depth]))
    hidden = jnp.concatenate(hidden)
    kv_ref[:, :width] = dot(hidden, wk_ref[...]).astype(jnp.bfloat16)
    kv_ref[:, width:] = dot(hidden, wv_ref[...]).astype(jnp.bfloat16)
    q_ref[...] = dot(hidden, wq_ref[...]).astype(jnp.bfloat16)


def project(where, slots, own, across, mods, weights):
    local, depth = own[0].shape
    width = weights[0].shape[1]
    rows = 2 * local * len(slots)
    return pl.pallas_call(
        functools.partial(project_kernel, slots=slots),
        out_shape=(
            jax.ShapeDtypeStruct((rows, 2 * width), jnp.bfloat16),
            jax.ShapeDtypeStruct((rows, width), jnp.bfloat16),
        ),
        in_specs=[SMEM] + [VMEM] * (2 * len(slots) + 4),
        out_specs=(VMEM, VMEM),
        compiler_params=pltpu.CompilerParams(vmem_limit_bytes=12 << 20),
        cost_estimate=pl.CostEstimate(
            flops=6 * rows * depth * width, bytes_accessed=2 << 20, transcendentals=0
        ),
        name="project",
    )(where, *own, *across, mods, *weights)


def state_shapes(rows, width):
    stat = jax.ShapeDtypeStruct((width // HEAD_DIM, rows, 1), jnp.float32)
    return stat, stat, jax.ShapeDtypeStruct((rows, width), jnp.float32)


def split(refs, *counts):
    refs = list(refs)
    return [[refs.pop(0) for _ in range(n)] for n in counts] + refs


def begin_kernel(where, *refs, groups):
    slots = [slot for group in groups for slot in group if slot is not None]
    known = len(groups) - 1
    kv_mine, kv_theirs, q_in, own_in, across_in, *refs = split(
        refs, known, known, len(groups), len(slots), len(slots)
    )
    q_ref, x_ref, top_ref, total_ref, sum_ref, kv_ref = refs
    local = own_in[0].shape[0]
    half, span = 2 * local, 4 * local
    width = q_ref.shape[1]
    section = where[0]
    at_last = section == LAST
    for g, group in enumerate(groups):
        for i, slot in enumerate(group):
            if slot is None:
                continue
            rows = slice(i * half, (i + 1) * half)
            source = section ^ slot
            base = pl.multiple_of(source * half, half)
            q_ref[pl.ds(base, half), :] = q_in[g][rows, :]
            n = slots.index(slot)
            x_ref[pl.ds(base, local), :] = own_in[n][...].astype(jnp.float32)
            x_ref[pl.ds(base + local, local), :] = across_in[n][...].astype(jnp.float32)
            if g < known:
                swapped = jnp.where(at_last, 1 - source, source)
                place = jnp.where(source > 1, source - 1, jnp.where(swapped == 1, 0, LAST))
                base = pl.multiple_of(place * span, span)
                kv_ref[pl.ds(base, half), :] = kv_mine[g][rows, :]
                kv_ref[pl.ds(base + half, half), :] = kv_theirs[g][rows, :]
    for s in range(1, SECTIONS):
        rows = slice((s - 1) * half, s * half)
        for head, (cols, v_cols) in enumerate(head_columns(width)):
            top, total, summed = attend(
                q_ref[s * half : (s + 1) * half, cols],
                [(kv_ref[0 : s * span, cols], kv_ref[0 : s * span, v_cols])],
            )
            top_ref[head, rows, :] = top
            total_ref[head, rows, :] = total
            sum_ref[rows, cols] = summed


def begin_first(where, groups, kv_mine, kv_theirs, q, own, across):
    local, depth = own[0].shape
    width = q[0].shape[1]
    half, span = 2 * local, 4 * local
    args = [*kv_mine[:-1], *kv_theirs[:-1], *q, *own, *across]
    return pl.pallas_call(
        functools.partial(begin_kernel, groups=groups),
        out_shape=(
            jax.ShapeDtypeStruct((SECTIONS * half, width), jnp.bfloat16),
            jax.ShapeDtypeStruct((SECTIONS * half, depth), jnp.float32),
            *state_shapes(LAST * half, width),
        ),
        in_specs=[SMEM] + [VMEM] * len(args),
        out_specs=(VMEM,) * 5,
        scratch_shapes=[pltpu.VMEM((SECTIONS * span, 2 * width), jnp.bfloat16)],
        compiler_params=pltpu.CompilerParams(vmem_limit_bytes=12 << 20),
        cost_estimate=pl.CostEstimate(
            flops=24 * half * span * width, bytes_accessed=2 << 20, transcendentals=0
        ),
        name="begin_first",
    )(where, *args)


def finish_kernel(where, steps, *refs, groups):
    known = len(groups)
    kv_mine, kv_theirs, refs_q = split(refs, known, known, 5)[:3]
    refs = list(refs)[2 * known + 5 :]
    q_ref, x_ref, top_ref, total_ref, sum_ref = refs_q
    mods_ref, wk_ref, wv_ref, wo_ref = refs[:4]
    stepped_hbm, velocity_hbm, kv2_ref, own2_ref, next_ref = refs[4:9]
    late_ref, o_ref, v_ref, st_ref, hid_ref, out_ref, sem = refs[9:]
    local, depth = next_ref.shape
    half = 2 * local
    width = wk_ref.shape[1]
    section = where[0]

    def set_late(slot):
        for g, group in enumerate(groups):
            if slot in group:
                rows = slice(group.index(slot) * half, (group.index(slot) + 1) * half)
                late_ref[0:half, :] = kv_mine[g][rows, :]
                late_ref[half:, :] = kv_theirs[g][rows, :]

    for s in range(LAST):
        pl.when(section == s)(functools.partial(set_late, s))
    pl.when(section == LAST)(functools.partial(set_late, LAST ^ 1))

    for head, (cols, v_cols) in enumerate(head_columns(width)):
        _, total, summed = attend(
            q_ref[half:, cols],
            [(late_ref[:, cols], late_ref[:, v_cols])],
            (top_ref[head], total_ref[head], sum_ref[:, cols]),
        )
        o_ref[:, cols] = (summed / total).astype(jnp.bfloat16)
    v_ref[...] = dot(o_ref[...], wo_ref[...])
    for s in range(1, SECTIONS):
        rows = slice((s - 1) * half, s * half)
        stepped = (x_ref[s * half : (s + 1) * half, :] + steps[s] * v_ref[rows, :]).astype(jnp.bfloat16)
        st_ref[rows, :] = stepped
        hid_ref[rows, :] = modulate(
            stepped.astype(jnp.float32), mods_ref[s - 1 : s, depth:], mods_ref[s - 1 : s, :depth]
        )

    @pl.when(section == 0)
    def _():
        for cols, v_cols in head_columns(width):
            _, total, summed = attend(q_ref[0:local, cols], [(late_ref[:, cols], late_ref[:, v_cols])])
            o_ref[0:local, cols] = (summed / total).astype(jnp.bfloat16)
        moving = dot(o_ref[0:local, :], wo_ref[...])
        out_ref[0] = (x_ref[0:local, :] + steps[0] * moving).astype(jnp.bfloat16)
        out_ref[1] = moving.astype(jnp.bfloat16)

    @pl.when(section > 0)
    def _():
        base = pl.multiple_of((section - 1) * half, half)
        out_ref[0] = st_ref[pl.ds(base, half), :][:local]
        out_ref[1] = v_ref[pl.ds(base, half), :][:local].astype(jnp.bfloat16)

    copies = [
        pltpu.make_async_copy(out_ref.at[0], stepped_hbm.at[0], sem.at[0]),
        pltpu.make_async_copy(out_ref.at[1], velocity_hbm.at[0], sem.at[1]),
    ]
    for c in copies:
        c.start()
    base = pl.multiple_of(jnp.minimum(section, LAST - 1) * half, half)
    own2_ref[...] = hid_ref[pl.ds(base, half), :][:local]
    next_ref[...] = st_ref[pl.ds(base, half), :][:local]
    kv2_ref[:, :width] = dot(hid_ref[...], wk_ref[...]).astype(jnp.bfloat16)
    kv2_ref[:, width:] = dot(hid_ref[...], wv_ref[...]).astype(jnp.bfloat16)
    for c in copies:
        c.wait()


def finish_first(where, steps, groups, kv_mine, kv_theirs, begun, mods, w_key, w_value, w_out):
    depth, width = w_key.shape
    half = begun[0].shape[0] // SECTIONS
    local = half // 2
    pair = jax.ShapeDtypeStruct((2, local, depth), jnp.bfloat16)
    one = jax.ShapeDtypeStruct((local, depth), jnp.bfloat16)
    args = [*kv_mine, *kv_theirs, *begun, mods, w_key, w_value, w_out]
    return pl.pallas_call(
        functools.partial(finish_kernel, groups=groups),
        out_shape=(pair, pair, jax.ShapeDtypeStruct((LAST * half, 2 * width), jnp.bfloat16), one, one),
        in_specs=[SMEM, SMEM] + [VMEM] * len(args),
        out_specs=(HBM, HBM, VMEM, VMEM, VMEM),
        scratch_shapes=[
            pltpu.VMEM((2 * half, 2 * width), jnp.bfloat16),
            pltpu.VMEM((LAST * half, width), jnp.bfloat16),
            pltpu.VMEM((LAST * half, depth), jnp.float32),
            pltpu.VMEM((LAST * half, depth), jnp.bfloat16),
            pltpu.VMEM((LAST * half, depth), jnp.bfloat16),
            pltpu.VMEM((2, local, depth), jnp.bfloat16),
            pltpu.SemaphoreType.DMA((2,)),
        ],
        compiler_params=pltpu.CompilerParams(vmem_limit_bytes=18 << 20),
        cost_estimate=pl.CostEstimate(
            flops=8 * LAST * half * depth * width, bytes_accessed=4 << 20, transcendentals=0
        ),
        name="finish_first",
    )(where, steps, *args)


def begin_second_kernel(
    where, own_ref, wq_ref, mine_ref, fresh_q_ref, fresh_mine_ref, fresh_theirs_ref,
    q_ref, top_ref, total_ref, sum_ref, *, fresh_row,
):
    local, width = q_ref.shape
    half = 2 * local
    section = where[0]

    def run(seen):
        for head, (cols, v_cols) in enumerate(head_columns(width)):
            top_ref[head], total_ref[head], sum_ref[:, cols] = attend(
                q_ref[:, cols], [(r[rows, cols], r[rows, v_cols]) for r, rows in seen]
            )

    for s in range(LAST):

        @pl.when(section == s)
        def _():
            q_ref[...] = dot(own_ref[...], wq_ref[...]).astype(jnp.bfloat16)
            run([(mine_ref, slice(0, (s + 1) * half))])

    @pl.when(section == LAST)
    def _():
        fresh_rows = slice(fresh_row, fresh_row + half)
        q_ref[...] = fresh_q_ref[fresh_row : fresh_row + local, :]
        run([(mine_ref, slice(0, LAST * half)), (fresh_mine_ref, fresh_rows), (fresh_theirs_ref, fresh_rows)])


def begin_second(where, own2, w_query, mine2, fresh_q, fresh_mine, fresh_theirs, fresh_row):
    local, width = own2.shape[0], w_query.shape[1]
    return pl.pallas_call(
        functools.partial(begin_second_kernel, fresh_row=fresh_row),
        out_shape=(jax.ShapeDtypeStruct((local, width), jnp.bfloat16), *state_shapes(local, width)),
        in_specs=[SMEM] + [VMEM] * 6,
        out_specs=(VMEM,) * 4,
        compiler_params=pltpu.CompilerParams(vmem_limit_bytes=8 << 20),
        cost_estimate=pl.CostEstimate(
            flops=4 * local * own2.shape[1] * width, bytes_accessed=2 << 20, transcendentals=0
        ),
        name="begin_second",
    )(where, own2, w_query, mine2, fresh_q, fresh_mine, fresh_theirs)


def finish_second_kernel(
    where, steps, q_ref, top_ref, total_ref, sum_ref, theirs_ref, old_ref, fresh_ref, wo_ref, _s, _v,
    stepped_hbm, velocity_hbm, o_ref, x_ref, out_ref, sem,
):
    local, width = q_ref.shape
    section = where[0]

    def run(seen):
        for head, (cols, v_cols) in enumerate(head_columns(width)):
            _, total, summed = attend(
                q_ref[:, cols],
                [(theirs_ref[0:seen, cols], theirs_ref[0:seen, v_cols])],
                (top_ref[head], total_ref[head], sum_ref[:, cols]),
            )
            o_ref[:, cols] = (summed / total).astype(jnp.bfloat16)

    for s in range(LAST):
        reached = (section >= s) if s == LAST - 1 else (section == s)
        pl.when(reached)(functools.partial(run, (s + 1) * 2 * local))
    x_ref[...] = old_ref[...]

    @pl.when(section == LAST)
    def _():
        x_ref[...] = fresh_ref[...]

    moving = dot(o_ref[...], wo_ref[...])
    out_ref[0] = (x_ref[...].astype(jnp.float32) + steps[section] * moving).astype(jnp.bfloat16)
    out_ref[1] = moving.astype(jnp.bfloat16)
    copies = [
        pltpu.make_async_copy(out_ref.at[0], stepped_hbm.at[1], sem.at[0]),
        pltpu.make_async_copy(out_ref.at[1], velocity_hbm.at[1], sem.at[1]),
    ]
    for c in copies:
        c.start()
    for c in copies:
        c.wait()


def finish_second(where, steps, begun, theirs2, old, fresh, w_out, stepped, velocity):
    local, width = begun[0].shape
    pair = jax.ShapeDtypeStruct(stepped.shape, stepped.dtype)
    return pl.pallas_call(
        finish_second_kernel,
        out_shape=(pair, pair),
        in_specs=[SMEM, SMEM] + [VMEM] * 8 + [HBM, HBM],
        out_specs=(HBM, HBM),
        scratch_shapes=[
            pltpu.VMEM((local, width), jnp.bfloat16),
            pltpu.VMEM(old.shape, jnp.bfloat16),
            pltpu.VMEM((2, *old.shape), jnp.bfloat16),
            pltpu.SemaphoreType.DMA((2,)),
        ],
        input_output_aliases={10: 0, 11: 1},
        compiler_params=pltpu.CompilerParams(vmem_limit_bytes=8 << 20),
        cost_estimate=pl.CostEstimate(
            flops=4 * local * old.shape[1] * width, bytes_accessed=4 << 20, transcendentals=0
        ),
        name="finish_second",
    )(where, steps, *begun, theirs2, old, fresh, w_out, stepped, velocity)


def chip_body(latents, fresh_noise, levels, time_weight, w_query, w_key, w_value, w_out):
    per_section = lax.axis_size("tok") // SECTIONS
    where = (lax.axis_index("tok") // per_section).astype(jnp.int32).reshape(1)

    def needs(section, source):
        return source <= section + 1

    def from_section(block, slot):
        def move(i):
            section, within = i // per_section, i % per_section
            target = section ^ slot
            return target * per_section + within if needs(target, section) else None

        return permuted(block, "tok", move)

    def chip_swap(block, slot):
        def move(i):
            section = i // per_section
            if slot is None:
                return i ^ CORES if section == LAST else None
            return i ^ CORES if needs(section, section ^ slot) else None

        return permuted(block, "tok", move)

    def core_swap(block):
        return permuted(block, "tok", lambda i: i ^ 1)

    def after(value, *others):
        return lax.optimization_barrier((value, *others))[0]

    embedding, steps = lax.optimization_barrier(
        (level_embedding(levels, time_weight.shape[0] // 2), level_steps(levels))
    )
    w_key, w_value, w_query, w_out, mods = fetch(
        (w_key, w_value, w_query, w_out), embedding, time_weight
    )
    weights = (w_key, w_value, w_query)

    groups = ((0, None), (1, 3), (2,))
    own = {0: latents, None: fresh_noise}
    for slot in (3, 1, 2):
        own[slot] = from_section(latents, slot)
    across = {slot: chip_swap(own[slot], slot) for slot in (0, None, 3)}
    across[1] = from_section(across[0], 1)
    mine, theirs, q = {}, {}, {}

    def work(group):
        mine[group], q[group] = project(
            where, group, [own[x] for x in group], [across[x] for x in group], mods, weights
        )
        theirs[group] = core_swap(mine[group])

    work(groups[0])
    own[2] = after(own[2], own[3], mine[groups[0]])
    across[2] = chip_swap(own[2], 2)
    work(groups[1])
    across[2] = after(across[2], theirs[groups[0]], mine[groups[1]])
    work(groups[2])
    slots = [x for group in groups for x in group if x is not None]
    all_mine, all_theirs = [mine[g] for g in groups], [theirs[g] for g in groups]
    begun = begin_first(
        where, groups, all_mine, all_theirs, [q[g] for g in groups],
        [own[x] for x in slots], [across[x] for x in slots],
    )
    stepped, velocity, mine2, own2, old = finish_first(
        where, steps, groups, all_mine, all_theirs, begun, mods, w_key, w_value, w_out
    )
    theirs2 = core_swap(mine2)
    first = groups[0]
    begun = begin_second(
        where, own2, w_query, mine2, q[first], mine[first], theirs[first],
        first.index(None) * 2 * latents.shape[0],
    )
    return finish_second(where, steps, begun, theirs2, old, fresh_noise, w_out, stepped, velocity)


def solution(mesh):
    per_section = mesh.shape["tok"] // SECTIONS
    on_chips = per_section == 2 * CORES
    rows = P(("groups", "tok"), None)
    return jax.shard_map(
        chip_body if on_chips else gathered_body,
        mesh=mesh,
        in_specs=(rows, rows, P(), P(), P(), P(), P(), P()),
        out_specs=(P(None, ("groups", "tok"), None), P(None, ("groups", "tok"), None)),
        check_vma=False,
    )
```

```python
import functools
import math

import jax
import jax.numpy as jnp
from jax import lax
from jax.experimental import pallas as pl
from jax.experimental.pallas import tpu as pltpu
from jax.sharding import PartitionSpec as P


HEAD_DIM = 128
SECTIONS = 4
CORES = 2

epsilon = 1e-06


def permuted(block, axis, move):
    devices = range(lax.axis_size(axis))
    route = [(i, move(i)) for i in devices if move(i) is not None and move(i) in devices]
    return lax.ppermute(block, axis, route)


def level_embedding(levels, half_width):
    frequency = jnp.exp(-math.log(10000.0) * jnp.arange(half_width, dtype=jnp.float32) / half_width)
    angles = levels.astype(jnp.float32)[:, None] * frequency[None, :]
    return jnp.concatenate([jnp.cos(angles), jnp.sin(angles)], axis=1)


def embed_levels(levels, time_weight):
    return jnp.dot(
        level_embedding(levels, time_weight.shape[0] // 2),
        time_weight.astype(jnp.float32),
        precision=lax.Precision.HIGHEST,
    )


def level_steps(levels):
    previous = jnp.concatenate([jnp.zeros((1,), jnp.int32), levels[:-1]])
    return (previous - levels).astype(jnp.float32) / 1000.0


def gathered_body(latents, fresh_noise, levels, time_weight, w_query, w_key, w_value, w_out):
    local_rows = latents.shape[0]
    heads = w_query.shape[1] // HEAD_DIM
    per_section = lax.axis_size("tok") // SECTIONS
    span_rows = local_rows * per_section
    my_block = lax.axis_index("tok") // per_section
    section_ids = jnp.arange(SECTIONS, dtype=jnp.int32)
    mods = embed_levels(levels, time_weight)
    width = mods.shape[1] // 2
    shift_all, scale_all = mods[:, :width], mods[:, width:]
    chosen = section_ids == my_block
    shift_vec = jnp.sum(jnp.where(chosen[:, None], shift_all, 0.0), axis=0)
    scale_vec = jnp.sum(jnp.where(chosen[:, None], scale_all, 0.0), axis=0)
    step_size = jnp.sum(jnp.where(chosen, level_steps(levels), 0.0))

    def denoise_local(rows):
        rows_f = rows.astype(jnp.float32)
        normed = rows_f * lax.rsqrt(jnp.mean(rows_f * rows_f, axis=-1, keepdims=True) + epsilon)
        hidden = (normed * (1.0 + scale_vec) + shift_vec).astype(jnp.bfloat16)

        def project(weight):
            return jnp.dot(hidden, weight, preferred_element_type=jnp.float32).astype(jnp.bfloat16)

        queries = project(w_query).reshape(local_rows, heads, HEAD_DIM)
        keys = lax.all_gather(project(w_key), "tok", axis=0, tiled=True)
        values = lax.all_gather(project(w_value), "tok", axis=0, tiled=True)
        count = keys.shape[0]
        allowed = (jnp.arange(count, dtype=jnp.int32) // span_rows <= my_block)[None, None, :]
        scores = jnp.einsum(
            "rhd,phd->hrp",
            queries,
            keys.reshape(count, heads, HEAD_DIM),
            preferred_element_type=jnp.float32,
        ) / math.sqrt(HEAD_DIM)
        scores = jnp.where(allowed, scores, -1e30)
        best = jnp.max(scores, axis=-1)
        weights = jnp.where(allowed, jnp.exp(scores - best[..., None]), 0.0)
        denominator = jnp.sum(weights, axis=-1)
        summed = jnp.einsum(
            "hrp,phd->hrd",
            weights.astype(jnp.bfloat16),
            values.reshape(count, heads, HEAD_DIM),
            preferred_element_type=jnp.float32,
        )
        attended = (summed / denominator[..., None]).astype(jnp.bfloat16)
        attended = attended.transpose(1, 0, 2).reshape(local_rows, heads * HEAD_DIM)
        moving = jnp.dot(attended, w_out, preferred_element_type=jnp.float32)
        stepped = (rows_f + step_size * moving).astype(jnp.bfloat16)
        return (stepped, moving.astype(jnp.bfloat16))

    first, first_moving = denoise_local(latents)
    incoming = permuted(first, "tok", lambda i: i - per_section)
    second_input = jnp.where(my_block == SECTIONS - 1, fresh_noise, incoming)
    second, second_moving = denoise_local(second_input)
    return (jnp.stack([first, second]), jnp.stack([first_moving, second_moving]))


VMEM = pl.BlockSpec(memory_space=pltpu.VMEM)
SMEM = pl.BlockSpec(memory_space=pltpu.SMEM)
HBM = pl.BlockSpec(memory_space=pltpu.HBM)
LAST = SECTIONS - 1


def modulate(rows_f, scale_row, shift_row):
    normed = rows_f * lax.rsqrt(jnp.mean(rows_f * rows_f, axis=-1, keepdims=True) + epsilon)
    return (normed * (1.0 + scale_row) + shift_row).astype(jnp.bfloat16)


def dot(a, b):
    return jnp.dot(a, b, preferred_element_type=jnp.float32)


SHARPNESS = math.log2(math.e) / math.sqrt(HEAD_DIM)


def score(queries, pairs):
    return [
        lax.dot_general(queries(), keys(), (((1,), (1,)), ((), ())), preferred_element_type=jnp.float32)
        for keys, _ in pairs
    ]


def weigh(scores, pairs, state=None):
    top = functools.reduce(jnp.maximum, [jnp.max(s, axis=-1, keepdims=True) for s in scores])
    total, summed = 0.0, 0.0
    if state is not None:
        old_top, old_total, old_summed = state()
        top = jnp.maximum(top, old_top)
        fade = jnp.exp2((old_top - top) * SHARPNESS)
        total, summed = old_total * fade, old_summed * fade
    for part, (_, values) in zip(scores, pairs):
        weights = jnp.exp2((part - top) * SHARPNESS)
        total = total + jnp.sum(weights, axis=-1, keepdims=True)
        summed = summed + dot(weights.astype(jnp.bfloat16), values())
    return top, total, summed


AHEAD = 3


def attend_all(jobs):
    pending = [score(*job[:2]) for job in jobs[:AHEAD]]
    for i, (_, pairs, state, emit) in enumerate(jobs):
        if i + AHEAD < len(jobs):
            pending.append(score(*jobs[i + AHEAD][:2]))
        emit(*weigh(pending.pop(0), pairs, state))


def view(ref, *where):
    return lambda: ref[where]


def head_columns(width):
    for head in range(width // HEAD_DIM):
        yield slice(head * HEAD_DIM, (head + 1) * HEAD_DIM), slice(
            width + head * HEAD_DIM, width + (head + 1) * HEAD_DIM
        )


def fetch_kernel(*refs, count):
    sources, embedding_ref, time_hbm = refs[:count], refs[count], refs[count + 1]
    outs, mods_ref = refs[count + 2 : 2 * count + 2], refs[2 * count + 2]
    time_ref, sem = refs[2 * count + 3 :]
    time_copy = pltpu.make_async_copy(time_hbm, time_ref, sem.at[count])
    time_copy.start()
    copies = [pltpu.make_async_copy(sources[i], outs[i], sem.at[i]) for i in range(count)]
    for c in copies:
        c.start()
    rest = embedding_ref[...]
    modulated = None
    time_copy.wait()
    for _ in range(3):
        term = rest.astype(jnp.bfloat16)
        rest = rest - term.astype(jnp.float32)
        product = dot(term, time_ref[...])
        modulated = product if modulated is None else modulated + product
    mods_ref[...] = modulated
    for c in copies:
        c.wait()


def fetch(arrays, embedding, time_weight):
    in_hbm = [pltpu.with_memory_space_constraint(a, pltpu.HBM) for a in (*arrays, time_weight)]
    return pl.pallas_call(
        functools.partial(fetch_kernel, count=len(arrays)),
        out_shape=[jax.ShapeDtypeStruct(a.shape, a.dtype) for a in arrays]
        + [jax.ShapeDtypeStruct((embedding.shape[0], time_weight.shape[1]), jnp.float32)],
        in_specs=[HBM] * len(arrays) + [VMEM, HBM],
        out_specs=[VMEM] * (len(arrays) + 1),
        scratch_shapes=[
            pltpu.VMEM(time_weight.shape, time_weight.dtype),
            pltpu.SemaphoreType.DMA((len(arrays) + 1,)),
        ],
        compiler_params=pltpu.CompilerParams(vmem_limit_bytes=6 << 20),
        cost_estimate=pl.CostEstimate(
            flops=0, bytes_accessed=sum(a.size * 2 for a in arrays), transcendentals=0
        ),
        name="fetch",
    )(*in_hbm[:-1], embedding, in_hbm[-1])


def project_kernel(where, *refs, slots):
    refs = list(refs)
    own = [refs.pop(0) for _ in slots]
    across = [refs.pop(0) for _ in slots]
    mods_ref, wk_ref, wv_ref, wq_ref, kv_ref, q_ref = refs
    depth, width = wk_ref.shape
    hidden = []
    for i, slot in enumerate(slots):
        rows_f = jnp.concatenate([own[i][...].astype(jnp.float32), across[i][...].astype(jnp.float32)])
        section = LAST if slot is None else where[0] ^ slot
        row = mods_ref[pl.ds(section, 1), :]
        hidden.append(modulate(rows_f, row[:, depth:], row[:, :depth]))
    hidden = jnp.concatenate(hidden)
    kv_ref[:, :width] = dot(hidden, wk_ref[...]).astype(jnp.bfloat16)
    kv_ref[:, width:] = dot(hidden, wv_ref[...]).astype(jnp.bfloat16)
    q_ref[...] = dot(hidden, wq_ref[...]).astype(jnp.bfloat16)


def project(where, slots, own, across, mods, weights):
    local, depth = own[0].shape
    width = weights[0].shape[1]
    rows = 2 * local * len(slots)
    return pl.pallas_call(
        functools.partial(project_kernel, slots=slots),
        out_shape=(
            jax.ShapeDtypeStruct((rows, 2 * width), jnp.bfloat16),
            jax.ShapeDtypeStruct((rows, width), jnp.bfloat16),
        ),
        in_specs=[SMEM] + [VMEM] * (2 * len(slots) + 4),
        out_specs=(VMEM, VMEM),
        compiler_params=pltpu.CompilerParams(vmem_limit_bytes=12 << 20),
        cost_estimate=pl.CostEstimate(
            flops=6 * rows * depth * width, bytes_accessed=2 << 20, transcendentals=0
        ),
        name="project",
    )(where, *own, *across, mods, *weights)


def state_shapes(rows, width):
    stat = jax.ShapeDtypeStruct((width // HEAD_DIM, rows, 1), jnp.float32)
    return stat, stat, jax.ShapeDtypeStruct((rows, width), jnp.float32)


def split(refs, *counts):
    refs = list(refs)
    return [[refs.pop(0) for _ in range(n)] for n in counts] + refs


def begin_kernel(where, *refs, groups):
    slots = [slot for group in groups for slot in group if slot is not None]
    known = len(groups) - 1
    kv_mine, kv_theirs, q_in, own_in, across_in, *refs = split(
        refs, known, known, len(groups), len(slots), len(slots)
    )
    q_ref, x_ref, top_ref, total_ref, sum_ref, kv_ref = refs
    local = own_in[0].shape[0]
    half, span = 2 * local, 4 * local
    width = q_ref.shape[1]
    section = where[0]
    at_last = section == LAST
    for g, group in enumerate(groups):
        for i, slot in enumerate(group):
            if slot is None:
                continue
            rows = slice(i * half, (i + 1) * half)
            source = section ^ slot
            base = pl.multiple_of(source * half, half)
            q_ref[pl.ds(base, half), :] = q_in[g][rows, :]
            n = slots.index(slot)
            x_ref[pl.ds(base, local), :] = own_in[n][...].astype(jnp.float32)
            x_ref[pl.ds(base + local, local), :] = across_in[n][...].astype(jnp.float32)
            if g < known:
                swapped = jnp.where(at_last, 1 - source, source)
                place = jnp.where(source > 1, source - 1, jnp.where(swapped == 1, 0, LAST))
                base = pl.multiple_of(place * span, span)
                kv_ref[pl.ds(base, half), :] = kv_mine[g][rows, :]
                kv_ref[pl.ds(base + half, half), :] = kv_theirs[g][rows, :]
    jobs = []
    for s in range(1, SECTIONS):
        rows, seen = slice((s - 1) * half, s * half), slice(0, s * span)
        for head, (cols, v_cols) in enumerate(head_columns(width)):

            def emit(top, total, summed, head=head, rows=rows, cols=cols):
                top_ref[head, rows, :] = top
                total_ref[head, rows, :] = total
                sum_ref[rows, cols] = summed

            queries = view(q_ref, slice(s * half, (s + 1) * half), cols)
            jobs.append((queries, [(view(kv_ref, seen, cols), view(kv_ref, seen, v_cols))], None, emit))
    attend_all(jobs)


def begin_first(where, groups, kv_mine, kv_theirs, q, own, across):
    local, depth = own[0].shape
    width = q[0].shape[1]
    half, span = 2 * local, 4 * local
    args = [*kv_mine[:-1], *kv_theirs[:-1], *q, *own, *across]
    return pl.pallas_call(
        functools.partial(begin_kernel, groups=groups),
        out_shape=(
            jax.ShapeDtypeStruct((SECTIONS * half, width), jnp.bfloat16),
            jax.ShapeDtypeStruct((SECTIONS * half, depth), jnp.float32),
            *state_shapes(LAST * half, width),
        ),
        in_specs=[SMEM] + [VMEM] * len(args),
        out_specs=(VMEM,) * 5,
        scratch_shapes=[pltpu.VMEM((SECTIONS * span, 2 * width), jnp.bfloat16)],
        compiler_params=pltpu.CompilerParams(vmem_limit_bytes=12 << 20),
        cost_estimate=pl.CostEstimate(
            flops=24 * half * span * width, bytes_accessed=2 << 20, transcendentals=0
        ),
        name="begin_first",
    )(where, *args)


def finish_kernel(where, steps, *refs, groups):
    known = len(groups)
    kv_mine, kv_theirs, refs_q = split(refs, known, known, 5)[:3]
    refs = list(refs)[2 * known + 5 :]
    q_ref, x_ref, top_ref, total_ref, sum_ref = refs_q
    mods_ref, wk_ref, wv_ref, wo_ref = refs[:4]
    stepped_hbm, velocity_hbm, kv2_ref, own2_ref, next_ref = refs[4:9]
    late_ref, o_ref, v_ref, st_ref, hid_ref, out_ref, sem = refs[9:]
    local, depth = next_ref.shape
    half = 2 * local
    width = wk_ref.shape[1]
    section = where[0]

    def set_late(slot):
        for g, group in enumerate(groups):
            if slot in group:
                rows = slice(group.index(slot) * half, (group.index(slot) + 1) * half)
                late_ref[0:half, :] = kv_mine[g][rows, :]
                late_ref[half:, :] = kv_theirs[g][rows, :]

    for s in range(LAST):
        pl.when(section == s)(functools.partial(set_late, s))
    pl.when(section == LAST)(functools.partial(set_late, LAST ^ 1))

    everything = slice(None)

    def late_jobs(queries, into, with_state):
        for head, (cols, v_cols) in enumerate(head_columns(width)):

            def emit(_, total, summed, cols=cols):
                o_ref[into, cols] = (summed / total).astype(jnp.bfloat16)

            def state(head=head, cols=cols):
                return top_ref[head, into], total_ref[head, into], sum_ref[into, cols]

            pairs = [(view(late_ref, everything, cols), view(late_ref, everything, v_cols))]
            yield view(q_ref, queries, cols), pairs, state if with_state else None, emit

    attend_all(list(late_jobs(slice(half, SECTIONS * half), slice(0, LAST * half), True)))
    v_ref[...] = dot(o_ref[...], wo_ref[...])
    for s in range(1, SECTIONS):
        rows = slice((s - 1) * half, s * half)
        stepped = (x_ref[s * half : (s + 1) * half, :] + steps[s] * v_ref[rows, :]).astype(jnp.bfloat16)
        st_ref[rows, :] = stepped
        hid_ref[rows, :] = modulate(
            stepped.astype(jnp.float32), mods_ref[s - 1 : s, depth:], mods_ref[s - 1 : s, :depth]
        )

    @pl.when(section == 0)
    def _():
        attend_all(list(late_jobs(slice(0, local), slice(0, local), False)))
        moving = dot(o_ref[0:local, :], wo_ref[...])
        out_ref[0] = (x_ref[0:local, :] + steps[0] * moving).astype(jnp.bfloat16)
        out_ref[1] = moving.astype(jnp.bfloat16)

    @pl.when(section > 0)
    def _():
        base = pl.multiple_of((section - 1) * half, half)
        out_ref[0] = st_ref[pl.ds(base, half), :][:local]
        out_ref[1] = v_ref[pl.ds(base, half), :][:local].astype(jnp.bfloat16)

    copies = [
        pltpu.make_async_copy(out_ref.at[0], stepped_hbm.at[0], sem.at[0]),
        pltpu.make_async_copy(out_ref.at[1], velocity_hbm.at[0], sem.at[1]),
    ]
    for c in copies:
        c.start()
    base = pl.multiple_of(jnp.minimum(section, LAST - 1) * half, half)
    own2_ref[...] = hid_ref[pl.ds(base, half), :][:local]
    next_ref[...] = st_ref[pl.ds(base, half), :][:local]
    kv2_ref[:, :width] = dot(hid_ref[...], wk_ref[...]).astype(jnp.bfloat16)
    kv2_ref[:, width:] = dot(hid_ref[...], wv_ref[...]).astype(jnp.bfloat16)
    for c in copies:
        c.wait()


def finish_first(where, steps, groups, kv_mine, kv_theirs, begun, mods, w_key, w_value, w_out):
    depth, width = w_key.shape
    half = begun[0].shape[0] // SECTIONS
    local = half // 2
    pair = jax.ShapeDtypeStruct((2, local, depth), jnp.bfloat16)
    one = jax.ShapeDtypeStruct((local, depth), jnp.bfloat16)
    args = [*kv_mine, *kv_theirs, *begun, mods, w_key, w_value, w_out]
    return pl.pallas_call(
        functools.partial(finish_kernel, groups=groups),
        out_shape=(pair, pair, jax.ShapeDtypeStruct((LAST * half, 2 * width), jnp.bfloat16), one, one),
        in_specs=[SMEM, SMEM] + [VMEM] * len(args),
        out_specs=(HBM, HBM, VMEM, VMEM, VMEM),
        scratch_shapes=[
            pltpu.VMEM((2 * half, 2 * width), jnp.bfloat16),
            pltpu.VMEM((LAST * half, width), jnp.bfloat16),
            pltpu.VMEM((LAST * half, depth), jnp.float32),
            pltpu.VMEM((LAST * half, depth), jnp.bfloat16),
            pltpu.VMEM((LAST * half, depth), jnp.bfloat16),
            pltpu.VMEM((2, local, depth), jnp.bfloat16),
            pltpu.SemaphoreType.DMA((2,)),
        ],
        compiler_params=pltpu.CompilerParams(vmem_limit_bytes=18 << 20),
        cost_estimate=pl.CostEstimate(
            flops=8 * LAST * half * depth * width, bytes_accessed=4 << 20, transcendentals=0
        ),
        name="finish_first",
    )(where, steps, *args)


def begin_second_kernel(
    where, own_ref, wq_ref, mine_ref, fresh_q_ref, fresh_mine_ref, fresh_theirs_ref,
    q_ref, top_ref, total_ref, sum_ref, *, fresh_row,
):
    local, width = q_ref.shape
    half = 2 * local
    section = where[0]

    def run(seen):
        jobs = []
        for head, (cols, v_cols) in enumerate(head_columns(width)):

            def emit(top, total, summed, head=head, cols=cols):
                top_ref[head], total_ref[head], sum_ref[:, cols] = top, total, summed

            pairs = [(view(r, rows, cols), view(r, rows, v_cols)) for r, rows in seen]
            jobs.append((view(q_ref, slice(None), cols), pairs, None, emit))
        attend_all(jobs)

    for s in range(LAST):

        @pl.when(section == s)
        def _():
            q_ref[...] = dot(own_ref[...], wq_ref[...]).astype(jnp.bfloat16)
            run([(mine_ref, slice(0, (s + 1) * half))])

    @pl.when(section == LAST)
    def _():
        fresh_rows = slice(fresh_row, fresh_row + half)
        q_ref[...] = fresh_q_ref[fresh_row : fresh_row + local, :]
        run([(mine_ref, slice(0, LAST * half)), (fresh_mine_ref, fresh_rows), (fresh_theirs_ref, fresh_rows)])


def begin_second(where, own2, w_query, mine2, fresh_q, fresh_mine, fresh_theirs, fresh_row):
    local, width = own2.shape[0], w_query.shape[1]
    return pl.pallas_call(
        functools.partial(begin_second_kernel, fresh_row=fresh_row),
        out_shape=(jax.ShapeDtypeStruct((local, width), jnp.bfloat16), *state_shapes(local, width)),
        in_specs=[SMEM] + [VMEM] * 6,
        out_specs=(VMEM,) * 4,
        compiler_params=pltpu.CompilerParams(vmem_limit_bytes=8 << 20),
        cost_estimate=pl.CostEstimate(
            flops=4 * local * own2.shape[1] * width, bytes_accessed=2 << 20, transcendentals=0
        ),
        name="begin_second",
    )(where, own2, w_query, mine2, fresh_q, fresh_mine, fresh_theirs)


def finish_second_kernel(
    where, steps, q_ref, top_ref, total_ref, sum_ref, theirs_ref, old_ref, fresh_ref, wo_ref, _s, _v,
    stepped_hbm, velocity_hbm, o_ref, x_ref, out_ref, sem,
):
    local, width = q_ref.shape
    section = where[0]

    def run(seen):
        jobs = []
        for head, (cols, v_cols) in enumerate(head_columns(width)):

            def emit(_, total, summed, cols=cols):
                o_ref[:, cols] = (summed / total).astype(jnp.bfloat16)

            def state(head=head, cols=cols):
                return top_ref[head], total_ref[head], sum_ref[:, cols]

            pairs = [(view(theirs_ref, slice(0, seen), cols), view(theirs_ref, slice(0, seen), v_cols))]
            jobs.append((view(q_ref, slice(None), cols), pairs, state, emit))
        attend_all(jobs)

    for s in range(LAST):
        reached = (section >= s) if s == LAST - 1 else (section == s)
        pl.when(reached)(functools.partial(run, (s + 1) * 2 * local))
    x_ref[...] = old_ref[...]

    @pl.when(section == LAST)
    def _():
        x_ref[...] = fresh_ref[...]

    moving = dot(o_ref[...], wo_ref[...])
    out_ref[0] = (x_ref[...].astype(jnp.float32) + steps[section] * moving).astype(jnp.bfloat16)
    out_ref[1] = moving.astype(jnp.bfloat16)
    copies = [
        pltpu.make_async_copy(out_ref.at[0], stepped_hbm.at[1], sem.at[0]),
        pltpu.make_async_copy(out_ref.at[1], velocity_hbm.at[1], sem.at[1]),
    ]
    for c in copies:
        c.start()
    for c in copies:
        c.wait()


def finish_second(where, steps, begun, theirs2, old, fresh, w_out, stepped, velocity):
    local, width = begun[0].shape
    pair = jax.ShapeDtypeStruct(stepped.shape, stepped.dtype)
    return pl.pallas_call(
        finish_second_kernel,
        out_shape=(pair, pair),
        in_specs=[SMEM, SMEM] + [VMEM] * 8 + [HBM, HBM],
        out_specs=(HBM, HBM),
        scratch_shapes=[
            pltpu.VMEM((local, width), jnp.bfloat16),
            pltpu.VMEM(old.shape, jnp.bfloat16),
            pltpu.VMEM((2, *old.shape), jnp.bfloat16),
            pltpu.SemaphoreType.DMA((2,)),
        ],
        input_output_aliases={10: 0, 11: 1},
        compiler_params=pltpu.CompilerParams(vmem_limit_bytes=8 << 20),
        cost_estimate=pl.CostEstimate(
            flops=4 * local * old.shape[1] * width, bytes_accessed=4 << 20, transcendentals=0
        ),
        name="finish_second",
    )(where, steps, *begun, theirs2, old, fresh, w_out, stepped, velocity)


def chip_body(latents, fresh_noise, levels, time_weight, w_query, w_key, w_value, w_out):
    per_section = lax.axis_size("tok") // SECTIONS
    where = (lax.axis_index("tok") // per_section).astype(jnp.int32).reshape(1)

    def needs(section, source):
        return source <= section + 1

    def from_section(block, slot):
        def move(i):
            section, within = i // per_section, i % per_section
            target = section ^ slot
            return target * per_section + within if needs(target, section) else None

        return permuted(block, "tok", move)

    def chip_swap(block, slot):
        def move(i):
            section = i // per_section
            if slot is None:
                return i ^ CORES if section == LAST else None
            return i ^ CORES if needs(section, section ^ slot) else None

        return permuted(block, "tok", move)

    def core_swap(block):
        return permuted(block, "tok", lambda i: i ^ 1)

    def after(value, *others):
        return lax.optimization_barrier((value, *others))[0]

    embedding, steps = lax.optimization_barrier(
        (level_embedding(levels, time_weight.shape[0] // 2), level_steps(levels))
    )
    w_key, w_value, w_query, w_out, mods = fetch(
        (w_key, w_value, w_query, w_out), embedding, time_weight
    )
    weights = (w_key, w_value, w_query)

    groups = ((0, None), (1, 3), (2,))
    own = {0: latents, None: fresh_noise}
    for slot in (3, 1, 2):
        own[slot] = from_section(latents, slot)
    across = {slot: chip_swap(own[slot], slot) for slot in (0, None, 3)}
    across[1] = from_section(across[0], 1)
    mine, theirs, q = {}, {}, {}

    def work(group):
        mine[group], q[group] = project(
            where, group, [own[x] for x in group], [across[x] for x in group], mods, weights
        )
        theirs[group] = core_swap(mine[group])

    work(groups[0])
    own[2] = after(own[2], own[3], mine[groups[0]])
    across[2] = chip_swap(own[2], 2)
    work(groups[1])
    across[2] = after(across[2], theirs[groups[0]], mine[groups[1]])
    work(groups[2])
    slots = [x for group in groups for x in group if x is not None]
    all_mine, all_theirs = [mine[g] for g in groups], [theirs[g] for g in groups]
    begun = begin_first(
        where, groups, all_mine, all_theirs, [q[g] for g in groups],
        [own[x] for x in slots], [across[x] for x in slots],
    )
    stepped, velocity, mine2, own2, old = finish_first(
        where, steps, groups, all_mine, all_theirs, begun, mods, w_key, w_value, w_out
    )
    theirs2 = core_swap(mine2)
    first = groups[0]
    begun = begin_second(
        where, own2, w_query, mine2, q[first], mine[first], theirs[first],
        first.index(None) * 2 * latents.shape[0],
    )
    return finish_second(where, steps, begun, theirs2, old, fresh_noise, w_out, stepped, velocity)


def solution(mesh):
    per_section = mesh.shape["tok"] // SECTIONS
    on_chips = per_section == 2 * CORES
    rows = P(("groups", "tok"), None)
    return jax.shard_map(
        chip_body if on_chips else gathered_body,
        mesh=mesh,
        in_specs=(rows, rows, P(), P(), P(), P(), P(), P()),
        out_specs=(P(None, ("groups", "tok"), None), P(None, ("groups", "tok"), None)),
        check_vma=False,
    )
```

```python
import functools
import math

import jax
import jax.numpy as jnp
from jax import lax
from jax.experimental import pallas as pl
from jax.experimental.pallas import tpu as pltpu
from jax.sharding import PartitionSpec as P


HEAD_DIM = 128
SECTIONS = 4
CORES = 2

epsilon = 1e-06


def permuted(block, axis, move):
    devices = range(lax.axis_size(axis))
    route = [(i, move(i)) for i in devices if move(i) is not None and move(i) in devices]
    return lax.ppermute(block, axis, route)


def level_embedding(levels, half_width):
    frequency = jnp.exp(-math.log(10000.0) * jnp.arange(half_width, dtype=jnp.float32) / half_width)
    angles = levels.astype(jnp.float32)[:, None] * frequency[None, :]
    return jnp.concatenate([jnp.cos(angles), jnp.sin(angles)], axis=1)


def embed_levels(levels, time_weight):
    return jnp.dot(
        level_embedding(levels, time_weight.shape[0] // 2),
        time_weight.astype(jnp.float32),
        precision=lax.Precision.HIGHEST,
    )


def level_steps(levels):
    previous = jnp.concatenate([jnp.zeros((1,), jnp.int32), levels[:-1]])
    return (previous - levels).astype(jnp.float32) / 1000.0


def gathered_body(latents, fresh_noise, levels, time_weight, w_query, w_key, w_value, w_out):
    local_rows = latents.shape[0]
    heads = w_query.shape[1] // HEAD_DIM
    per_section = lax.axis_size("tok") // SECTIONS
    span_rows = local_rows * per_section
    my_block = lax.axis_index("tok") // per_section
    section_ids = jnp.arange(SECTIONS, dtype=jnp.int32)
    mods = embed_levels(levels, time_weight)
    width = mods.shape[1] // 2
    shift_all, scale_all = mods[:, :width], mods[:, width:]
    chosen = section_ids == my_block
    shift_vec = jnp.sum(jnp.where(chosen[:, None], shift_all, 0.0), axis=0)
    scale_vec = jnp.sum(jnp.where(chosen[:, None], scale_all, 0.0), axis=0)
    step_size = jnp.sum(jnp.where(chosen, level_steps(levels), 0.0))

    def denoise_local(rows):
        rows_f = rows.astype(jnp.float32)
        normed = rows_f * lax.rsqrt(jnp.mean(rows_f * rows_f, axis=-1, keepdims=True) + epsilon)
        hidden = (normed * (1.0 + scale_vec) + shift_vec).astype(jnp.bfloat16)

        def project(weight):
            return jnp.dot(hidden, weight, preferred_element_type=jnp.float32).astype(jnp.bfloat16)

        queries = project(w_query).reshape(local_rows, heads, HEAD_DIM)
        keys = lax.all_gather(project(w_key), "tok", axis=0, tiled=True)
        values = lax.all_gather(project(w_value), "tok", axis=0, tiled=True)
        count = keys.shape[0]
        allowed = (jnp.arange(count, dtype=jnp.int32) // span_rows <= my_block)[None, None, :]
        scores = jnp.einsum(
            "rhd,phd->hrp",
            queries,
            keys.reshape(count, heads, HEAD_DIM),
            preferred_element_type=jnp.float32,
        ) / math.sqrt(HEAD_DIM)
        scores = jnp.where(allowed, scores, -1e30)
        best = jnp.max(scores, axis=-1)
        weights = jnp.where(allowed, jnp.exp(scores - best[..., None]), 0.0)
        denominator = jnp.sum(weights, axis=-1)
        summed = jnp.einsum(
            "hrp,phd->hrd",
            weights.astype(jnp.bfloat16),
            values.reshape(count, heads, HEAD_DIM),
            preferred_element_type=jnp.float32,
        )
        attended = (summed / denominator[..., None]).astype(jnp.bfloat16)
        attended = attended.transpose(1, 0, 2).reshape(local_rows, heads * HEAD_DIM)
        moving = jnp.dot(attended, w_out, preferred_element_type=jnp.float32)
        stepped = (rows_f + step_size * moving).astype(jnp.bfloat16)
        return (stepped, moving.astype(jnp.bfloat16))

    first, first_moving = denoise_local(latents)
    incoming = permuted(first, "tok", lambda i: i - per_section)
    second_input = jnp.where(my_block == SECTIONS - 1, fresh_noise, incoming)
    second, second_moving = denoise_local(second_input)
    return (jnp.stack([first, second]), jnp.stack([first_moving, second_moving]))


VMEM = pl.BlockSpec(memory_space=pltpu.VMEM)
SMEM = pl.BlockSpec(memory_space=pltpu.SMEM)
HBM = pl.BlockSpec(memory_space=pltpu.HBM)
LAST = SECTIONS - 1


def modulate(rows_f, scale_row, shift_row):
    normed = rows_f * lax.rsqrt(jnp.mean(rows_f * rows_f, axis=-1, keepdims=True) + epsilon)
    return (normed * (1.0 + scale_row) + shift_row).astype(jnp.bfloat16)


def dot(a, b):
    return jnp.dot(a, b, preferred_element_type=jnp.float32)


SHARPNESS = math.log2(math.e) / math.sqrt(HEAD_DIM)


def score(queries, pairs):
    return [
        lax.dot_general(queries(), keys(), (((1,), (1,)), ((), ())), preferred_element_type=jnp.float32)
        for keys, _ in pairs
    ]


def weigh(scores, pairs, state=None):
    top = functools.reduce(jnp.maximum, [jnp.max(s, axis=-1, keepdims=True) for s in scores])
    rows = top.shape[0]
    top = jnp.broadcast_to(top, (rows, HEAD_DIM))
    if state is not None:
        old_top, old_total, old_summed = state()
        top = jnp.maximum(top, old_top)
    total, summed = 0.0, 0.0
    for part, (_, values) in zip(scores, pairs):
        rounded = []
        sums = []
        for low in range(0, part.shape[1], HEAD_DIM):
            piece = part[:, low : low + HEAD_DIM]
            weights = jnp.exp2((piece - top[:, : piece.shape[1]]) * SHARPNESS)
            sums.append(jnp.sum(weights, axis=-1, keepdims=True) if piece.shape[1] < HEAD_DIM else weights)
            rounded.append(weights.astype(jnp.bfloat16))
        full = [w for w in sums if w.shape[1] == HEAD_DIM]
        for w in [functools.reduce(jnp.add, full)] * (len(full) > 0) + [w for w in sums if w.shape[1] < HEAD_DIM]:
            total = total + jnp.sum(w, axis=-1, keepdims=True)
        summed = summed + dot(jnp.concatenate(rounded, axis=1), values())
    total = jnp.broadcast_to(total, (rows, HEAD_DIM))
    if state is not None:
        fade = jnp.exp2((old_top - top) * SHARPNESS)
        total, summed = old_total * fade + total, old_summed * fade + summed
    return top, total, summed


AHEAD = 3


def attend_all(jobs):
    pending = [score(*job[:2]) for job in jobs[:AHEAD]]
    for i, (_, pairs, state, emit) in enumerate(jobs):
        if i + AHEAD < len(jobs):
            pending.append(score(*jobs[i + AHEAD][:2]))
        emit(*weigh(pending.pop(0), pairs, state))


def view(ref, *where):
    return lambda: ref[where]


def head_columns(width):
    for head in range(width // HEAD_DIM):
        yield slice(head * HEAD_DIM, (head + 1) * HEAD_DIM), slice(
            width + head * HEAD_DIM, width + (head + 1) * HEAD_DIM
        )


def fetch_kernel(*refs, count):
    sources, embedding_ref, time_hbm = refs[:count], refs[count], refs[count + 1]
    outs, mods_ref = refs[count + 2 : 2 * count + 2], refs[2 * count + 2]
    time_ref, sem = refs[2 * count + 3 :]
    time_copy = pltpu.make_async_copy(time_hbm, time_ref, sem.at[count])
    time_copy.start()
    copies = [pltpu.make_async_copy(sources[i], outs[i], sem.at[i]) for i in range(count)]
    for c in copies:
        c.start()
    rest = embedding_ref[...]
    modulated = None
    time_copy.wait()
    for _ in range(3):
        term = rest.astype(jnp.bfloat16)
        rest = rest - term.astype(jnp.float32)
        product = dot(term, time_ref[...])
        modulated = product if modulated is None else modulated + product
    mods_ref[...] = modulated
    for c in copies:
        c.wait()


def fetch(arrays, embedding, time_weight):
    in_hbm = [pltpu.with_memory_space_constraint(a, pltpu.HBM) for a in (*arrays, time_weight)]
    return pl.pallas_call(
        functools.partial(fetch_kernel, count=len(arrays)),
        out_shape=[jax.ShapeDtypeStruct(a.shape, a.dtype) for a in arrays]
        + [jax.ShapeDtypeStruct((embedding.shape[0], time_weight.shape[1]), jnp.float32)],
        in_specs=[HBM] * len(arrays) + [VMEM, HBM],
        out_specs=[VMEM] * (len(arrays) + 1),
        scratch_shapes=[
            pltpu.VMEM(time_weight.shape, time_weight.dtype),
            pltpu.SemaphoreType.DMA((len(arrays) + 1,)),
        ],
        compiler_params=pltpu.CompilerParams(vmem_limit_bytes=6 << 20),
        cost_estimate=pl.CostEstimate(
            flops=0, bytes_accessed=sum(a.size * 2 for a in arrays), transcendentals=0
        ),
        name="fetch",
    )(*in_hbm[:-1], embedding, in_hbm[-1])


def project_kernel(where, *refs, slots, counts):
    refs = list(refs)
    parts = [[refs.pop(0) for _ in range(n)] for n in counts]
    mods_ref, wk_ref, wv_ref, wq_ref, kv_ref, q_ref = refs
    depth, width = wk_ref.shape
    hidden = []
    for i, slot in enumerate(slots):
        rows_f = jnp.concatenate([part[...].astype(jnp.float32) for part in parts[i]])
        section = LAST if slot is None else where[0] ^ slot
        row = mods_ref[pl.ds(section, 1), :]
        hidden.append(modulate(rows_f, row[:, depth:], row[:, :depth]))
    hidden = jnp.concatenate(hidden)
    kv_ref[:, :width] = dot(hidden, wk_ref[...]).astype(jnp.bfloat16)
    kv_ref[:, width:] = dot(hidden, wv_ref[...]).astype(jnp.bfloat16)
    q_ref[...] = dot(hidden, wq_ref[...]).astype(jnp.bfloat16)


def project(where, slots, parts, mods, weights):
    args = [p for rows in parts for p in rows]
    depth, width = weights[0].shape
    rows = sum(p.shape[0] for p in args)
    return pl.pallas_call(
        functools.partial(project_kernel, slots=slots, counts=[len(p) for p in parts]),
        out_shape=(
            jax.ShapeDtypeStruct((rows, 2 * width), jnp.bfloat16),
            jax.ShapeDtypeStruct((rows, width), jnp.bfloat16),
        ),
        in_specs=[SMEM] + [VMEM] * (len(args) + 4),
        out_specs=(VMEM, VMEM),
        compiler_params=pltpu.CompilerParams(vmem_limit_bytes=12 << 20),
        cost_estimate=pl.CostEstimate(
            flops=6 * rows * depth * width, bytes_accessed=2 << 20, transcendentals=0
        ),
        name="project",
    )(where, *args, mods, *weights)


def state_shapes(rows, width):
    stat = jax.ShapeDtypeStruct((width // HEAD_DIM, rows, HEAD_DIM), jnp.float32)
    return stat, stat, jax.ShapeDtypeStruct((rows, width), jnp.float32)


def split(refs, *counts):
    refs = list(refs)
    return [[refs.pop(0) for _ in range(n)] for n in counts] + refs


def key_place(section, slot):
    source = section ^ slot
    swapped = jnp.where(section == LAST, 1 - source, source)
    return jnp.where(source > 1, source - 1, jnp.where(swapped == 1, 0, LAST))


def set_keys(kv_ref, section, slot, offset, block):
    base = key_place(section, slot) * (kv_ref.shape[0] // SECTIONS) + offset
    kv_ref[pl.ds(pl.multiple_of(base, 16), block.shape[0]), :] = block


def set_rows(x_ref, q_ref, section, slot, parts, queries):
    half = q_ref.shape[0] // SECTIONS
    base = pl.multiple_of((section ^ slot) * half, half)
    q_ref[pl.ds(base, half), :] = queries
    low = 0
    for part in parts:
        x_ref[pl.ds(pl.multiple_of(base + low, 8), part.shape[0]), :] = part[...].astype(jnp.float32)
        low += part.shape[0]


def place_kernel(where, *refs, groups, swapped):
    slots = [slot for group in groups for slot in group if slot is not None]
    kv_mine, kv_theirs, q_in, *refs = split(refs, len(groups), swapped, len(groups))
    *x_in, out = split(refs, *[2] * len(slots), 3)
    kv_ref, x_ref, q_ref = out
    half = q_ref.shape[0] // SECTIONS
    section = where[0]
    for g, group in enumerate(groups):
        for i, slot in enumerate(group):
            if slot is None:
                continue
            rows = slice(i * half, (i + 1) * half)
            set_rows(x_ref, q_ref, section, slot, x_in[slots.index(slot)], q_in[g][rows, :])
            set_keys(kv_ref, section, slot, 0, kv_mine[g][rows, :])
            if g < swapped:
                set_keys(kv_ref, section, slot, half, kv_theirs[g][rows, :])


def place(where, groups, kv_mine, kv_theirs, q, parts):
    local, depth = parts[0][0].shape
    half, width = 2 * local, q[0].shape[1]
    args = [*kv_mine, *kv_theirs, *q, *(p for rows in parts for p in rows)]
    return pl.pallas_call(
        functools.partial(place_kernel, groups=groups, swapped=len(kv_theirs)),
        out_shape=(
            jax.ShapeDtypeStruct((SECTIONS * 2 * half, 2 * width), jnp.bfloat16),
            jax.ShapeDtypeStruct((SECTIONS * half, depth), jnp.float32),
            jax.ShapeDtypeStruct((SECTIONS * half, width), jnp.bfloat16),
        ),
        in_specs=[SMEM] + [VMEM] * len(args),
        out_specs=(VMEM,) * 3,
        compiler_params=pltpu.CompilerParams(vmem_limit_bytes=4 << 20),
        cost_estimate=pl.CostEstimate(flops=0, bytes_accessed=4 << 20, transcendentals=0),
        name="place",
    )(where, *args)


def begin_kernel(where, theirs_ref, late_q_ref, own_ref, across_ref, kv_in, x_in, q_in,
                 kv_ref, x_ref, q_ref, top_ref, total_ref, sum_ref, *, groups):
    half = q_ref.shape[0] // SECTIONS
    span = 2 * half
    width = q_ref.shape[1]
    section = where[0]
    for i, slot in enumerate(groups[1]):
        set_keys(kv_ref, section, slot, half, theirs_ref[i * half : (i + 1) * half, :])
    set_rows(x_ref, q_ref, section, groups[2][0], (own_ref, across_ref), late_q_ref[...])
    jobs = []
    for s in range(1, SECTIONS):
        rows, seen = slice((s - 1) * half, s * half), slice(0, s * span)
        for head, (cols, v_cols) in enumerate(head_columns(width)):

            def emit(top, total, summed, head=head, rows=rows, cols=cols):
                top_ref[head, rows, :] = top
                total_ref[head, rows, :] = total
                sum_ref[rows, cols] = summed

            queries = view(q_ref, slice(s * half, (s + 1) * half), cols)
            jobs.append((queries, [(view(kv_ref, seen, cols), view(kv_ref, seen, v_cols))], None, emit))
    attend_all(jobs)


def begin_first(where, groups, placed, theirs, late_q, late_parts):
    half, width = placed[2].shape[0] // SECTIONS, late_q.shape[1]
    same = [jax.ShapeDtypeStruct(p.shape, p.dtype) for p in placed]
    return pl.pallas_call(
        functools.partial(begin_kernel, groups=groups),
        out_shape=(*same, *state_shapes(LAST * half, width)),
        in_specs=[SMEM] + [VMEM] * 7,
        out_specs=(VMEM,) * 6,
        input_output_aliases={5: 0, 6: 1, 7: 2},
        compiler_params=pltpu.CompilerParams(vmem_limit_bytes=12 << 20),
        cost_estimate=pl.CostEstimate(
            flops=24 * half * 2 * half * width, bytes_accessed=2 << 20, transcendentals=0
        ),
        name="begin_first",
    )(where, theirs, late_q, *late_parts, *placed)[1:]


def finish_kernel(where, steps, *refs, groups):
    known = len(groups)
    kv_mine, kv_theirs, refs_q = split(refs, known, known, 5)[:3]
    refs = list(refs)[2 * known + 5 :]
    x_ref, q_ref, top_ref, total_ref, sum_ref = refs_q
    mods_ref, wk_ref, wv_ref, wo_ref = refs[:4]
    stepped_hbm, velocity_hbm, kv2_ref, own2_ref, next_ref = refs[4:9]
    late_ref, o_ref, v_ref, st_ref, hid_ref, out_ref, sem = refs[9:]
    local, depth = next_ref.shape
    half = 2 * local
    width = wk_ref.shape[1]
    section = where[0]

    def set_late(slot):
        for g, group in enumerate(groups):
            if slot in group:
                rows = slice(group.index(slot) * half, (group.index(slot) + 1) * half)
                late_ref[0:half, :] = kv_mine[g][rows, :]
                late_ref[half:, :] = kv_theirs[g][rows, :]

    for s in range(LAST):
        pl.when(section == s)(functools.partial(set_late, s))
    pl.when(section == LAST)(functools.partial(set_late, LAST ^ 1))

    everything = slice(None)

    def late_jobs(queries, into, with_state):
        for head, (cols, v_cols) in enumerate(head_columns(width)):

            def emit(_, total, summed, cols=cols):
                o_ref[into, cols] = (summed / total).astype(jnp.bfloat16)

            def state(head=head, cols=cols):
                return top_ref[head, into], total_ref[head, into], sum_ref[into, cols]

            pairs = [(view(late_ref, everything, cols), view(late_ref, everything, v_cols))]
            yield view(q_ref, queries, cols), pairs, state if with_state else None, emit

    attend_all(list(late_jobs(slice(half, SECTIONS * half), slice(0, LAST * half), True)))
    v_ref[...] = dot(o_ref[...], wo_ref[...])
    for s in range(1, SECTIONS):
        rows = slice((s - 1) * half, s * half)
        stepped = (x_ref[s * half : (s + 1) * half, :] + steps[s] * v_ref[rows, :]).astype(jnp.bfloat16)
        st_ref[rows, :] = stepped
        hid_ref[rows, :] = modulate(
            stepped.astype(jnp.float32), mods_ref[s - 1 : s, depth:], mods_ref[s - 1 : s, :depth]
        )

    @pl.when(section == 0)
    def _():
        attend_all(list(late_jobs(slice(0, local), slice(0, local), False)))
        moving = dot(o_ref[0:local, :], wo_ref[...])
        out_ref[0] = (x_ref[0:local, :] + steps[0] * moving).astype(jnp.bfloat16)
        out_ref[1] = moving.astype(jnp.bfloat16)

    @pl.when(section > 0)
    def _():
        base = pl.multiple_of((section - 1) * half, half)
        out_ref[0] = st_ref[pl.ds(base, half), :][:local]
        out_ref[1] = v_ref[pl.ds(base, half), :][:local].astype(jnp.bfloat16)

    copies = [
        pltpu.make_async_copy(out_ref.at[0], stepped_hbm.at[0], sem.at[0]),
        pltpu.make_async_copy(out_ref.at[1], velocity_hbm.at[0], sem.at[1]),
    ]
    for c in copies:
        c.start()
    base = pl.multiple_of(jnp.minimum(section, LAST - 1) * half, half)
    own2_ref[...] = hid_ref[pl.ds(base, half), :][:local]
    next_ref[...] = st_ref[pl.ds(base, half), :][:local]
    kv2_ref[:, :width] = dot(hid_ref[...], wk_ref[...]).astype(jnp.bfloat16)
    kv2_ref[:, width:] = dot(hid_ref[...], wv_ref[...]).astype(jnp.bfloat16)
    for c in copies:
        c.wait()


def finish_first(where, steps, groups, kv_mine, kv_theirs, begun, mods, w_key, w_value, w_out):
    depth, width = w_key.shape
    half = begun[0].shape[0] // SECTIONS
    local = half // 2
    pair = jax.ShapeDtypeStruct((2, local, depth), jnp.bfloat16)
    one = jax.ShapeDtypeStruct((local, depth), jnp.bfloat16)
    args = [*kv_mine, *kv_theirs, *begun, mods, w_key, w_value, w_out]
    return pl.pallas_call(
        functools.partial(finish_kernel, groups=groups),
        out_shape=(pair, pair, jax.ShapeDtypeStruct((LAST * half, 2 * width), jnp.bfloat16), one, one),
        in_specs=[SMEM, SMEM] + [VMEM] * len(args),
        out_specs=(HBM, HBM, VMEM, VMEM, VMEM),
        scratch_shapes=[
            pltpu.VMEM((2 * half, 2 * width), jnp.bfloat16),
            pltpu.VMEM((LAST * half, width), jnp.bfloat16),
            pltpu.VMEM((LAST * half, depth), jnp.float32),
            pltpu.VMEM((LAST * half, depth), jnp.bfloat16),
            pltpu.VMEM((LAST * half, depth), jnp.bfloat16),
            pltpu.VMEM((2, local, depth), jnp.bfloat16),
            pltpu.SemaphoreType.DMA((2,)),
        ],
        compiler_params=pltpu.CompilerParams(vmem_limit_bytes=18 << 20),
        cost_estimate=pl.CostEstimate(
            flops=8 * LAST * half * depth * width, bytes_accessed=4 << 20, transcendentals=0
        ),
        name="finish_first",
    )(where, steps, *args)


def begin_second_kernel(
    where, own_ref, wq_ref, mine_ref, fresh_q_ref, fresh_mine_ref, fresh_theirs_ref,
    q_ref, top_ref, total_ref, sum_ref, *, fresh_row,
):
    local, width = q_ref.shape
    half = 2 * local
    section = where[0]

    def run(seen):
        jobs = []
        for head, (cols, v_cols) in enumerate(head_columns(width)):

            def emit(top, total, summed, head=head, cols=cols):
                top_ref[head], total_ref[head], sum_ref[:, cols] = top, total, summed

            pairs = [(view(r, rows, cols), view(r, rows, v_cols)) for r, rows in seen]
            jobs.append((view(q_ref, slice(None), cols), pairs, None, emit))
        attend_all(jobs)

    for s in range(LAST):

        @pl.when(section == s)
        def _():
            q_ref[...] = dot(own_ref[...], wq_ref[...]).astype(jnp.bfloat16)
            run([(mine_ref, slice(0, (s + 1) * half))])

    @pl.when(section == LAST)
    def _():
        fresh_rows = slice(fresh_row, fresh_row + half)
        q_ref[...] = fresh_q_ref[fresh_row : fresh_row + local, :]
        run([(mine_ref, slice(0, LAST * half)), (fresh_mine_ref, fresh_rows), (fresh_theirs_ref, fresh_rows)])


def begin_second(where, own2, w_query, mine2, fresh_q, fresh_mine, fresh_theirs, fresh_row):
    local, width = own2.shape[0], w_query.shape[1]
    return pl.pallas_call(
        functools.partial(begin_second_kernel, fresh_row=fresh_row),
        out_shape=(jax.ShapeDtypeStruct((local, width), jnp.bfloat16), *state_shapes(local, width)),
        in_specs=[SMEM] + [VMEM] * 6,
        out_specs=(VMEM,) * 4,
        compiler_params=pltpu.CompilerParams(vmem_limit_bytes=8 << 20),
        cost_estimate=pl.CostEstimate(
            flops=4 * local * own2.shape[1] * width, bytes_accessed=2 << 20, transcendentals=0
        ),
        name="begin_second",
    )(where, own2, w_query, mine2, fresh_q, fresh_mine, fresh_theirs)


def finish_second_kernel(
    where, steps, q_ref, top_ref, total_ref, sum_ref, theirs_ref, old_ref, fresh_ref, wo_ref, _s, _v,
    stepped_hbm, velocity_hbm, o_ref, x_ref, out_ref, sem,
):
    local, width = q_ref.shape
    section = where[0]

    def run(seen):
        jobs = []
        for head, (cols, v_cols) in enumerate(head_columns(width)):

            def emit(_, total, summed, cols=cols):
                o_ref[:, cols] = (summed / total).astype(jnp.bfloat16)

            def state(head=head, cols=cols):
                return top_ref[head], total_ref[head], sum_ref[:, cols]

            pairs = [(view(theirs_ref, slice(0, seen), cols), view(theirs_ref, slice(0, seen), v_cols))]
            jobs.append((view(q_ref, slice(None), cols), pairs, state, emit))
        attend_all(jobs)

    for s in range(LAST):
        reached = (section >= s) if s == LAST - 1 else (section == s)
        pl.when(reached)(functools.partial(run, (s + 1) * 2 * local))
    x_ref[...] = old_ref[...]

    @pl.when(section == LAST)
    def _():
        x_ref[...] = fresh_ref[...]

    moving = dot(o_ref[...], wo_ref[...])
    out_ref[0] = (x_ref[...].astype(jnp.float32) + steps[section] * moving).astype(jnp.bfloat16)
    out_ref[1] = moving.astype(jnp.bfloat16)
    copies = [
        pltpu.make_async_copy(out_ref.at[0], stepped_hbm.at[1], sem.at[0]),
        pltpu.make_async_copy(out_ref.at[1], velocity_hbm.at[1], sem.at[1]),
    ]
    for c in copies:
        c.start()
    for c in copies:
        c.wait()


def finish_second(where, steps, begun, theirs2, old, fresh, w_out, stepped, velocity):
    local, width = begun[0].shape
    pair = jax.ShapeDtypeStruct(stepped.shape, stepped.dtype)
    return pl.pallas_call(
        finish_second_kernel,
        out_shape=(pair, pair),
        in_specs=[SMEM, SMEM] + [VMEM] * 8 + [HBM, HBM],
        out_specs=(HBM, HBM),
        scratch_shapes=[
            pltpu.VMEM((local, width), jnp.bfloat16),
            pltpu.VMEM(old.shape, jnp.bfloat16),
            pltpu.VMEM((2, *old.shape), jnp.bfloat16),
            pltpu.SemaphoreType.DMA((2,)),
        ],
        input_output_aliases={10: 0, 11: 1},
        compiler_params=pltpu.CompilerParams(vmem_limit_bytes=8 << 20),
        cost_estimate=pl.CostEstimate(
            flops=4 * local * old.shape[1] * width, bytes_accessed=4 << 20, transcendentals=0
        ),
        name="finish_second",
    )(where, steps, *begun, theirs2, old, fresh, w_out, stepped, velocity)


def chip_body(latents, fresh_noise, levels, time_weight, w_query, w_key, w_value, w_out):
    per_section = lax.axis_size("tok") // SECTIONS
    where = (lax.axis_index("tok") // per_section).astype(jnp.int32).reshape(1)

    def needs(section, source):
        return source <= section + 1

    def from_section(block, slot):
        def move(i):
            section, within = i // per_section, i % per_section
            target = section ^ slot
            return target * per_section + within if needs(target, section) else None

        return permuted(block, "tok", move)

    def chip_swap(block, slot):
        def move(i):
            section = i // per_section
            if slot is None:
                return i ^ CORES if section == LAST else None
            return i ^ CORES if needs(section, section ^ slot) else None

        return permuted(block, "tok", move)

    def core_swap(block):
        return permuted(block, "tok", lambda i: i ^ 1)

    def after(value, *others):
        return lax.optimization_barrier((value, *others))[0]

    embedding, steps = lax.optimization_barrier(
        (level_embedding(levels, time_weight.shape[0] // 2), level_steps(levels))
    )
    w_key, w_value, w_query, w_out, mods = fetch(
        (w_key, w_value, w_query, w_out), embedding, time_weight
    )
    weights = (w_key, w_value, w_query)

    groups = ((0, None), (1, 3), (2,))
    own = {0: latents, None: fresh_noise}
    for slot in (3, 1, 2):
        own[slot] = from_section(latents, slot)
    parts = {slot: [own[slot], chip_swap(own[slot], slot)] for slot in (0, None, 3)}
    parts[1] = [own[1], from_section(parts[0][1], 1)]
    mine, theirs, q = {}, {}, {}

    def work(group):
        mine[group], q[group] = project(where, group, [parts[x] for x in group], mods, weights)
        theirs[group] = core_swap(mine[group])

    work(groups[0])
    own[2] = after(own[2], own[3], mine[groups[0]])
    parts[2] = [own[2], chip_swap(own[2], 2)]
    work(groups[1])
    early = groups[:-1]
    placed = place(
        where, early, [mine[g] for g in early], [theirs[groups[0]]], [q[g] for g in early],
        [parts[x] for g in early for x in g if x is not None],
    )
    parts[2][1] = after(parts[2][1], *placed)
    work(groups[2])
    all_mine, all_theirs = [mine[g] for g in groups], [theirs[g] for g in groups]
    begun = begin_first(
        where, groups, placed, theirs[groups[1]], q[groups[2]], parts[groups[2][0]]
    )
    stepped, velocity, mine2, own2, old = finish_first(
        where, steps, groups, all_mine, all_theirs, begun, mods, w_key, w_value, w_out
    )
    theirs2 = core_swap(mine2)
    first = groups[0]
    begun = begin_second(
        where, own2, w_query, mine2, q[first], mine[first], theirs[first],
        first.index(None) * 2 * latents.shape[0],
    )
    return finish_second(where, steps, begun, theirs2, old, fresh_noise, w_out, stepped, velocity)


def solution(mesh):
    per_section = mesh.shape["tok"] // SECTIONS
    on_chips = per_section == 2 * CORES
    rows = P(("groups", "tok"), None)
    return jax.shard_map(
        chip_body if on_chips else gathered_body,
        mesh=mesh,
        in_specs=(rows, rows, P(), P(), P(), P(), P(), P()),
        out_specs=(P(None, ("groups", "tok"), None), P(None, ("groups", "tok"), None)),
        check_vma=False,
    )
```

```python
import functools
import math

import jax
import jax.numpy as jnp
from jax import lax
from jax.experimental import pallas as pl
from jax.experimental.pallas import tpu as pltpu
from jax.sharding import PartitionSpec as P


HEAD_DIM = 128
SECTIONS = 4
CORES = 2

epsilon = 1e-06


def permuted(block, axis, move):
    devices = range(lax.axis_size(axis))
    route = [(i, move(i)) for i in devices if move(i) is not None and move(i) in devices]
    return lax.ppermute(block, axis, route)


def level_embedding(levels, half_width):
    frequency = jnp.exp(-math.log(10000.0) * jnp.arange(half_width, dtype=jnp.float32) / half_width)
    angles = levels.astype(jnp.float32)[:, None] * frequency[None, :]
    return jnp.concatenate([jnp.cos(angles), jnp.sin(angles)], axis=1)


def embed_levels(levels, time_weight):
    return jnp.dot(
        level_embedding(levels, time_weight.shape[0] // 2),
        time_weight.astype(jnp.float32),
        precision=lax.Precision.HIGHEST,
    )


def level_steps(levels):
    previous = jnp.concatenate([jnp.zeros((1,), jnp.int32), levels[:-1]])
    return (previous - levels).astype(jnp.float32) / 1000.0


def gathered_body(latents, fresh_noise, levels, time_weight, w_query, w_key, w_value, w_out):
    local_rows = latents.shape[0]
    heads = w_query.shape[1] // HEAD_DIM
    per_section = lax.axis_size("tok") // SECTIONS
    span_rows = local_rows * per_section
    my_block = lax.axis_index("tok") // per_section
    section_ids = jnp.arange(SECTIONS, dtype=jnp.int32)
    mods = embed_levels(levels, time_weight)
    width = mods.shape[1] // 2
    shift_all, scale_all = mods[:, :width], mods[:, width:]
    chosen = section_ids == my_block
    shift_vec = jnp.sum(jnp.where(chosen[:, None], shift_all, 0.0), axis=0)
    scale_vec = jnp.sum(jnp.where(chosen[:, None], scale_all, 0.0), axis=0)
    step_size = jnp.sum(jnp.where(chosen, level_steps(levels), 0.0))

    def denoise_local(rows):
        rows_f = rows.astype(jnp.float32)
        normed = rows_f * lax.rsqrt(jnp.mean(rows_f * rows_f, axis=-1, keepdims=True) + epsilon)
        hidden = (normed * (1.0 + scale_vec) + shift_vec).astype(jnp.bfloat16)

        def project(weight):
            return jnp.dot(hidden, weight, preferred_element_type=jnp.float32).astype(jnp.bfloat16)

        queries = project(w_query).reshape(local_rows, heads, HEAD_DIM)
        keys = lax.all_gather(project(w_key), "tok", axis=0, tiled=True)
        values = lax.all_gather(project(w_value), "tok", axis=0, tiled=True)
        count = keys.shape[0]
        allowed = (jnp.arange(count, dtype=jnp.int32) // span_rows <= my_block)[None, None, :]
        scores = jnp.einsum(
            "rhd,phd->hrp",
            queries,
            keys.reshape(count, heads, HEAD_DIM),
            preferred_element_type=jnp.float32,
        ) / math.sqrt(HEAD_DIM)
        scores = jnp.where(allowed, scores, -1e30)
        best = jnp.max(scores, axis=-1)
        weights = jnp.where(allowed, jnp.exp(scores - best[..., None]), 0.0)
        denominator = jnp.sum(weights, axis=-1)
        summed = jnp.einsum(
            "hrp,phd->hrd",
            weights.astype(jnp.bfloat16),
            values.reshape(count, heads, HEAD_DIM),
            preferred_element_type=jnp.float32,
        )
        attended = (summed / denominator[..., None]).astype(jnp.bfloat16)
        attended = attended.transpose(1, 0, 2).reshape(local_rows, heads * HEAD_DIM)
        moving = jnp.dot(attended, w_out, preferred_element_type=jnp.float32)
        stepped = (rows_f + step_size * moving).astype(jnp.bfloat16)
        return (stepped, moving.astype(jnp.bfloat16))

    first, first_moving = denoise_local(latents)
    incoming = permuted(first, "tok", lambda i: i - per_section)
    second_input = jnp.where(my_block == SECTIONS - 1, fresh_noise, incoming)
    second, second_moving = denoise_local(second_input)
    return (jnp.stack([first, second]), jnp.stack([first_moving, second_moving]))


VMEM = pl.BlockSpec(memory_space=pltpu.VMEM)
SMEM = pl.BlockSpec(memory_space=pltpu.SMEM)
HBM = pl.BlockSpec(memory_space=pltpu.HBM)
LAST = SECTIONS - 1


def modulate(rows_f, scale_row, shift_row):
    normed = rows_f * lax.rsqrt(jnp.mean(rows_f * rows_f, axis=-1, keepdims=True) + epsilon)
    return (normed * (1.0 + scale_row) + shift_row).astype(jnp.bfloat16)


def dot(a, b):
    return jnp.dot(a, b, preferred_element_type=jnp.float32)


SHARPNESS = math.log2(math.e) / math.sqrt(HEAD_DIM)


def score(queries, pairs):
    return [
        lax.dot_general(queries(), keys(), (((1,), (1,)), ((), ())), preferred_element_type=jnp.float32)
        for keys, _ in pairs
    ]


def weigh(scores, pairs, state=None):
    top = functools.reduce(jnp.maximum, [jnp.max(s, axis=-1, keepdims=True) for s in scores])
    rows = top.shape[0]
    top = jnp.broadcast_to(top, (rows, HEAD_DIM))
    if state is not None:
        old_top, old_total, old_summed = state()
        top = jnp.maximum(top, old_top)
    total, summed = 0.0, 0.0
    for part, (_, values) in zip(scores, pairs):
        rounded = []
        sums = []
        for low in range(0, part.shape[1], HEAD_DIM):
            piece = part[:, low : low + HEAD_DIM]
            weights = jnp.exp2((piece - top[:, : piece.shape[1]]) * SHARPNESS)
            sums.append(jnp.sum(weights, axis=-1, keepdims=True) if piece.shape[1] < HEAD_DIM else weights)
            rounded.append(weights.astype(jnp.bfloat16))
        full = [w for w in sums if w.shape[1] == HEAD_DIM]
        for w in [functools.reduce(jnp.add, full)] * (len(full) > 0) + [w for w in sums if w.shape[1] < HEAD_DIM]:
            total = total + jnp.sum(w, axis=-1, keepdims=True)
        summed = summed + dot(jnp.concatenate(rounded, axis=1), values())
    total = jnp.broadcast_to(total, (rows, HEAD_DIM))
    if state is not None:
        fade = jnp.exp2((old_top - top) * SHARPNESS)
        total, summed = old_total * fade + total, old_summed * fade + summed
    return top, total, summed


AHEAD = 3


def attend_all(jobs):
    pending = [score(*job[:2]) for job in jobs[:AHEAD]]
    for i, (_, pairs, state, emit) in enumerate(jobs):
        if i + AHEAD < len(jobs):
            pending.append(score(*jobs[i + AHEAD][:2]))
        emit(*weigh(pending.pop(0), pairs, state))


def view(ref, *where):
    return lambda: ref[where]


def head_columns(width):
    for head in range(width // HEAD_DIM):
        yield slice(head * HEAD_DIM, (head + 1) * HEAD_DIM), slice(
            width + head * HEAD_DIM, width + (head + 1) * HEAD_DIM
        )


def fetch_kernel(*refs, count):
    sources, embedding_ref, time_hbm = refs[:count], refs[count], refs[count + 1]
    outs, mods_ref = refs[count + 2 : 2 * count + 2], refs[2 * count + 2]
    time_ref, sem = refs[2 * count + 3 :]
    time_copy = pltpu.make_async_copy(time_hbm, time_ref, sem.at[count])
    time_copy.start()
    copies = [pltpu.make_async_copy(sources[i], outs[i], sem.at[i]) for i in range(count)]
    for c in copies:
        c.start()
    rest = embedding_ref[...]
    modulated = None
    time_copy.wait()
    for _ in range(3):
        term = rest.astype(jnp.bfloat16)
        rest = rest - term.astype(jnp.float32)
        product = dot(term, time_ref[...])
        modulated = product if modulated is None else modulated + product
    mods_ref[...] = modulated
    for c in copies:
        c.wait()


def fetch(arrays, embedding, time_weight):
    in_hbm = [pltpu.with_memory_space_constraint(a, pltpu.HBM) for a in (*arrays, time_weight)]
    return pl.pallas_call(
        functools.partial(fetch_kernel, count=len(arrays)),
        out_shape=[jax.ShapeDtypeStruct(a.shape, a.dtype) for a in arrays]
        + [jax.ShapeDtypeStruct((embedding.shape[0], time_weight.shape[1]), jnp.float32)],
        in_specs=[HBM] * len(arrays) + [VMEM, HBM],
        out_specs=[VMEM] * (len(arrays) + 1),
        scratch_shapes=[
            pltpu.VMEM(time_weight.shape, time_weight.dtype),
            pltpu.SemaphoreType.DMA((len(arrays) + 1,)),
        ],
        compiler_params=pltpu.CompilerParams(vmem_limit_bytes=6 << 20),
        cost_estimate=pl.CostEstimate(
            flops=0, bytes_accessed=sum(a.size * 2 for a in arrays), transcendentals=0
        ),
        name="fetch",
    )(*in_hbm[:-1], embedding, in_hbm[-1])


OWN, NEXT, EARLY, LATE = range(4)


def source_of(section, slot):
    if slot == EARLY:
        return jnp.where(section == LAST, 1, jnp.where(section == LAST - 1, 0, 2))
    if slot == LATE:
        return jnp.where(section == LAST, 0, jnp.where(section == LAST - 1, 1, LAST))
    return section ^ slot


def arrived(section, parts):
    for part in parts:
        if isinstance(part, tuple):
            direct, relayed = (ref[...].astype(jnp.float32) for ref in part)
            yield jnp.where(section == LAST, relayed, direct)
        else:
            yield part[...].astype(jnp.float32)


def flat(parts):
    return [x for part in parts for x in (part if isinstance(part, tuple) else (part,))]


def like(parts, refs):
    return [tuple(refs.pop(0) for _ in part) if isinstance(part, tuple) else refs.pop(0) for part in parts]


def project_kernel(where, *refs, slots, forms):
    refs = list(refs)
    parts = [like(form, refs) for form in forms]
    mods_ref, wk_ref, wv_ref, wq_ref, kv_ref, q_ref = refs
    depth, width = wk_ref.shape
    hidden = []
    for i, slot in enumerate(slots):
        rows_f = jnp.concatenate(list(arrived(where[0], parts[i])))
        section = LAST if slot is None else source_of(where[0], slot)
        row = mods_ref[pl.ds(section, 1), :]
        hidden.append(modulate(rows_f, row[:, depth:], row[:, :depth]))
    hidden = jnp.concatenate(hidden)
    kv_ref[:, :width] = dot(hidden, wk_ref[...]).astype(jnp.bfloat16)
    kv_ref[:, width:] = dot(hidden, wv_ref[...]).astype(jnp.bfloat16)
    q_ref[...] = dot(hidden, wq_ref[...]).astype(jnp.bfloat16)


def project(where, slots, parts, mods, weights):
    args = [p for rows in parts for p in flat(rows)]
    depth, width = weights[0].shape
    rows = 2 * args[0].shape[0] * len(slots)
    forms = [[tuple(None for _ in p) if isinstance(p, tuple) else None for p in rows] for rows in parts]
    return pl.pallas_call(
        functools.partial(project_kernel, slots=slots, forms=forms),
        out_shape=(
            jax.ShapeDtypeStruct((rows, 2 * width), jnp.bfloat16),
            jax.ShapeDtypeStruct((rows, width), jnp.bfloat16),
        ),
        in_specs=[SMEM] + [VMEM] * (len(args) + 4),
        out_specs=(VMEM, VMEM),
        compiler_params=pltpu.CompilerParams(vmem_limit_bytes=12 << 20),
        cost_estimate=pl.CostEstimate(
            flops=6 * rows * depth * width, bytes_accessed=2 << 20, transcendentals=0
        ),
        name="project",
    )(where, *args, mods, *weights)


def state_shapes(rows, width):
    stat = jax.ShapeDtypeStruct((width // HEAD_DIM, rows, HEAD_DIM), jnp.float32)
    return stat, stat, jax.ShapeDtypeStruct((rows, width), jnp.float32)


def split(refs, *counts):
    refs = list(refs)
    return [[refs.pop(0) for _ in range(n)] for n in counts] + refs


def key_place(section, slot):
    source = source_of(section, slot)
    swapped = jnp.where(section == LAST - 1, 1 - source, source)
    return jnp.where(source > 1, source - 1, jnp.where(swapped == 1, 0, LAST))


def set_keys(kv_ref, section, slot, offset, block):
    base = key_place(section, slot) * (kv_ref.shape[0] // SECTIONS) + offset
    kv_ref[pl.ds(pl.multiple_of(base, 16), block.shape[0]), :] = block


def set_rows(x_ref, q_ref, section, slot, parts, queries):
    half = q_ref.shape[0] // SECTIONS
    base = pl.multiple_of(source_of(section, slot) * half, half)
    q_ref[pl.ds(base, half), :] = queries
    low = 0
    for rows_f in arrived(section, parts):
        x_ref[pl.ds(pl.multiple_of(base + low, 8), rows_f.shape[0]), :] = rows_f
        low += rows_f.shape[0]


def place_kernel(where, *refs, groups, swapped):
    slots = [slot for group in groups for slot in group if slot is not None]
    kv_mine, kv_theirs, q_in, *refs = split(refs, len(groups), swapped, len(groups))
    *x_in, out = split(refs, *[2] * len(slots), 3)
    kv_ref, x_ref, q_ref = out
    half = q_ref.shape[0] // SECTIONS
    section = where[0]
    for g, group in enumerate(groups):
        for i, slot in enumerate(group):
            if slot is None:
                continue
            rows = slice(i * half, (i + 1) * half)
            set_rows(x_ref, q_ref, section, slot, x_in[slots.index(slot)], q_in[g][rows, :])
            set_keys(kv_ref, section, slot, 0, kv_mine[g][rows, :])
            if g < swapped:
                set_keys(kv_ref, section, slot, half, kv_theirs[g][rows, :])


def place(where, groups, kv_mine, kv_theirs, q, parts):
    local, depth = parts[0][0].shape
    half, width = 2 * local, q[0].shape[1]
    args = [*kv_mine, *kv_theirs, *q, *(p for rows in parts for p in rows)]
    return pl.pallas_call(
        functools.partial(place_kernel, groups=groups, swapped=len(kv_theirs)),
        out_shape=(
            jax.ShapeDtypeStruct((SECTIONS * 2 * half, 2 * width), jnp.bfloat16),
            jax.ShapeDtypeStruct((SECTIONS * half, depth), jnp.float32),
            jax.ShapeDtypeStruct((SECTIONS * half, width), jnp.bfloat16),
        ),
        in_specs=[SMEM] + [VMEM] * len(args),
        out_specs=(VMEM,) * 3,
        compiler_params=pltpu.CompilerParams(vmem_limit_bytes=4 << 20),
        cost_estimate=pl.CostEstimate(flops=0, bytes_accessed=4 << 20, transcendentals=0),
        name="place",
    )(where, *args)


def begin_kernel(where, theirs_ref, late_q_ref, direct_ref, relayed_ref, direct2_ref, relayed2_ref, kv_in, x_in, q_in,
                 kv_ref, x_ref, q_ref, top_ref, total_ref, sum_ref, *, groups):
    half = q_ref.shape[0] // SECTIONS
    span = 2 * half
    width = q_ref.shape[1]
    section = where[0]
    for i, slot in enumerate(groups[1]):
        set_keys(kv_ref, section, slot, half, theirs_ref[i * half : (i + 1) * half, :])
    set_rows(x_ref, q_ref, section, LATE, [(direct_ref, relayed_ref), (direct2_ref, relayed2_ref)], late_q_ref[...])
    jobs = []
    for s in range(1, SECTIONS):
        rows, seen = slice((s - 1) * half, s * half), slice(0, s * span)
        for head, (cols, v_cols) in enumerate(head_columns(width)):

            def emit(top, total, summed, head=head, rows=rows, cols=cols):
                top_ref[head, rows, :] = top
                total_ref[head, rows, :] = total
                sum_ref[rows, cols] = summed

            queries = view(q_ref, slice(s * half, (s + 1) * half), cols)
            jobs.append((queries, [(view(kv_ref, seen, cols), view(kv_ref, seen, v_cols))], None, emit))
    attend_all(jobs)


def begin_first(where, groups, placed, theirs, late_q, late_parts):
    half, width = placed[2].shape[0] // SECTIONS, late_q.shape[1]
    same = [jax.ShapeDtypeStruct(p.shape, p.dtype) for p in placed]
    return pl.pallas_call(
        functools.partial(begin_kernel, groups=groups),
        out_shape=(*same, *state_shapes(LAST * half, width)),
        in_specs=[SMEM] + [VMEM] * 9,
        out_specs=(VMEM,) * 6,
        input_output_aliases={7: 0, 8: 1, 9: 2},
        compiler_params=pltpu.CompilerParams(vmem_limit_bytes=12 << 20),
        cost_estimate=pl.CostEstimate(
            flops=24 * half * 2 * half * width, bytes_accessed=2 << 20, transcendentals=0
        ),
        name="begin_first",
    )(where, theirs, late_q, *flat(late_parts), *placed)[1:]


def finish_kernel(where, steps, *refs, groups):
    known = len(groups)
    kv_mine, kv_theirs, refs_q = split(refs, known, known, 5)[:3]
    refs = list(refs)[2 * known + 5 :]
    x_ref, q_ref, top_ref, total_ref, sum_ref = refs_q
    mods_ref, wk_ref, wv_ref, wo_ref = refs[:4]
    stepped_hbm, velocity_hbm, kv2_ref, own2_ref, next_ref = refs[4:9]
    late_ref, o_ref, v_ref, st_ref, hid_ref, out_ref, sem = refs[9:]
    local, depth = next_ref.shape
    half = 2 * local
    width = wk_ref.shape[1]
    section = where[0]

    def set_late(slot):
        for g, group in enumerate(groups):
            if slot in group:
                rows = slice(group.index(slot) * half, (group.index(slot) + 1) * half)
                late_ref[0:half, :] = kv_mine[g][rows, :]
                late_ref[half:, :] = kv_theirs[g][rows, :]

    for s in range(LAST - 1):
        pl.when(section == s)(functools.partial(set_late, s))
    pl.when(section >= LAST - 1)(functools.partial(set_late, LATE))

    everything = slice(None)

    def late_jobs(queries, into, with_state):
        for head, (cols, v_cols) in enumerate(head_columns(width)):

            def emit(_, total, summed, cols=cols):
                o_ref[into, cols] = (summed / total).astype(jnp.bfloat16)

            def state(head=head, cols=cols):
                return top_ref[head, into], total_ref[head, into], sum_ref[into, cols]

            pairs = [(view(late_ref, everything, cols), view(late_ref, everything, v_cols))]
            yield view(q_ref, queries, cols), pairs, state if with_state else None, emit

    attend_all(list(late_jobs(slice(half, SECTIONS * half), slice(0, LAST * half), True)))
    v_ref[...] = dot(o_ref[...], wo_ref[...])
    for s in range(1, SECTIONS):
        rows = slice((s - 1) * half, s * half)
        stepped = (x_ref[s * half : (s + 1) * half, :] + steps[s] * v_ref[rows, :]).astype(jnp.bfloat16)
        st_ref[rows, :] = stepped
        hid_ref[rows, :] = modulate(
            stepped.astype(jnp.float32), mods_ref[s - 1 : s, depth:], mods_ref[s - 1 : s, :depth]
        )

    @pl.when(section == 0)
    def _():
        attend_all(list(late_jobs(slice(0, local), slice(0, local), False)))
        moving = dot(o_ref[0:local, :], wo_ref[...])
        out_ref[0] = (x_ref[0:local, :] + steps[0] * moving).astype(jnp.bfloat16)
        out_ref[1] = moving.astype(jnp.bfloat16)

    @pl.when(section > 0)
    def _():
        base = pl.multiple_of((section - 1) * half, half)
        out_ref[0] = st_ref[pl.ds(base, half), :][:local]
        out_ref[1] = v_ref[pl.ds(base, half), :][:local].astype(jnp.bfloat16)

    copies = [
        pltpu.make_async_copy(out_ref.at[0], stepped_hbm.at[0], sem.at[0]),
        pltpu.make_async_copy(out_ref.at[1], velocity_hbm.at[0], sem.at[1]),
    ]
    for c in copies:
        c.start()
    base = pl.multiple_of(jnp.minimum(section, LAST - 1) * half, half)
    own2_ref[...] = hid_ref[pl.ds(base, half), :][:local]
    next_ref[...] = st_ref[pl.ds(base, half), :][:local]
    kv2_ref[:, :width] = dot(hid_ref[...], wk_ref[...]).astype(jnp.bfloat16)
    kv2_ref[:, width:] = dot(hid_ref[...], wv_ref[...]).astype(jnp.bfloat16)
    for c in copies:
        c.wait()


def finish_first(where, steps, groups, kv_mine, kv_theirs, begun, mods, w_key, w_value, w_out):
    depth, width = w_key.shape
    half = begun[0].shape[0] // SECTIONS
    local = half // 2
    pair = jax.ShapeDtypeStruct((2, local, depth), jnp.bfloat16)
    one = jax.ShapeDtypeStruct((local, depth), jnp.bfloat16)
    args = [*kv_mine, *kv_theirs, *begun, mods, w_key, w_value, w_out]
    return pl.pallas_call(
        functools.partial(finish_kernel, groups=groups),
        out_shape=(pair, pair, jax.ShapeDtypeStruct((LAST * half, 2 * width), jnp.bfloat16), one, one),
        in_specs=[SMEM, SMEM] + [VMEM] * len(args),
        out_specs=(HBM, HBM, VMEM, VMEM, VMEM),
        scratch_shapes=[
            pltpu.VMEM((2 * half, 2 * width), jnp.bfloat16),
            pltpu.VMEM((LAST * half, width), jnp.bfloat16),
            pltpu.VMEM((LAST * half, depth), jnp.float32),
            pltpu.VMEM((LAST * half, depth), jnp.bfloat16),
            pltpu.VMEM((LAST * half, depth), jnp.bfloat16),
            pltpu.VMEM((2, local, depth), jnp.bfloat16),
            pltpu.SemaphoreType.DMA((2,)),
        ],
        compiler_params=pltpu.CompilerParams(vmem_limit_bytes=18 << 20),
        cost_estimate=pl.CostEstimate(
            flops=8 * LAST * half * depth * width, bytes_accessed=4 << 20, transcendentals=0
        ),
        name="finish_first",
    )(where, steps, *args)


def begin_second_kernel(
    where, own_ref, wq_ref, mine_ref, fresh_q_ref, fresh_mine_ref, fresh_theirs_ref,
    q_ref, top_ref, total_ref, sum_ref, *, fresh_row,
):
    local, width = q_ref.shape
    half = 2 * local
    section = where[0]

    def run(seen):
        jobs = []
        for head, (cols, v_cols) in enumerate(head_columns(width)):

            def emit(top, total, summed, head=head, cols=cols):
                top_ref[head], total_ref[head], sum_ref[:, cols] = top, total, summed

            pairs = [(view(r, rows, cols), view(r, rows, v_cols)) for r, rows in seen]
            jobs.append((view(q_ref, slice(None), cols), pairs, None, emit))
        attend_all(jobs)

    for s in range(LAST):

        @pl.when(section == s)
        def _():
            q_ref[...] = dot(own_ref[...], wq_ref[...]).astype(jnp.bfloat16)
            run([(mine_ref, slice(0, (s + 1) * half))])

    @pl.when(section == LAST)
    def _():
        fresh_rows = slice(fresh_row, fresh_row + half)
        q_ref[...] = fresh_q_ref[fresh_row : fresh_row + local, :]
        run([(mine_ref, slice(0, LAST * half)), (fresh_mine_ref, fresh_rows), (fresh_theirs_ref, fresh_rows)])


def begin_second(where, own2, w_query, mine2, fresh_q, fresh_mine, fresh_theirs, fresh_row):
    local, width = own2.shape[0], w_query.shape[1]
    return pl.pallas_call(
        functools.partial(begin_second_kernel, fresh_row=fresh_row),
        out_shape=(jax.ShapeDtypeStruct((local, width), jnp.bfloat16), *state_shapes(local, width)),
        in_specs=[SMEM] + [VMEM] * 6,
        out_specs=(VMEM,) * 4,
        compiler_params=pltpu.CompilerParams(vmem_limit_bytes=8 << 20),
        cost_estimate=pl.CostEstimate(
            flops=4 * local * own2.shape[1] * width, bytes_accessed=2 << 20, transcendentals=0
        ),
        name="begin_second",
    )(where, own2, w_query, mine2, fresh_q, fresh_mine, fresh_theirs)


def finish_second_kernel(
    where, steps, q_ref, top_ref, total_ref, sum_ref, theirs_ref, old_ref, fresh_ref, wo_ref, _s, _v,
    stepped_hbm, velocity_hbm, o_ref, x_ref, out_ref, sem,
):
    local, width = q_ref.shape
    section = where[0]

    def run(seen):
        jobs = []
        for head, (cols, v_cols) in enumerate(head_columns(width)):

            def emit(_, total, summed, cols=cols):
                o_ref[:, cols] = (summed / total).astype(jnp.bfloat16)

            def state(head=head, cols=cols):
                return top_ref[head], total_ref[head], sum_ref[:, cols]

            pairs = [(view(theirs_ref, slice(0, seen), cols), view(theirs_ref, slice(0, seen), v_cols))]
            jobs.append((view(q_ref, slice(None), cols), pairs, state, emit))
        attend_all(jobs)

    for s in range(LAST):
        reached = (section >= s) if s == LAST - 1 else (section == s)
        pl.when(reached)(functools.partial(run, (s + 1) * 2 * local))
    x_ref[...] = old_ref[...]

    @pl.when(section == LAST)
    def _():
        x_ref[...] = fresh_ref[...]

    moving = dot(o_ref[...], wo_ref[...])
    out_ref[0] = (x_ref[...].astype(jnp.float32) + steps[section] * moving).astype(jnp.bfloat16)
    out_ref[1] = moving.astype(jnp.bfloat16)
    copies = [
        pltpu.make_async_copy(out_ref.at[0], stepped_hbm.at[1], sem.at[0]),
        pltpu.make_async_copy(out_ref.at[1], velocity_hbm.at[1], sem.at[1]),
    ]
    for c in copies:
        c.start()
    for c in copies:
        c.wait()


def finish_second(where, steps, begun, theirs2, old, fresh, w_out, stepped, velocity):
    local, width = begun[0].shape
    pair = jax.ShapeDtypeStruct(stepped.shape, stepped.dtype)
    return pl.pallas_call(
        finish_second_kernel,
        out_shape=(pair, pair),
        in_specs=[SMEM, SMEM] + [VMEM] * 8 + [HBM, HBM],
        out_specs=(HBM, HBM),
        scratch_shapes=[
            pltpu.VMEM((local, width), jnp.bfloat16),
            pltpu.VMEM(old.shape, jnp.bfloat16),
            pltpu.VMEM((2, *old.shape), jnp.bfloat16),
            pltpu.SemaphoreType.DMA((2,)),
        ],
        input_output_aliases={10: 0, 11: 1},
        compiler_params=pltpu.CompilerParams(vmem_limit_bytes=8 << 20),
        cost_estimate=pl.CostEstimate(
            flops=4 * local * old.shape[1] * width, bytes_accessed=4 << 20, transcendentals=0
        ),
        name="finish_second",
    )(where, steps, *begun, theirs2, old, fresh, w_out, stepped, velocity)


def chip_body(latents, fresh_noise, levels, time_weight, w_query, w_key, w_value, w_out):
    per_section = lax.axis_size("tok") // SECTIONS
    where = (lax.axis_index("tok") // per_section).astype(jnp.int32).reshape(1)

    def between(block, pairs):
        target = dict(pairs)

        def move(i):
            section, within = i // per_section, i % per_section
            return target[section] * per_section + within if section in target else None

        return permuted(block, "tok", move)

    def chip_swap(block, sections):
        return permuted(block, "tok", lambda i: i ^ CORES if i // per_section in sections else None)

    def core_swap(block):
        return permuted(block, "tok", lambda i: i ^ 1)

    def after(value, *others):
        return lax.optimization_barrier((value, *others))[0]

    embedding, steps = lax.optimization_barrier(
        (level_embedding(levels, time_weight.shape[0] // 2), level_steps(levels))
    )
    w_key, w_value, w_query, w_out, mods = fetch(
        (w_key, w_value, w_query, w_out), embedding, time_weight
    )
    weights = (w_key, w_value, w_query)

    groups = ((OWN, None), (NEXT, EARLY), (LATE,))
    neighbours = [(s, s ^ 1) for s in range(SECTIONS)]
    early_in = between(latents, [(0, 2), (1, 3), (2, 1)])
    own_across = chip_swap(latents, range(SECTIONS))
    next_in = between(latents, neighbours)
    direct = between(latents, [(LAST - 2, LAST - 1)])
    fresh_across = chip_swap(fresh_noise, (LAST,))
    next_across = between(own_across, neighbours)
    relayed = between(early_in, [(LAST - 1, LAST)])
    parts = {
        OWN: [latents, own_across],
        None: [fresh_noise, fresh_across],
        NEXT: [next_in, next_across],
        EARLY: [early_in, chip_swap(early_in, range(1, SECTIONS))],
    }
    mine, theirs, q = {}, {}, {}

    def work(group):
        mine[group], q[group] = project(where, group, [parts[x] for x in group], mods, weights)
        theirs[group] = core_swap(mine[group])

    work(groups[0])
    direct = after(direct, early_in, mine[groups[0]])
    relayed = after(relayed, direct)
    direct_across = chip_swap(direct, (LAST - 1,))
    relayed_across = chip_swap(relayed, (LAST,))
    work(groups[1])
    early = groups[:-1]
    placed = place(
        where, early, [mine[g] for g in early], [theirs[groups[0]]], [q[g] for g in early],
        [parts[x] for g in early for x in g if x is not None],
    )
    relayed_across = after(relayed_across, *placed)
    parts[LATE] = [(direct, relayed), (direct_across, relayed_across)]
    work(groups[2])
    all_mine, all_theirs = [mine[g] for g in groups], [theirs[g] for g in groups]
    begun = begin_first(
        where, groups, placed, theirs[groups[1]], q[groups[2]], parts[groups[2][0]]
    )
    stepped, velocity, mine2, own2, old = finish_first(
        where, steps, groups, all_mine, all_theirs, begun, mods, w_key, w_value, w_out
    )
    theirs2 = core_swap(mine2)
    first = groups[0]
    begun = begin_second(
        where, own2, w_query, mine2, q[first], mine[first], theirs[first],
        first.index(None) * 2 * latents.shape[0],
    )
    return finish_second(where, steps, begun, theirs2, old, fresh_noise, w_out, stepped, velocity)


def solution(mesh):
    per_section = mesh.shape["tok"] // SECTIONS
    on_chips = per_section == 2 * CORES
    rows = P(("groups", "tok"), None)
    return jax.shard_map(
        chip_body if on_chips else gathered_body,
        mesh=mesh,
        in_specs=(rows, rows, P(), P(), P(), P(), P(), P()),
        out_specs=(P(None, ("groups", "tok"), None), P(None, ("groups", "tok"), None)),
        check_vma=False,
    )
```

```python
import functools
import math

import jax
import jax.numpy as jnp
from jax import lax
from jax.experimental import pallas as pl
from jax.experimental.pallas import tpu as pltpu
from jax.sharding import PartitionSpec as P


HEAD_DIM = 128
SECTIONS = 4
CORES = 2

epsilon = 1e-06


def permuted(block, axis, move):
    devices = range(lax.axis_size(axis))
    route = [(i, move(i)) for i in devices if move(i) is not None and move(i) in devices]
    return lax.ppermute(block, axis, route)


def level_embedding(levels, half_width):
    frequency = jnp.exp(-math.log(10000.0) * jnp.arange(half_width, dtype=jnp.float32) / half_width)
    angles = levels.astype(jnp.float32)[:, None] * frequency[None, :]
    return jnp.concatenate([jnp.cos(angles), jnp.sin(angles)], axis=1)


def embed_levels(levels, time_weight):
    return jnp.dot(
        level_embedding(levels, time_weight.shape[0] // 2),
        time_weight.astype(jnp.float32),
        precision=lax.Precision.HIGHEST,
    )


def level_steps(levels):
    previous = jnp.concatenate([jnp.zeros((1,), jnp.int32), levels[:-1]])
    return (previous - levels).astype(jnp.float32) / 1000.0


def gathered_body(latents, fresh_noise, levels, time_weight, w_query, w_key, w_value, w_out):
    local_rows = latents.shape[0]
    heads = w_query.shape[1] // HEAD_DIM
    per_section = lax.axis_size("tok") // SECTIONS
    span_rows = local_rows * per_section
    my_block = lax.axis_index("tok") // per_section
    section_ids = jnp.arange(SECTIONS, dtype=jnp.int32)
    mods = embed_levels(levels, time_weight)
    width = mods.shape[1] // 2
    shift_all, scale_all = mods[:, :width], mods[:, width:]
    chosen = section_ids == my_block
    shift_vec = jnp.sum(jnp.where(chosen[:, None], shift_all, 0.0), axis=0)
    scale_vec = jnp.sum(jnp.where(chosen[:, None], scale_all, 0.0), axis=0)
    step_size = jnp.sum(jnp.where(chosen, level_steps(levels), 0.0))

    def denoise_local(rows):
        rows_f = rows.astype(jnp.float32)
        normed = rows_f * lax.rsqrt(jnp.mean(rows_f * rows_f, axis=-1, keepdims=True) + epsilon)
        hidden = (normed * (1.0 + scale_vec) + shift_vec).astype(jnp.bfloat16)

        def project(weight):
            return jnp.dot(hidden, weight, preferred_element_type=jnp.float32).astype(jnp.bfloat16)

        queries = project(w_query).reshape(local_rows, heads, HEAD_DIM)
        keys = lax.all_gather(project(w_key), "tok", axis=0, tiled=True)
        values = lax.all_gather(project(w_value), "tok", axis=0, tiled=True)
        count = keys.shape[0]
        allowed = (jnp.arange(count, dtype=jnp.int32) // span_rows <= my_block)[None, None, :]
        scores = jnp.einsum(
            "rhd,phd->hrp",
            queries,
            keys.reshape(count, heads, HEAD_DIM),
            preferred_element_type=jnp.float32,
        ) / math.sqrt(HEAD_DIM)
        scores = jnp.where(allowed, scores, -1e30)
        best = jnp.max(scores, axis=-1)
        weights = jnp.where(allowed, jnp.exp(scores - best[..., None]), 0.0)
        denominator = jnp.sum(weights, axis=-1)
        summed = jnp.einsum(
            "hrp,phd->hrd",
            weights.astype(jnp.bfloat16),
            values.reshape(count, heads, HEAD_DIM),
            preferred_element_type=jnp.float32,
        )
        attended = (summed / denominator[..., None]).astype(jnp.bfloat16)
        attended = attended.transpose(1, 0, 2).reshape(local_rows, heads * HEAD_DIM)
        moving = jnp.dot(attended, w_out, preferred_element_type=jnp.float32)
        stepped = (rows_f + step_size * moving).astype(jnp.bfloat16)
        return (stepped, moving.astype(jnp.bfloat16))

    first, first_moving = denoise_local(latents)
    incoming = permuted(first, "tok", lambda i: i - per_section)
    second_input = jnp.where(my_block == SECTIONS - 1, fresh_noise, incoming)
    second, second_moving = denoise_local(second_input)
    return (jnp.stack([first, second]), jnp.stack([first_moving, second_moving]))


VMEM = pl.BlockSpec(memory_space=pltpu.VMEM)
SMEM = pl.BlockSpec(memory_space=pltpu.SMEM)
HBM = pl.BlockSpec(memory_space=pltpu.HBM)
LAST = SECTIONS - 1


def modulate(rows_f, scale_row, shift_row):
    normed = rows_f * lax.rsqrt(jnp.mean(rows_f * rows_f, axis=-1, keepdims=True) + epsilon)
    return (normed * (1.0 + scale_row) + shift_row).astype(jnp.bfloat16)


def dot(a, b):
    return jnp.dot(a, b, preferred_element_type=jnp.float32)


SHARPNESS = math.log2(math.e) / math.sqrt(HEAD_DIM)


def score(queries, pairs):
    return [
        lax.dot_general(queries(), keys(), (((1,), (1,)), ((), ())), preferred_element_type=jnp.float32)
        for keys, _ in pairs
    ]


def weigh(scores, pairs, state=None):
    top = functools.reduce(jnp.maximum, [jnp.max(s, axis=-1, keepdims=True) for s in scores])
    rows = top.shape[0]
    top = jnp.broadcast_to(top, (rows, HEAD_DIM))
    if state is not None:
        old_top, old_total, old_summed = state()
        top = jnp.maximum(top, old_top)
    total, summed = 0.0, 0.0
    for part, (_, values) in zip(scores, pairs):
        rounded = []
        sums = []
        for low in range(0, part.shape[1], HEAD_DIM):
            piece = part[:, low : low + HEAD_DIM]
            weights = jnp.exp2((piece - top[:, : piece.shape[1]]) * SHARPNESS)
            sums.append(jnp.sum(weights, axis=-1, keepdims=True) if piece.shape[1] < HEAD_DIM else weights)
            rounded.append(weights.astype(jnp.bfloat16))
        full = [w for w in sums if w.shape[1] == HEAD_DIM]
        for w in [functools.reduce(jnp.add, full)] * (len(full) > 0) + [w for w in sums if w.shape[1] < HEAD_DIM]:
            total = total + jnp.sum(w, axis=-1, keepdims=True)
        summed = summed + dot(jnp.concatenate(rounded, axis=1), values())
    total = jnp.broadcast_to(total, (rows, HEAD_DIM))
    if state is not None:
        fade = jnp.exp2((old_top - top) * SHARPNESS)
        total, summed = old_total * fade + total, old_summed * fade + summed
    return top, total, summed


AHEAD = 3


def attend_all(jobs):
    pending = [score(*job[:2]) for job in jobs[:AHEAD]]
    for i, (_, pairs, state, emit) in enumerate(jobs):
        if i + AHEAD < len(jobs):
            pending.append(score(*jobs[i + AHEAD][:2]))
        emit(*weigh(pending.pop(0), pairs, state))


def view(ref, *where):
    return lambda: ref[where]


def head_columns(width):
    for head in range(width // HEAD_DIM):
        yield slice(head * HEAD_DIM, (head + 1) * HEAD_DIM), slice(
            width + head * HEAD_DIM, width + (head + 1) * HEAD_DIM
        )


def fetch_kernel(*refs, count):
    sources, embedding_ref, time_hbm = refs[:count], refs[count], refs[count + 1]
    outs, mods_ref = refs[count + 2 : 2 * count + 2], refs[2 * count + 2]
    time_ref, sem = refs[2 * count + 3 :]
    time_copy = pltpu.make_async_copy(time_hbm, time_ref, sem.at[count])
    time_copy.start()
    copies = [pltpu.make_async_copy(sources[i], outs[i], sem.at[i]) for i in range(count)]
    for c in copies:
        c.start()
    rest = embedding_ref[...]
    modulated = None
    time_copy.wait()
    for _ in range(3):
        term = rest.astype(jnp.bfloat16)
        rest = rest - term.astype(jnp.float32)
        product = dot(term, time_ref[...])
        modulated = product if modulated is None else modulated + product
    mods_ref[...] = modulated
    for c in copies:
        c.wait()


def fetch(arrays, embedding, time_weight):
    in_hbm = [pltpu.with_memory_space_constraint(a, pltpu.HBM) for a in (*arrays, time_weight)]
    return pl.pallas_call(
        functools.partial(fetch_kernel, count=len(arrays)),
        out_shape=[jax.ShapeDtypeStruct(a.shape, a.dtype) for a in arrays]
        + [jax.ShapeDtypeStruct((embedding.shape[0], time_weight.shape[1]), jnp.float32)],
        in_specs=[HBM] * len(arrays) + [VMEM, HBM],
        out_specs=[VMEM] * (len(arrays) + 1),
        scratch_shapes=[
            pltpu.VMEM(time_weight.shape, time_weight.dtype),
            pltpu.SemaphoreType.DMA((len(arrays) + 1,)),
        ],
        compiler_params=pltpu.CompilerParams(vmem_limit_bytes=6 << 20),
        cost_estimate=pl.CostEstimate(
            flops=0, bytes_accessed=sum(a.size * 2 for a in arrays), transcendentals=0
        ),
        name="fetch",
    )(*in_hbm[:-1], embedding, in_hbm[-1])


def project_kernel(where, *refs, slots, counts):
    refs = list(refs)
    parts = [[refs.pop(0) for _ in range(n)] for n in counts]
    mods_ref, wk_ref, wv_ref, wq_ref, kv_ref, q_ref = refs
    depth, width = wk_ref.shape
    hidden = []
    for i, slot in enumerate(slots):
        rows_f = jnp.concatenate([part[...].astype(jnp.float32) for part in parts[i]])
        section = LAST if slot is None else where[0] ^ slot
        row = mods_ref[pl.ds(section, 1), :]
        hidden.append(modulate(rows_f, row[:, depth:], row[:, :depth]))
    hidden = jnp.concatenate(hidden)
    kv_ref[:, :width] = dot(hidden, wk_ref[...]).astype(jnp.bfloat16)
    kv_ref[:, width:] = dot(hidden, wv_ref[...]).astype(jnp.bfloat16)
    q_ref[...] = dot(hidden, wq_ref[...]).astype(jnp.bfloat16)


def project(where, slots, parts, mods, weights):
    args = [p for rows in parts for p in rows]
    depth, width = weights[0].shape
    rows = sum(p.shape[0] for p in args)
    return pl.pallas_call(
        functools.partial(project_kernel, slots=slots, counts=[len(p) for p in parts]),
        out_shape=(
            jax.ShapeDtypeStruct((rows, 2 * width), jnp.bfloat16),
            jax.ShapeDtypeStruct((rows, width), jnp.bfloat16),
        ),
        in_specs=[SMEM] + [VMEM] * (len(args) + 4),
        out_specs=(VMEM, VMEM),
        compiler_params=pltpu.CompilerParams(vmem_limit_bytes=12 << 20),
        cost_estimate=pl.CostEstimate(
            flops=6 * rows * depth * width, bytes_accessed=2 << 20, transcendentals=0
        ),
        name="project",
    )(where, *args, mods, *weights)


def state_shapes(rows, width):
    stat = jax.ShapeDtypeStruct((width // HEAD_DIM, rows, HEAD_DIM), jnp.float32)
    return stat, stat, jax.ShapeDtypeStruct((rows, width), jnp.float32)


def split(refs, *counts):
    refs = list(refs)
    return [[refs.pop(0) for _ in range(n)] for n in counts] + refs


def key_place(section, slot):
    source = section ^ slot
    swapped = jnp.where(section == LAST, 1 - source, source)
    return jnp.where(source > 1, source - 1, jnp.where(swapped == 1, 0, LAST))


def set_keys(kv_ref, section, slot, offset, block):
    base = key_place(section, slot) * (kv_ref.shape[0] // SECTIONS) + offset
    kv_ref[pl.ds(pl.multiple_of(base, 16), block.shape[0]), :] = block


def set_rows(x_ref, q_ref, section, slot, parts, queries):
    half = q_ref.shape[0] // SECTIONS
    base = pl.multiple_of((section ^ slot) * half, half)
    q_ref[pl.ds(base, half), :] = queries
    low = 0
    for part in parts:
        x_ref[pl.ds(pl.multiple_of(base + low, 8), part.shape[0]), :] = part[...].astype(jnp.float32)
        low += part.shape[0]


def place_kernel(where, *refs, groups, swapped):
    slots = [slot for group in groups for slot in group if slot is not None]
    kv_mine, kv_theirs, q_in, *refs = split(refs, len(groups), swapped, len(groups))
    *x_in, out = split(refs, *[2] * len(slots), 3)
    kv_ref, x_ref, q_ref = out
    half = q_ref.shape[0] // SECTIONS
    section = where[0]
    for g, group in enumerate(groups):
        for i, slot in enumerate(group):
            if slot is None:
                continue
            rows = slice(i * half, (i + 1) * half)
            set_rows(x_ref, q_ref, section, slot, x_in[slots.index(slot)], q_in[g][rows, :])
            set_keys(kv_ref, section, slot, 0, kv_mine[g][rows, :])
            if g < swapped:
                set_keys(kv_ref, section, slot, half, kv_theirs[g][rows, :])


def place(where, groups, kv_mine, kv_theirs, q, parts):
    local, depth = parts[0][0].shape
    half, width = 2 * local, q[0].shape[1]
    args = [*kv_mine, *kv_theirs, *q, *(p for rows in parts for p in rows)]
    return pl.pallas_call(
        functools.partial(place_kernel, groups=groups, swapped=len(kv_theirs)),
        out_shape=(
            jax.ShapeDtypeStruct((SECTIONS * 2 * half, 2 * width), jnp.bfloat16),
            jax.ShapeDtypeStruct((SECTIONS * half, depth), jnp.float32),
            jax.ShapeDtypeStruct((SECTIONS * half, width), jnp.bfloat16),
        ),
        in_specs=[SMEM] + [VMEM] * len(args),
        out_specs=(VMEM,) * 3,
        compiler_params=pltpu.CompilerParams(vmem_limit_bytes=4 << 20),
        cost_estimate=pl.CostEstimate(flops=0, bytes_accessed=4 << 20, transcendentals=0),
        name="place",
    )(where, *args)


def begin_kernel(where, theirs_ref, late_q_ref, own_ref, across_ref, kv_in, x_in, q_in,
                 kv_ref, x_ref, q_ref, top_ref, total_ref, sum_ref, *, groups):
    half = q_ref.shape[0] // SECTIONS
    span = 2 * half
    width = q_ref.shape[1]
    section = where[0]
    for i, slot in enumerate(groups[1]):
        set_keys(kv_ref, section, slot, half, theirs_ref[i * half : (i + 1) * half, :])
    set_rows(x_ref, q_ref, section, groups[2][0], (own_ref, across_ref), late_q_ref[...])
    jobs = []
    for s in range(1, SECTIONS):
        rows, seen = slice((s - 1) * half, s * half), slice(0, s * span)
        for head, (cols, v_cols) in enumerate(head_columns(width)):

            def emit(top, total, summed, head=head, rows=rows, cols=cols):
                top_ref[head, rows, :] = top
                total_ref[head, rows, :] = total
                sum_ref[rows, cols] = summed

            queries = view(q_ref, slice(s * half, (s + 1) * half), cols)
            jobs.append((queries, [(view(kv_ref, seen, cols), view(kv_ref, seen, v_cols))], None, emit))
    attend_all(jobs)


def begin_first(where, groups, placed, theirs, late_q, late_parts):
    half, width = placed[2].shape[0] // SECTIONS, late_q.shape[1]
    same = [jax.ShapeDtypeStruct(p.shape, p.dtype) for p in placed]
    return pl.pallas_call(
        functools.partial(begin_kernel, groups=groups),
        out_shape=(*same, *state_shapes(LAST * half, width)),
        in_specs=[SMEM] + [VMEM] * 7,
        out_specs=(VMEM,) * 6,
        input_output_aliases={5: 0, 6: 1, 7: 2},
        compiler_params=pltpu.CompilerParams(vmem_limit_bytes=12 << 20),
        cost_estimate=pl.CostEstimate(
            flops=24 * half * 2 * half * width, bytes_accessed=2 << 20, transcendentals=0
        ),
        name="begin_first",
    )(where, theirs, late_q, *late_parts, *placed)[1:]


def finish_kernel(where, steps, *refs, groups):
    known = len(groups)
    kv_mine, kv_theirs, refs_q = split(refs, known, known, 5)[:3]
    refs = list(refs)[2 * known + 5 :]
    x_ref, q_ref, top_ref, total_ref, sum_ref = refs_q
    mods_ref, wk_ref, wv_ref, wo_ref = refs[:4]
    stepped_hbm, velocity_hbm, kv2_ref, own2_ref, next_ref = refs[4:9]
    late_ref, o_ref, v_ref, st_ref, hid_ref, out_ref, sem = refs[9:]
    local, depth = next_ref.shape
    half = 2 * local
    width = wk_ref.shape[1]
    section = where[0]

    def set_late(slot):
        for g, group in enumerate(groups):
            if slot in group:
                rows = slice(group.index(slot) * half, (group.index(slot) + 1) * half)
                late_ref[0:half, :] = kv_mine[g][rows, :]
                late_ref[half:, :] = kv_theirs[g][rows, :]

    for s in range(LAST):
        pl.when(section == s)(functools.partial(set_late, s))
    pl.when(section == LAST)(functools.partial(set_late, LAST ^ 1))

    everything = slice(None)

    def late_jobs(queries, into, with_state):
        for head, (cols, v_cols) in enumerate(head_columns(width)):

            def emit(_, total, summed, cols=cols):
                o_ref[into, cols] = (summed / total).astype(jnp.bfloat16)

            def state(head=head, cols=cols):
                return top_ref[head, into], total_ref[head, into], sum_ref[into, cols]

            pairs = [(view(late_ref, everything, cols), view(late_ref, everything, v_cols))]
            yield view(q_ref, queries, cols), pairs, state if with_state else None, emit

    attend_all(list(late_jobs(slice(half, SECTIONS * half), slice(0, LAST * half), True)))
    v_ref[...] = dot(o_ref[...], wo_ref[...])
    for s in range(1, SECTIONS):
        rows = slice((s - 1) * half, s * half)
        stepped = (x_ref[s * half : (s + 1) * half, :] + steps[s] * v_ref[rows, :]).astype(jnp.bfloat16)
        st_ref[rows, :] = stepped
        hid_ref[rows, :] = modulate(
            stepped.astype(jnp.float32), mods_ref[s - 1 : s, depth:], mods_ref[s - 1 : s, :depth]
        )

    @pl.when(section == 0)
    def _():
        attend_all(list(late_jobs(slice(0, local), slice(0, local), False)))
        moving = dot(o_ref[0:local, :], wo_ref[...])
        out_ref[0] = (x_ref[0:local, :] + steps[0] * moving).astype(jnp.bfloat16)
        out_ref[1] = moving.astype(jnp.bfloat16)

    @pl.when(section > 0)
    def _():
        base = pl.multiple_of((section - 1) * half, half)
        out_ref[0] = st_ref[pl.ds(base, half), :][:local]
        out_ref[1] = v_ref[pl.ds(base, half), :][:local].astype(jnp.bfloat16)

    copies = [
        pltpu.make_async_copy(out_ref.at[0], stepped_hbm.at[0], sem.at[0]),
        pltpu.make_async_copy(out_ref.at[1], velocity_hbm.at[0], sem.at[1]),
    ]
    for c in copies:
        c.start()
    base = pl.multiple_of(jnp.minimum(section, LAST - 1) * half, half)
    own2_ref[...] = hid_ref[pl.ds(base, half), :][:local]
    next_ref[...] = st_ref[pl.ds(base, half), :][:local]
    kv2_ref[:, :width] = dot(hid_ref[...], wk_ref[...]).astype(jnp.bfloat16)
    kv2_ref[:, width:] = dot(hid_ref[...], wv_ref[...]).astype(jnp.bfloat16)
    for c in copies:
        c.wait()


def finish_first(where, steps, groups, kv_mine, kv_theirs, begun, mods, w_key, w_value, w_out):
    depth, width = w_key.shape
    half = begun[0].shape[0] // SECTIONS
    local = half // 2
    pair = jax.ShapeDtypeStruct((2, local, depth), jnp.bfloat16)
    one = jax.ShapeDtypeStruct((local, depth), jnp.bfloat16)
    args = [*kv_mine, *kv_theirs, *begun, mods, w_key, w_value, w_out]
    return pl.pallas_call(
        functools.partial(finish_kernel, groups=groups),
        out_shape=(pair, pair, jax.ShapeDtypeStruct((LAST * half, 2 * width), jnp.bfloat16), one, one),
        in_specs=[SMEM, SMEM] + [VMEM] * len(args),
        out_specs=(HBM, HBM, VMEM, VMEM, VMEM),
        scratch_shapes=[
            pltpu.VMEM((2 * half, 2 * width), jnp.bfloat16),
            pltpu.VMEM((LAST * half, width), jnp.bfloat16),
            pltpu.VMEM((LAST * half, depth), jnp.float32),
            pltpu.VMEM((LAST * half, depth), jnp.bfloat16),
            pltpu.VMEM((LAST * half, depth), jnp.bfloat16),
            pltpu.VMEM((2, local, depth), jnp.bfloat16),
            pltpu.SemaphoreType.DMA((2,)),
        ],
        compiler_params=pltpu.CompilerParams(vmem_limit_bytes=18 << 20),
        cost_estimate=pl.CostEstimate(
            flops=8 * LAST * half * depth * width, bytes_accessed=4 << 20, transcendentals=0
        ),
        name="finish_first",
    )(where, steps, *args)


def begin_second_kernel(
    where, own_ref, wq_ref, mine_ref, fresh_q_ref, fresh_mine_ref, fresh_theirs_ref,
    q_ref, top_ref, total_ref, sum_ref, *, fresh_row,
):
    local, width = q_ref.shape
    half = 2 * local
    section = where[0]

    def run(seen):
        jobs = []
        for head, (cols, v_cols) in enumerate(head_columns(width)):

            def emit(top, total, summed, head=head, cols=cols):
                top_ref[head], total_ref[head], sum_ref[:, cols] = top, total, summed

            pairs = [(view(r, rows, cols), view(r, rows, v_cols)) for r, rows in seen]
            jobs.append((view(q_ref, slice(None), cols), pairs, None, emit))
        attend_all(jobs)

    for s in range(LAST):

        @pl.when(section == s)
        def _():
            q_ref[...] = dot(own_ref[...], wq_ref[...]).astype(jnp.bfloat16)
            run([(mine_ref, slice(0, (s + 1) * half))])

    @pl.when(section == LAST)
    def _():
        fresh_rows = slice(fresh_row, fresh_row + half)
        q_ref[...] = fresh_q_ref[fresh_row : fresh_row + local, :]
        run([(mine_ref, slice(0, LAST * half)), (fresh_mine_ref, fresh_rows), (fresh_theirs_ref, fresh_rows)])


def begin_second(where, own2, w_query, mine2, fresh_q, fresh_mine, fresh_theirs, fresh_row):
    local, width = own2.shape[0], w_query.shape[1]
    return pl.pallas_call(
        functools.partial(begin_second_kernel, fresh_row=fresh_row),
        out_shape=(jax.ShapeDtypeStruct((local, width), jnp.bfloat16), *state_shapes(local, width)),
        in_specs=[SMEM] + [VMEM] * 6,
        out_specs=(VMEM,) * 4,
        compiler_params=pltpu.CompilerParams(vmem_limit_bytes=8 << 20),
        cost_estimate=pl.CostEstimate(
            flops=4 * local * own2.shape[1] * width, bytes_accessed=2 << 20, transcendentals=0
        ),
        name="begin_second",
    )(where, own2, w_query, mine2, fresh_q, fresh_mine, fresh_theirs)


def finish_second_kernel(
    where, steps, q_ref, top_ref, total_ref, sum_ref, theirs_ref, old_ref, fresh_ref, wo_ref, _s, _v,
    stepped_hbm, velocity_hbm, o_ref, x_ref, out_ref, sem,
):
    local, width = q_ref.shape
    section = where[0]

    def run(seen):
        jobs = []
        for head, (cols, v_cols) in enumerate(head_columns(width)):

            def emit(_, total, summed, cols=cols):
                o_ref[:, cols] = (summed / total).astype(jnp.bfloat16)

            def state(head=head, cols=cols):
                return top_ref[head], total_ref[head], sum_ref[:, cols]

            pairs = [(view(theirs_ref, slice(0, seen), cols), view(theirs_ref, slice(0, seen), v_cols))]
            jobs.append((view(q_ref, slice(None), cols), pairs, state, emit))
        attend_all(jobs)

    for s in range(LAST):
        reached = (section >= s) if s == LAST - 1 else (section == s)
        pl.when(reached)(functools.partial(run, (s + 1) * 2 * local))
    x_ref[...] = old_ref[...]

    @pl.when(section == LAST)
    def _():
        x_ref[...] = fresh_ref[...]

    moving = dot(o_ref[...], wo_ref[...])
    out_ref[0] = (x_ref[...].astype(jnp.float32) + steps[section] * moving).astype(jnp.bfloat16)
    out_ref[1] = moving.astype(jnp.bfloat16)
    copies = [
        pltpu.make_async_copy(out_ref.at[0], stepped_hbm.at[1], sem.at[0]),
        pltpu.make_async_copy(out_ref.at[1], velocity_hbm.at[1], sem.at[1]),
    ]
    for c in copies:
        c.start()
    for c in copies:
        c.wait()


def finish_second(where, steps, begun, theirs2, old, fresh, w_out, stepped, velocity):
    local, width = begun[0].shape
    pair = jax.ShapeDtypeStruct(stepped.shape, stepped.dtype)
    return pl.pallas_call(
        finish_second_kernel,
        out_shape=(pair, pair),
        in_specs=[SMEM, SMEM] + [VMEM] * 8 + [HBM, HBM],
        out_specs=(HBM, HBM),
        scratch_shapes=[
            pltpu.VMEM((local, width), jnp.bfloat16),
            pltpu.VMEM(old.shape, jnp.bfloat16),
            pltpu.VMEM((2, *old.shape), jnp.bfloat16),
            pltpu.SemaphoreType.DMA((2,)),
        ],
        input_output_aliases={10: 0, 11: 1},
        compiler_params=pltpu.CompilerParams(vmem_limit_bytes=8 << 20),
        cost_estimate=pl.CostEstimate(
            flops=4 * local * old.shape[1] * width, bytes_accessed=4 << 20, transcendentals=0
        ),
        name="finish_second",
    )(where, steps, *begun, theirs2, old, fresh, w_out, stepped, velocity)


def chip_body(latents, fresh_noise, levels, time_weight, w_query, w_key, w_value, w_out):
    per_section = lax.axis_size("tok") // SECTIONS
    where = (lax.axis_index("tok") // per_section).astype(jnp.int32).reshape(1)

    def needs(section, source):
        return source <= section + 1

    def from_section(block, slot):
        def move(i):
            section, within = i // per_section, i % per_section
            target = section ^ slot
            return target * per_section + within if needs(target, section) else None

        return permuted(block, "tok", move)

    def chip_swap(block):
        return permuted(block, "tok", lambda i: i ^ CORES)

    def core_swap(block):
        return permuted(block, "tok", lambda i: i ^ 1)

    def after(value, *others):
        return lax.optimization_barrier((value, *others))[0]

    embedding, steps = lax.optimization_barrier(
        (level_embedding(levels, time_weight.shape[0] // 2), level_steps(levels))
    )
    w_key, w_value, w_query, w_out, mods = fetch(
        (w_key, w_value, w_query, w_out), embedding, time_weight
    )
    weights = (w_key, w_value, w_query)

    groups = ((0, None), (1, 3), (2,))
    own = {0: latents, None: fresh_noise}
    for slot in (3, 1, 2):
        own[slot] = from_section(latents, slot)
    parts = {slot: [own[slot], chip_swap(own[slot])] for slot in (0, None, 3)}
    parts[1] = [own[1], from_section(parts[0][1], 1)]
    mine, theirs, q = {}, {}, {}

    def work(group):
        mine[group], q[group] = project(where, group, [parts[x] for x in group], mods, weights)
        theirs[group] = core_swap(mine[group])

    work(groups[0])
    own[2] = after(own[2], own[3], mine[groups[0]])
    parts[2] = [own[2], chip_swap(own[2])]
    work(groups[1])
    early = groups[:-1]
    placed = place(
        where, early, [mine[g] for g in early], [theirs[groups[0]]], [q[g] for g in early],
        [parts[x] for g in early for x in g if x is not None],
    )
    parts[2][1] = after(parts[2][1], *placed)
    work(groups[2])
    all_mine, all_theirs = [mine[g] for g in groups], [theirs[g] for g in groups]
    begun = begin_first(
        where, groups, placed, theirs[groups[1]], q[groups[2]], parts[groups[2][0]]
    )
    stepped, velocity, mine2, own2, old = finish_first(
        where, steps, groups, all_mine, all_theirs, begun, mods, w_key, w_value, w_out
    )
    theirs2 = core_swap(mine2)
    first = groups[0]
    begun = begin_second(
        where, own2, w_query, mine2, q[first], mine[first], theirs[first],
        first.index(None) * 2 * latents.shape[0],
    )
    return finish_second(where, steps, begun, theirs2, old, fresh_noise, w_out, stepped, velocity)


def solution(mesh):
    per_section = mesh.shape["tok"] // SECTIONS
    on_chips = per_section == 2 * CORES
    rows = P(("groups", "tok"), None)
    return jax.shard_map(
        chip_body if on_chips else gathered_body,
        mesh=mesh,
        in_specs=(rows, rows, P(), P(), P(), P(), P(), P()),
        out_specs=(P(None, ("groups", "tok"), None), P(None, ("groups", "tok"), None)),
        check_vma=False,
    )
```

```python
import functools
import math

import jax
import jax.numpy as jnp
from jax import lax
from jax.experimental import pallas as pl
from jax.experimental.pallas import tpu as pltpu
from jax.sharding import PartitionSpec as P


HEAD_DIM = 128
SECTIONS = 4
CORES = 2

epsilon = 1e-06


def permuted(block, axis, move):
    devices = range(lax.axis_size(axis))
    route = [(i, move(i)) for i in devices if move(i) is not None and move(i) in devices]
    return lax.ppermute(block, axis, route)


def level_embedding(levels, half_width):
    frequency = jnp.exp(-math.log(10000.0) * jnp.arange(half_width, dtype=jnp.float32) / half_width)
    angles = levels.astype(jnp.float32)[:, None] * frequency[None, :]
    return jnp.concatenate([jnp.cos(angles), jnp.sin(angles)], axis=1)


def embed_levels(levels, time_weight):
    return jnp.dot(
        level_embedding(levels, time_weight.shape[0] // 2),
        time_weight.astype(jnp.float32),
        precision=lax.Precision.HIGHEST,
    )


def level_steps(levels):
    previous = jnp.concatenate([jnp.zeros((1,), jnp.int32), levels[:-1]])
    return (previous - levels).astype(jnp.float32) / 1000.0


def gathered_body(latents, fresh_noise, levels, time_weight, w_query, w_key, w_value, w_out):
    local_rows = latents.shape[0]
    heads = w_query.shape[1] // HEAD_DIM
    per_section = lax.axis_size("tok") // SECTIONS
    span_rows = local_rows * per_section
    my_block = lax.axis_index("tok") // per_section
    section_ids = jnp.arange(SECTIONS, dtype=jnp.int32)
    mods = embed_levels(levels, time_weight)
    width = mods.shape[1] // 2
    shift_all, scale_all = mods[:, :width], mods[:, width:]
    chosen = section_ids == my_block
    shift_vec = jnp.sum(jnp.where(chosen[:, None], shift_all, 0.0), axis=0)
    scale_vec = jnp.sum(jnp.where(chosen[:, None], scale_all, 0.0), axis=0)
    step_size = jnp.sum(jnp.where(chosen, level_steps(levels), 0.0))

    def denoise_local(rows):
        rows_f = rows.astype(jnp.float32)
        normed = rows_f * lax.rsqrt(jnp.mean(rows_f * rows_f, axis=-1, keepdims=True) + epsilon)
        hidden = (normed * (1.0 + scale_vec) + shift_vec).astype(jnp.bfloat16)

        def project(weight):
            return jnp.dot(hidden, weight, preferred_element_type=jnp.float32).astype(jnp.bfloat16)

        queries = project(w_query).reshape(local_rows, heads, HEAD_DIM)
        keys = lax.all_gather(project(w_key), "tok", axis=0, tiled=True)
        values = lax.all_gather(project(w_value), "tok", axis=0, tiled=True)
        count = keys.shape[0]
        allowed = (jnp.arange(count, dtype=jnp.int32) // span_rows <= my_block)[None, None, :]
        scores = jnp.einsum(
            "rhd,phd->hrp",
            queries,
            keys.reshape(count, heads, HEAD_DIM),
            preferred_element_type=jnp.float32,
        ) / math.sqrt(HEAD_DIM)
        scores = jnp.where(allowed, scores, -1e30)
        best = jnp.max(scores, axis=-1)
        weights = jnp.where(allowed, jnp.exp(scores - best[..., None]), 0.0)
        denominator = jnp.sum(weights, axis=-1)
        summed = jnp.einsum(
            "hrp,phd->hrd",
            weights.astype(jnp.bfloat16),
            values.reshape(count, heads, HEAD_DIM),
            preferred_element_type=jnp.float32,
        )
        attended = (summed / denominator[..., None]).astype(jnp.bfloat16)
        attended = attended.transpose(1, 0, 2).reshape(local_rows, heads * HEAD_DIM)
        moving = jnp.dot(attended, w_out, preferred_element_type=jnp.float32)
        stepped = (rows_f + step_size * moving).astype(jnp.bfloat16)
        return (stepped, moving.astype(jnp.bfloat16))

    first, first_moving = denoise_local(latents)
    incoming = permuted(first, "tok", lambda i: i - per_section)
    second_input = jnp.where(my_block == SECTIONS - 1, fresh_noise, incoming)
    second, second_moving = denoise_local(second_input)
    return (jnp.stack([first, second]), jnp.stack([first_moving, second_moving]))


VMEM = pl.BlockSpec(memory_space=pltpu.VMEM)
SMEM = pl.BlockSpec(memory_space=pltpu.SMEM)
HBM = pl.BlockSpec(memory_space=pltpu.HBM)
LAST = SECTIONS - 1


def modulate(rows_f, scale_row, shift_row):
    normed = rows_f * lax.rsqrt(jnp.mean(rows_f * rows_f, axis=-1, keepdims=True) + epsilon)
    return (normed * (1.0 + scale_row) + shift_row).astype(jnp.bfloat16)


def dot(a, b):
    return jnp.dot(a, b, preferred_element_type=jnp.float32)


SHARPNESS = math.log2(math.e) / math.sqrt(HEAD_DIM)


def score(queries, pairs):
    return [
        lax.dot_general(queries(), keys(), (((1,), (1,)), ((), ())), preferred_element_type=jnp.float32)
        for keys, _ in pairs
    ]


def weigh(scores, pairs, state=None):
    top = functools.reduce(jnp.maximum, [jnp.max(s, axis=-1, keepdims=True) for s in scores])
    rows = top.shape[0]
    top = jnp.broadcast_to(top, (rows, HEAD_DIM))
    if state is not None:
        old_top, old_total, old_summed = state()
        top = jnp.maximum(top, old_top)
    total, summed = 0.0, 0.0
    for part, (_, values) in zip(scores, pairs):
        rounded = []
        sums = []
        for low in range(0, part.shape[1], HEAD_DIM):
            piece = part[:, low : low + HEAD_DIM]
            weights = jnp.exp2((piece - top[:, : piece.shape[1]]) * SHARPNESS)
            sums.append(jnp.sum(weights, axis=-1, keepdims=True) if piece.shape[1] < HEAD_DIM else weights)
            rounded.append(weights.astype(jnp.bfloat16))
        full = [w for w in sums if w.shape[1] == HEAD_DIM]
        for w in [functools.reduce(jnp.add, full)] * (len(full) > 0) + [w for w in sums if w.shape[1] < HEAD_DIM]:
            total = total + jnp.sum(w, axis=-1, keepdims=True)
        summed = summed + dot(jnp.concatenate(rounded, axis=1), values())
    total = jnp.broadcast_to(total, (rows, HEAD_DIM))
    if state is not None:
        fade = jnp.exp2((old_top - top) * SHARPNESS)
        total, summed = old_total * fade + total, old_summed * fade + summed
    return top, total, summed


AHEAD = 3


def attend_all(jobs):
    pending = [score(*job[:2]) for job in jobs[:AHEAD]]
    for i, (_, pairs, state, emit) in enumerate(jobs):
        if i + AHEAD < len(jobs):
            pending.append(score(*jobs[i + AHEAD][:2]))
        emit(*weigh(pending.pop(0), pairs, state))


def view(ref, *where):
    return lambda: ref[where]


def head_columns(width):
    for head in range(width // HEAD_DIM):
        yield slice(head * HEAD_DIM, (head + 1) * HEAD_DIM), slice(
            width + head * HEAD_DIM, width + (head + 1) * HEAD_DIM
        )


def fetch_kernel(*refs, count):
    sources, embedding_ref, time_hbm = refs[:count], refs[count], refs[count + 1]
    outs, mods_ref = refs[count + 2 : 2 * count + 2], refs[2 * count + 2]
    time_ref, sem = refs[2 * count + 3 :]
    time_copy = pltpu.make_async_copy(time_hbm, time_ref, sem.at[count])
    time_copy.start()
    copies = [pltpu.make_async_copy(sources[i], outs[i], sem.at[i]) for i in range(count)]
    for c in copies:
        c.start()
    rest = embedding_ref[...]
    modulated = None
    time_copy.wait()
    for _ in range(3):
        term = rest.astype(jnp.bfloat16)
        rest = rest - term.astype(jnp.float32)
        product = dot(term, time_ref[...])
        modulated = product if modulated is None else modulated + product
    mods_ref[...] = modulated
    for c in copies:
        c.wait()


def fetch(arrays, embedding, time_weight):
    in_hbm = [pltpu.with_memory_space_constraint(a, pltpu.HBM) for a in (*arrays, time_weight)]
    return pl.pallas_call(
        functools.partial(fetch_kernel, count=len(arrays)),
        out_shape=[jax.ShapeDtypeStruct(a.shape, a.dtype) for a in arrays]
        + [jax.ShapeDtypeStruct((embedding.shape[0], time_weight.shape[1]), jnp.float32)],
        in_specs=[HBM] * len(arrays) + [VMEM, HBM],
        out_specs=[VMEM] * (len(arrays) + 1),
        scratch_shapes=[
            pltpu.VMEM(time_weight.shape, time_weight.dtype),
            pltpu.SemaphoreType.DMA((len(arrays) + 1,)),
        ],
        compiler_params=pltpu.CompilerParams(vmem_limit_bytes=6 << 20),
        cost_estimate=pl.CostEstimate(
            flops=0, bytes_accessed=sum(a.size * 2 for a in arrays), transcendentals=0
        ),
        name="fetch",
    )(*in_hbm[:-1], embedding, in_hbm[-1])


def project_kernel(where, *refs, slots, counts):
    refs = list(refs)
    parts = [[refs.pop(0) for _ in range(n)] for n in counts]
    mods_ref, wk_ref, wv_ref, wq_ref, kv_ref, q_ref = refs
    depth, width = wk_ref.shape
    hidden = []
    for i, slot in enumerate(slots):
        rows_f = jnp.concatenate([part[...].astype(jnp.float32) for part in parts[i]])
        section = LAST if slot is None else where[0] ^ slot
        row = mods_ref[pl.ds(section, 1), :]
        hidden.append(modulate(rows_f, row[:, depth:], row[:, :depth]))
    hidden = jnp.concatenate(hidden)
    kv_ref[:, :width] = dot(hidden, wk_ref[...]).astype(jnp.bfloat16)
    kv_ref[:, width:] = dot(hidden, wv_ref[...]).astype(jnp.bfloat16)
    q_ref[...] = dot(hidden, wq_ref[...]).astype(jnp.bfloat16)


def project(where, slots, parts, mods, weights):
    args = [p for rows in parts for p in rows]
    depth, width = weights[0].shape
    rows = sum(p.shape[0] for p in args)
    return pl.pallas_call(
        functools.partial(project_kernel, slots=slots, counts=[len(p) for p in parts]),
        out_shape=(
            jax.ShapeDtypeStruct((rows, 2 * width), jnp.bfloat16),
            jax.ShapeDtypeStruct((rows, width), jnp.bfloat16),
        ),
        in_specs=[SMEM] + [VMEM] * (len(args) + 4),
        out_specs=(VMEM, VMEM),
        compiler_params=pltpu.CompilerParams(vmem_limit_bytes=12 << 20),
        cost_estimate=pl.CostEstimate(
            flops=6 * rows * depth * width, bytes_accessed=2 << 20, transcendentals=0
        ),
        name="project",
    )(where, *args, mods, *weights)


def state_shapes(rows, width):
    stat = jax.ShapeDtypeStruct((width // HEAD_DIM, rows, HEAD_DIM), jnp.float32)
    return stat, stat, jax.ShapeDtypeStruct((rows, width), jnp.float32)


def split(refs, *counts):
    refs = list(refs)
    return [[refs.pop(0) for _ in range(n)] for n in counts] + refs


def key_place(section, slot):
    source = section ^ slot
    swapped = jnp.where(section == LAST, 1 - source, source)
    return jnp.where(source > 1, source - 1, jnp.where(swapped == 1, 0, LAST))


def set_keys(kv_ref, section, slot, offset, block):
    base = key_place(section, slot) * (kv_ref.shape[0] // SECTIONS) + offset
    kv_ref[pl.ds(pl.multiple_of(base, 16), block.shape[0]), :] = block


def set_rows(x_ref, q_ref, section, slot, parts, queries):
    half = q_ref.shape[0] // SECTIONS
    base = pl.multiple_of((section ^ slot) * half, half)
    q_ref[pl.ds(base, half), :] = queries
    low = 0
    for part in parts:
        x_ref[pl.ds(pl.multiple_of(base + low, 8), part.shape[0]), :] = part[...].astype(jnp.float32)
        low += part.shape[0]


def place_kernel(where, *refs, groups, swapped):
    slots = [slot for group in groups for slot in group if slot is not None]
    kv_mine, kv_theirs, q_in, *refs = split(refs, len(groups), swapped, len(groups))
    *x_in, out = split(refs, *[2] * len(slots), 3)
    kv_ref, x_ref, q_ref = out
    half = q_ref.shape[0] // SECTIONS
    section = where[0]
    for g, group in enumerate(groups):
        for i, slot in enumerate(group):
            if slot is None:
                continue
            rows = slice(i * half, (i + 1) * half)
            set_rows(x_ref, q_ref, section, slot, x_in[slots.index(slot)], q_in[g][rows, :])
            set_keys(kv_ref, section, slot, 0, kv_mine[g][rows, :])
            if g < swapped:
                set_keys(kv_ref, section, slot, half, kv_theirs[g][rows, :])


def place(where, groups, kv_mine, kv_theirs, q, parts):
    local, depth = parts[0][0].shape
    half, width = 2 * local, q[0].shape[1]
    args = [*kv_mine, *kv_theirs, *q, *(p for rows in parts for p in rows)]
    return pl.pallas_call(
        functools.partial(place_kernel, groups=groups, swapped=len(kv_theirs)),
        out_shape=(
            jax.ShapeDtypeStruct((SECTIONS * 2 * half, 2 * width), jnp.bfloat16),
            jax.ShapeDtypeStruct((SECTIONS * half, depth), jnp.float32),
            jax.ShapeDtypeStruct((SECTIONS * half, width), jnp.bfloat16),
        ),
        in_specs=[SMEM] + [VMEM] * len(args),
        out_specs=(VMEM,) * 3,
        compiler_params=pltpu.CompilerParams(vmem_limit_bytes=4 << 20),
        cost_estimate=pl.CostEstimate(flops=0, bytes_accessed=4 << 20, transcendentals=0),
        name="place",
    )(where, *args)


def begin_kernel(where, theirs_ref, late_q_ref, own_ref, across_ref, kv_in, x_in, q_in,
                 kv_ref, x_ref, q_ref, top_ref, total_ref, sum_ref, *, groups):
    half = q_ref.shape[0] // SECTIONS
    span = 2 * half
    width = q_ref.shape[1]
    section = where[0]
    for i, slot in enumerate(groups[1]):
        set_keys(kv_ref, section, slot, half, theirs_ref[i * half : (i + 1) * half, :])
    set_rows(x_ref, q_ref, section, groups[2][0], (own_ref, across_ref), late_q_ref[...])
    jobs = []
    for s in range(1, SECTIONS):
        rows, seen = slice((s - 1) * half, s * half), slice(0, s * span)
        for head, (cols, v_cols) in enumerate(head_columns(width)):

            def emit(top, total, summed, head=head, rows=rows, cols=cols):
                top_ref[head, rows, :] = top
                total_ref[head, rows, :] = total
                sum_ref[rows, cols] = summed

            queries = view(q_ref, slice(s * half, (s + 1) * half), cols)
            jobs.append((queries, [(view(kv_ref, seen, cols), view(kv_ref, seen, v_cols))], None, emit))
    attend_all(jobs)


def begin_first(where, groups, placed, theirs, late_q, late_parts):
    half, width = placed[2].shape[0] // SECTIONS, late_q.shape[1]
    same = [jax.ShapeDtypeStruct(p.shape, p.dtype) for p in placed]
    return pl.pallas_call(
        functools.partial(begin_kernel, groups=groups),
        out_shape=(*same, *state_shapes(LAST * half, width)),
        in_specs=[SMEM] + [VMEM] * 7,
        out_specs=(VMEM,) * 6,
        input_output_aliases={5: 0, 6: 1, 7: 2},
        compiler_params=pltpu.CompilerParams(vmem_limit_bytes=12 << 20),
        cost_estimate=pl.CostEstimate(
            flops=24 * half * 2 * half * width, bytes_accessed=2 << 20, transcendentals=0
        ),
        name="begin_first",
    )(where, theirs, late_q, *late_parts, *placed)[1:]


def finish_kernel(where, steps, *refs, groups):
    known = len(groups)
    kv_mine, kv_theirs, refs_q = split(refs, known, known, 5)[:3]
    refs = list(refs)[2 * known + 5 :]
    x_ref, q_ref, top_ref, total_ref, sum_ref = refs_q
    mods_ref, wk_ref, wv_ref, wo_ref = refs[:4]
    stepped_hbm, velocity_hbm, kv2_ref, own2_ref, next_ref = refs[4:9]
    late_ref, o_ref, v_ref, st_ref, hid_ref, out_ref, sem = refs[9:]
    local, depth = next_ref.shape
    half = 2 * local
    width = wk_ref.shape[1]
    section = where[0]

    def set_late(slot):
        for g, group in enumerate(groups):
            if slot in group:
                rows = slice(group.index(slot) * half, (group.index(slot) + 1) * half)
                late_ref[0:half, :] = kv_mine[g][rows, :]
                late_ref[half:, :] = kv_theirs[g][rows, :]

    for s in range(LAST):
        pl.when(section == s)(functools.partial(set_late, s))
    pl.when(section == LAST)(functools.partial(set_late, LAST ^ 1))

    everything = slice(None)

    def late_jobs(queries, into, with_state):
        for head, (cols, v_cols) in enumerate(head_columns(width)):

            def emit(_, total, summed, cols=cols):
                o_ref[into, cols] = (summed / total).astype(jnp.bfloat16)

            def state(head=head, cols=cols):
                return top_ref[head, into], total_ref[head, into], sum_ref[into, cols]

            pairs = [(view(late_ref, everything, cols), view(late_ref, everything, v_cols))]
            yield view(q_ref, queries, cols), pairs, state if with_state else None, emit

    attend_all(list(late_jobs(slice(half, SECTIONS * half), slice(0, LAST * half), True)))
    v_ref[...] = dot(o_ref[...], wo_ref[...])
    for s in range(1, SECTIONS):
        rows = slice((s - 1) * half, s * half)
        stepped = (x_ref[s * half : (s + 1) * half, :] + steps[s] * v_ref[rows, :]).astype(jnp.bfloat16)
        st_ref[rows, :] = stepped
        hid_ref[rows, :] = modulate(
            stepped.astype(jnp.float32), mods_ref[s - 1 : s, depth:], mods_ref[s - 1 : s, :depth]
        )

    @pl.when(section == 0)
    def _():
        attend_all(list(late_jobs(slice(0, local), slice(0, local), False)))
        moving = dot(o_ref[0:local, :], wo_ref[...])
        out_ref[0] = (x_ref[0:local, :] + steps[0] * moving).astype(jnp.bfloat16)
        out_ref[1] = moving.astype(jnp.bfloat16)

    @pl.when(section > 0)
    def _():
        base = pl.multiple_of((section - 1) * half, half)
        out_ref[0] = st_ref[pl.ds(base, half), :][:local]
        out_ref[1] = v_ref[pl.ds(base, half), :][:local].astype(jnp.bfloat16)

    copies = [
        pltpu.make_async_copy(out_ref.at[0], stepped_hbm.at[0], sem.at[0]),
        pltpu.make_async_copy(out_ref.at[1], velocity_hbm.at[0], sem.at[1]),
    ]
    for c in copies:
        c.start()
    base = pl.multiple_of(jnp.minimum(section, LAST - 1) * half, half)
    own2_ref[...] = hid_ref[pl.ds(base, half), :][:local]
    next_ref[...] = st_ref[pl.ds(base, half), :][:local]
    kv2_ref[:, :width] = dot(hid_ref[...], wk_ref[...]).astype(jnp.bfloat16)
    kv2_ref[:, width:] = dot(hid_ref[...], wv_ref[...]).astype(jnp.bfloat16)
    for c in copies:
        c.wait()


def finish_first(where, steps, groups, kv_mine, kv_theirs, begun, mods, w_key, w_value, w_out):
    depth, width = w_key.shape
    half = begun[0].shape[0] // SECTIONS
    local = half // 2
    pair = jax.ShapeDtypeStruct((2, local, depth), jnp.bfloat16)
    one = jax.ShapeDtypeStruct((local, depth), jnp.bfloat16)
    args = [*kv_mine, *kv_theirs, *begun, mods, w_key, w_value, w_out]
    return pl.pallas_call(
        functools.partial(finish_kernel, groups=groups),
        out_shape=(pair, pair, jax.ShapeDtypeStruct((LAST * half, 2 * width), jnp.bfloat16), one, one),
        in_specs=[SMEM, SMEM] + [VMEM] * len(args),
        out_specs=(HBM, HBM, VMEM, VMEM, VMEM),
        scratch_shapes=[
            pltpu.VMEM((2 * half, 2 * width), jnp.bfloat16),
            pltpu.VMEM((LAST * half, width), jnp.bfloat16),
            pltpu.VMEM((LAST * half, depth), jnp.float32),
            pltpu.VMEM((LAST * half, depth), jnp.bfloat16),
            pltpu.VMEM((LAST * half, depth), jnp.bfloat16),
            pltpu.VMEM((2, local, depth), jnp.bfloat16),
            pltpu.SemaphoreType.DMA((2,)),
        ],
        compiler_params=pltpu.CompilerParams(vmem_limit_bytes=18 << 20),
        cost_estimate=pl.CostEstimate(
            flops=8 * LAST * half * depth * width, bytes_accessed=4 << 20, transcendentals=0
        ),
        name="finish_first",
    )(where, steps, *args)


def begin_second_kernel(
    where, own_ref, wq_ref, mine_ref, fresh_q_ref, fresh_mine_ref, fresh_theirs_ref,
    q_ref, top_ref, total_ref, sum_ref, *, fresh_row,
):
    local, width = q_ref.shape
    half = 2 * local
    section = where[0]

    def run(seen):
        jobs = []
        for head, (cols, v_cols) in enumerate(head_columns(width)):

            def emit(top, total, summed, head=head, cols=cols):
                top_ref[head], total_ref[head], sum_ref[:, cols] = top, total, summed

            pairs = [(view(r, rows, cols), view(r, rows, v_cols)) for r, rows in seen]
            jobs.append((view(q_ref, slice(None), cols), pairs, None, emit))
        attend_all(jobs)

    for s in range(LAST):

        @pl.when(section == s)
        def _():
            q_ref[...] = dot(own_ref[...], wq_ref[...]).astype(jnp.bfloat16)
            run([(mine_ref, slice(0, (s + 1) * half))])

    @pl.when(section == LAST)
    def _():
        fresh_rows = slice(fresh_row, fresh_row + half)
        q_ref[...] = fresh_q_ref[fresh_row : fresh_row + local, :]
        run([(mine_ref, slice(0, LAST * half)), (fresh_mine_ref, fresh_rows), (fresh_theirs_ref, fresh_rows)])


def begin_second(where, own2, w_query, mine2, fresh_q, fresh_mine, fresh_theirs, fresh_row):
    local, width = own2.shape[0], w_query.shape[1]
    return pl.pallas_call(
        functools.partial(begin_second_kernel, fresh_row=fresh_row),
        out_shape=(jax.ShapeDtypeStruct((local, width), jnp.bfloat16), *state_shapes(local, width)),
        in_specs=[SMEM] + [VMEM] * 6,
        out_specs=(VMEM,) * 4,
        compiler_params=pltpu.CompilerParams(vmem_limit_bytes=8 << 20),
        cost_estimate=pl.CostEstimate(
            flops=4 * local * own2.shape[1] * width, bytes_accessed=2 << 20, transcendentals=0
        ),
        name="begin_second",
    )(where, own2, w_query, mine2, fresh_q, fresh_mine, fresh_theirs)


def finish_second_kernel(
    where, steps, q_ref, top_ref, total_ref, sum_ref, theirs_ref, old_ref, fresh_ref, wo_ref, _s, _v,
    stepped_hbm, velocity_hbm, o_ref, x_ref, out_ref, sem,
):
    local, width = q_ref.shape
    section = where[0]

    def run(seen):
        jobs = []
        for head, (cols, v_cols) in enumerate(head_columns(width)):

            def emit(_, total, summed, cols=cols):
                o_ref[:, cols] = (summed / total).astype(jnp.bfloat16)

            def state(head=head, cols=cols):
                return top_ref[head], total_ref[head], sum_ref[:, cols]

            pairs = [(view(theirs_ref, slice(0, seen), cols), view(theirs_ref, slice(0, seen), v_cols))]
            jobs.append((view(q_ref, slice(None), cols), pairs, state, emit))
        attend_all(jobs)

    for s in range(LAST):
        reached = (section >= s) if s == LAST - 1 else (section == s)
        pl.when(reached)(functools.partial(run, (s + 1) * 2 * local))
    x_ref[...] = old_ref[...]

    @pl.when(section == LAST)
    def _():
        x_ref[...] = fresh_ref[...]

    moving = dot(o_ref[...], wo_ref[...])
    out_ref[0] = (x_ref[...].astype(jnp.float32) + steps[section] * moving).astype(jnp.bfloat16)
    out_ref[1] = moving.astype(jnp.bfloat16)
    copies = [
        pltpu.make_async_copy(out_ref.at[0], stepped_hbm.at[1], sem.at[0]),
        pltpu.make_async_copy(out_ref.at[1], velocity_hbm.at[1], sem.at[1]),
    ]
    for c in copies:
        c.start()
    for c in copies:
        c.wait()


def finish_second(where, steps, begun, theirs2, old, fresh, w_out, stepped, velocity):
    local, width = begun[0].shape
    pair = jax.ShapeDtypeStruct(stepped.shape, stepped.dtype)
    return pl.pallas_call(
        finish_second_kernel,
        out_shape=(pair, pair),
        in_specs=[SMEM, SMEM] + [VMEM] * 8 + [HBM, HBM],
        out_specs=(HBM, HBM),
        scratch_shapes=[
            pltpu.VMEM((local, width), jnp.bfloat16),
            pltpu.VMEM(old.shape, jnp.bfloat16),
            pltpu.VMEM((2, *old.shape), jnp.bfloat16),
            pltpu.SemaphoreType.DMA((2,)),
        ],
        input_output_aliases={10: 0, 11: 1},
        compiler_params=pltpu.CompilerParams(vmem_limit_bytes=8 << 20),
        cost_estimate=pl.CostEstimate(
            flops=4 * local * old.shape[1] * width, bytes_accessed=4 << 20, transcendentals=0
        ),
        name="finish_second",
    )(where, steps, *begun, theirs2, old, fresh, w_out, stepped, velocity)


def chip_body(latents, fresh_noise, levels, time_weight, w_query, w_key, w_value, w_out):
    per_section = lax.axis_size("tok") // SECTIONS
    where = (lax.axis_index("tok") // per_section).astype(jnp.int32).reshape(1)

    def needs(section, source):
        return source <= section + 1

    def from_section(block, slot):
        def move(i):
            section, within = i // per_section, i % per_section
            target = section ^ slot
            return target * per_section + within if needs(target, section) else None

        return permuted(block, "tok", move)

    def chip_swap(block, slot):
        def move(i):
            section = i // per_section
            needed = section == LAST if slot is None else needs(section, section ^ slot)
            return i ^ CORES if needed else i

        return permuted(block, "tok", move)

    def core_swap(block):
        return permuted(block, "tok", lambda i: i ^ 1)

    def after(value, *others):
        return lax.optimization_barrier((value, *others))[0]

    embedding, steps = lax.optimization_barrier(
        (level_embedding(levels, time_weight.shape[0] // 2), level_steps(levels))
    )
    w_key, w_value, w_query, w_out, mods = fetch(
        (w_key, w_value, w_query, w_out), embedding, time_weight
    )
    weights = (w_key, w_value, w_query)

    groups = ((0, None), (1, 3), (2,))
    own = {0: latents, None: fresh_noise}
    for slot in (3, 1, 2):
        own[slot] = from_section(latents, slot)
    parts = {slot: [own[slot], chip_swap(own[slot], slot)] for slot in (0, None, 3)}
    parts[1] = [own[1], from_section(parts[0][1], 1)]
    mine, theirs, q = {}, {}, {}

    def work(group):
        mine[group], q[group] = project(where, group, [parts[x] for x in group], mods, weights)
        theirs[group] = core_swap(mine[group])

    work(groups[0])
    own[2] = after(own[2], own[3], mine[groups[0]])
    parts[2] = [own[2], chip_swap(own[2], 2)]
    work(groups[1])
    early = groups[:-1]
    placed = place(
        where, early, [mine[g] for g in early], [theirs[groups[0]]], [q[g] for g in early],
        [parts[x] for g in early for x in g if x is not None],
    )
    parts[2][1] = after(parts[2][1], *placed)
    work(groups[2])
    all_mine, all_theirs = [mine[g] for g in groups], [theirs[g] for g in groups]
    begun = begin_first(
        where, groups, placed, theirs[groups[1]], q[groups[2]], parts[groups[2][0]]
    )
    stepped, velocity, mine2, own2, old = finish_first(
        where, steps, groups, all_mine, all_theirs, begun, mods, w_key, w_value, w_out
    )
    theirs2 = core_swap(mine2)
    first = groups[0]
    begun = begin_second(
        where, own2, w_query, mine2, q[first], mine[first], theirs[first],
        first.index(None) * 2 * latents.shape[0],
    )
    return finish_second(where, steps, begun, theirs2, old, fresh_noise, w_out, stepped, velocity)


def solution(mesh):
    per_section = mesh.shape["tok"] // SECTIONS
    on_chips = per_section == 2 * CORES
    rows = P(("groups", "tok"), None)
    return jax.shard_map(
        chip_body if on_chips else gathered_body,
        mesh=mesh,
        in_specs=(rows, rows, P(), P(), P(), P(), P(), P()),
        out_specs=(P(None, ("groups", "tok"), None), P(None, ("groups", "tok"), None)),
        check_vma=False,
    )
```

```python
import functools
import math

import jax
import jax.numpy as jnp
from jax import lax
from jax.experimental import pallas as pl
from jax.experimental.pallas import tpu as pltpu
from jax.sharding import PartitionSpec as P


HEAD_DIM = 128
SECTIONS = 4
CORES = 2

epsilon = 1e-06


def permuted(block, axis, move):
    devices = range(lax.axis_size(axis))
    route = [(i, move(i)) for i in devices if move(i) is not None and move(i) in devices]
    return lax.ppermute(block, axis, route)


def level_embedding(levels, half_width):
    frequency = jnp.exp(-math.log(10000.0) * jnp.arange(half_width, dtype=jnp.float32) / half_width)
    angles = levels.astype(jnp.float32)[:, None] * frequency[None, :]
    return jnp.concatenate([jnp.cos(angles), jnp.sin(angles)], axis=1)


def embed_levels(levels, time_weight):
    return jnp.dot(
        level_embedding(levels, time_weight.shape[0] // 2),
        time_weight.astype(jnp.float32),
        precision=lax.Precision.HIGHEST,
    )


def level_steps(levels):
    previous = jnp.concatenate([jnp.zeros((1,), jnp.int32), levels[:-1]])
    return (previous - levels).astype(jnp.float32) / 1000.0


def gathered_body(latents, fresh_noise, levels, time_weight, w_query, w_key, w_value, w_out):
    local_rows = latents.shape[0]
    heads = w_query.shape[1] // HEAD_DIM
    per_section = lax.axis_size("tok") // SECTIONS
    span_rows = local_rows * per_section
    my_block = lax.axis_index("tok") // per_section
    section_ids = jnp.arange(SECTIONS, dtype=jnp.int32)
    mods = embed_levels(levels, time_weight)
    width = mods.shape[1] // 2
    shift_all, scale_all = mods[:, :width], mods[:, width:]
    chosen = section_ids == my_block
    shift_vec = jnp.sum(jnp.where(chosen[:, None], shift_all, 0.0), axis=0)
    scale_vec = jnp.sum(jnp.where(chosen[:, None], scale_all, 0.0), axis=0)
    step_size = jnp.sum(jnp.where(chosen, level_steps(levels), 0.0))

    def denoise_local(rows):
        rows_f = rows.astype(jnp.float32)
        normed = rows_f * lax.rsqrt(jnp.mean(rows_f * rows_f, axis=-1, keepdims=True) + epsilon)
        hidden = (normed * (1.0 + scale_vec) + shift_vec).astype(jnp.bfloat16)

        def project(weight):
            return jnp.dot(hidden, weight, preferred_element_type=jnp.float32).astype(jnp.bfloat16)

        queries = project(w_query).reshape(local_rows, heads, HEAD_DIM)
        keys = lax.all_gather(project(w_key), "tok", axis=0, tiled=True)
        values = lax.all_gather(project(w_value), "tok", axis=0, tiled=True)
        count = keys.shape[0]
        allowed = (jnp.arange(count, dtype=jnp.int32) // span_rows <= my_block)[None, None, :]
        scores = jnp.einsum(
            "rhd,phd->hrp",
            queries,
            keys.reshape(count, heads, HEAD_DIM),
            preferred_element_type=jnp.float32,
        ) / math.sqrt(HEAD_DIM)
        scores = jnp.where(allowed, scores, -1e30)
        best = jnp.max(scores, axis=-1)
        weights = jnp.where(allowed, jnp.exp(scores - best[..., None]), 0.0)
        denominator = jnp.sum(weights, axis=-1)
        summed = jnp.einsum(
            "hrp,phd->hrd",
            weights.astype(jnp.bfloat16),
            values.reshape(count, heads, HEAD_DIM),
            preferred_element_type=jnp.float32,
        )
        attended = (summed / denominator[..., None]).astype(jnp.bfloat16)
        attended = attended.transpose(1, 0, 2).reshape(local_rows, heads * HEAD_DIM)
        moving = jnp.dot(attended, w_out, preferred_element_type=jnp.float32)
        stepped = (rows_f + step_size * moving).astype(jnp.bfloat16)
        return (stepped, moving.astype(jnp.bfloat16))

    first, first_moving = denoise_local(latents)
    incoming = permuted(first, "tok", lambda i: i - per_section)
    second_input = jnp.where(my_block == SECTIONS - 1, fresh_noise, incoming)
    second, second_moving = denoise_local(second_input)
    return (jnp.stack([first, second]), jnp.stack([first_moving, second_moving]))


VMEM = pl.BlockSpec(memory_space=pltpu.VMEM)
SMEM = pl.BlockSpec(memory_space=pltpu.SMEM)
HBM = pl.BlockSpec(memory_space=pltpu.HBM)
LAST = SECTIONS - 1


def modulate(rows_f, scale_row, shift_row):
    normed = rows_f * lax.rsqrt(jnp.mean(rows_f * rows_f, axis=-1, keepdims=True) + epsilon)
    return (normed * (1.0 + scale_row) + shift_row).astype(jnp.bfloat16)


def dot(a, b):
    return jnp.dot(a, b, preferred_element_type=jnp.float32)


SHARPNESS = math.log2(math.e) / math.sqrt(HEAD_DIM)


def score(queries, pairs):
    return [
        lax.dot_general(queries(), keys(), (((1,), (1,)), ((), ())), preferred_element_type=jnp.float32)
        for keys, _ in pairs
    ]


def weigh(scores, pairs, state=None):
    top = functools.reduce(jnp.maximum, [jnp.max(s, axis=-1, keepdims=True) for s in scores])
    rows = top.shape[0]
    top = jnp.broadcast_to(top, (rows, HEAD_DIM))
    if state is not None:
        old_top, old_total, old_summed = state()
        top = jnp.maximum(top, old_top)
    total, summed = 0.0, 0.0
    for part, (_, values) in zip(scores, pairs):
        rounded = []
        sums = []
        for low in range(0, part.shape[1], HEAD_DIM):
            piece = part[:, low : low + HEAD_DIM]
            weights = jnp.exp2((piece - top[:, : piece.shape[1]]) * SHARPNESS)
            sums.append(jnp.sum(weights, axis=-1, keepdims=True) if piece.shape[1] < HEAD_DIM else weights)
            rounded.append(weights.astype(jnp.bfloat16))
        full = [w for w in sums if w.shape[1] == HEAD_DIM]
        for w in [functools.reduce(jnp.add, full)] * (len(full) > 0) + [w for w in sums if w.shape[1] < HEAD_DIM]:
            total = total + jnp.sum(w, axis=-1, keepdims=True)
        summed = summed + dot(jnp.concatenate(rounded, axis=1), values())
    total = jnp.broadcast_to(total, (rows, HEAD_DIM))
    if state is not None:
        fade = jnp.exp2((old_top - top) * SHARPNESS)
        total, summed = old_total * fade + total, old_summed * fade + summed
    return top, total, summed


AHEAD = 3


def attend_all(jobs):
    pending = [score(*job[:2]) for job in jobs[:AHEAD]]
    for i, (_, pairs, state, emit) in enumerate(jobs):
        if i + AHEAD < len(jobs):
            pending.append(score(*jobs[i + AHEAD][:2]))
        emit(*weigh(pending.pop(0), pairs, state))


def view(ref, *where):
    return lambda: ref[where]


def head_columns(width):
    for head in range(width // HEAD_DIM):
        yield slice(head * HEAD_DIM, (head + 1) * HEAD_DIM), slice(
            width + head * HEAD_DIM, width + (head + 1) * HEAD_DIM
        )


def fetch_kernel(*refs, count):
    sources, embedding_ref, time_hbm = refs[:count], refs[count], refs[count + 1]
    outs, mods_ref = refs[count + 2 : 2 * count + 2], refs[2 * count + 2]
    time_ref, sem = refs[2 * count + 3 :]
    time_copy = pltpu.make_async_copy(time_hbm, time_ref, sem.at[count])
    time_copy.start()
    copies = [pltpu.make_async_copy(sources[i], outs[i], sem.at[i]) for i in range(count)]
    for c in copies:
        c.start()
    rest = embedding_ref[...]
    modulated = None
    time_copy.wait()
    for _ in range(3):
        term = rest.astype(jnp.bfloat16)
        rest = rest - term.astype(jnp.float32)
        product = dot(term, time_ref[...])
        modulated = product if modulated is None else modulated + product
    mods_ref[...] = modulated
    for c in copies:
        c.wait()


def fetch(arrays, embedding, time_weight):
    in_hbm = [pltpu.with_memory_space_constraint(a, pltpu.HBM) for a in (*arrays, time_weight)]
    return pl.pallas_call(
        functools.partial(fetch_kernel, count=len(arrays)),
        out_shape=[jax.ShapeDtypeStruct(a.shape, a.dtype) for a in arrays]
        + [jax.ShapeDtypeStruct((embedding.shape[0], time_weight.shape[1]), jnp.float32)],
        in_specs=[HBM] * len(arrays) + [VMEM, HBM],
        out_specs=[VMEM] * (len(arrays) + 1),
        scratch_shapes=[
            pltpu.VMEM(time_weight.shape, time_weight.dtype),
            pltpu.SemaphoreType.DMA((len(arrays) + 1,)),
        ],
        compiler_params=pltpu.CompilerParams(vmem_limit_bytes=6 << 20),
        cost_estimate=pl.CostEstimate(
            flops=0, bytes_accessed=sum(a.size * 2 for a in arrays), transcendentals=0
        ),
        name="fetch",
    )(*in_hbm[:-1], embedding, in_hbm[-1])


def project_kernel(where, *refs, slots, counts):
    refs = list(refs)
    parts = [[refs.pop(0) for _ in range(n)] for n in counts]
    mods_ref, wk_ref, wv_ref, wq_ref, kv_ref, q_ref = refs
    depth, width = wk_ref.shape
    hidden = []
    for i, slot in enumerate(slots):
        rows_f = jnp.concatenate([part[...].astype(jnp.float32) for part in parts[i]])
        section = LAST if slot is None else where[0] ^ slot
        row = mods_ref[pl.ds(section, 1), :]
        hidden.append(modulate(rows_f, row[:, depth:], row[:, :depth]))
    hidden = jnp.concatenate(hidden)
    kv_ref[:, :width] = dot(hidden, wk_ref[...]).astype(jnp.bfloat16)
    kv_ref[:, width:] = dot(hidden, wv_ref[...]).astype(jnp.bfloat16)
    q_ref[...] = dot(hidden, wq_ref[...]).astype(jnp.bfloat16)


def project(where, slots, parts, mods, weights):
    args = [p for rows in parts for p in rows]
    depth, width = weights[0].shape
    rows = sum(p.shape[0] for p in args)
    return pl.pallas_call(
        functools.partial(project_kernel, slots=slots, counts=[len(p) for p in parts]),
        out_shape=(
            jax.ShapeDtypeStruct((rows, 2 * width), jnp.bfloat16),
            jax.ShapeDtypeStruct((rows, width), jnp.bfloat16),
        ),
        in_specs=[SMEM] + [VMEM] * (len(args) + 4),
        out_specs=(VMEM, VMEM),
        compiler_params=pltpu.CompilerParams(vmem_limit_bytes=12 << 20),
        cost_estimate=pl.CostEstimate(
            flops=6 * rows * depth * width, bytes_accessed=2 << 20, transcendentals=0
        ),
        name="project",
    )(where, *args, mods, *weights)


def state_shapes(rows, width):
    stat = jax.ShapeDtypeStruct((width // HEAD_DIM, rows, HEAD_DIM), jnp.float32)
    return stat, stat, jax.ShapeDtypeStruct((rows, width), jnp.float32)


def split(refs, *counts):
    refs = list(refs)
    return [[refs.pop(0) for _ in range(n)] for n in counts] + refs


def key_place(section, slot):
    source = section ^ slot
    swapped = jnp.where(section == LAST, 1 - source, source)
    return jnp.where(source > 1, source - 1, jnp.where(swapped == 1, 0, LAST))


def set_keys(kv_ref, section, slot, offset, block):
    base = key_place(section, slot) * (kv_ref.shape[0] // SECTIONS) + offset
    kv_ref[pl.ds(pl.multiple_of(base, 16), block.shape[0]), :] = block


def set_rows(x_ref, q_ref, section, slot, parts, queries):
    half = q_ref.shape[0] // SECTIONS
    base = pl.multiple_of((section ^ slot) * half, half)
    q_ref[pl.ds(base, half), :] = queries
    low = 0
    for part in parts:
        x_ref[pl.ds(pl.multiple_of(base + low, 8), part.shape[0]), :] = part[...].astype(jnp.float32)
        low += part.shape[0]


def place_kernel(where, *refs, groups, swapped):
    slots = [slot for group in groups for slot in group if slot is not None]
    kv_mine, kv_theirs, q_in, *refs = split(refs, len(groups), swapped, len(groups))
    *x_in, out = split(refs, *[2] * len(slots), 3)
    kv_ref, x_ref, q_ref = out
    half = q_ref.shape[0] // SECTIONS
    section = where[0]
    for g, group in enumerate(groups):
        for i, slot in enumerate(group):
            if slot is None:
                continue
            rows = slice(i * half, (i + 1) * half)
            set_rows(x_ref, q_ref, section, slot, x_in[slots.index(slot)], q_in[g][rows, :])
            set_keys(kv_ref, section, slot, 0, kv_mine[g][rows, :])
            if g < swapped:
                set_keys(kv_ref, section, slot, half, kv_theirs[g][rows, :])

    @pl.when(section == 0)
    def _():
        q_ref[LAST * half :, :] = q_ref[0:half, :]
        x_ref[LAST * half :, :] = x_ref[0:half, :]


def place(where, groups, kv_mine, kv_theirs, q, parts):
    local, depth = parts[0][0].shape
    half, width = 2 * local, q[0].shape[1]
    args = [*kv_mine, *kv_theirs, *q, *(p for rows in parts for p in rows)]
    return pl.pallas_call(
        functools.partial(place_kernel, groups=groups, swapped=len(kv_theirs)),
        out_shape=(
            jax.ShapeDtypeStruct((SECTIONS * 2 * half, 2 * width), jnp.bfloat16),
            jax.ShapeDtypeStruct((SECTIONS * half, depth), jnp.float32),
            jax.ShapeDtypeStruct((SECTIONS * half, width), jnp.bfloat16),
        ),
        in_specs=[SMEM] + [VMEM] * len(args),
        out_specs=(VMEM,) * 3,
        compiler_params=pltpu.CompilerParams(vmem_limit_bytes=4 << 20),
        cost_estimate=pl.CostEstimate(flops=0, bytes_accessed=4 << 20, transcendentals=0),
        name="place",
    )(where, *args)


def begin_kernel(where, theirs_ref, late_q_ref, own_ref, across_ref, kv_in, x_in, q_in,
                 kv_ref, x_ref, q_ref, top_ref, total_ref, sum_ref, *, groups):
    half = q_ref.shape[0] // SECTIONS
    span = 2 * half
    width = q_ref.shape[1]
    section = where[0]
    for i, slot in enumerate(groups[1]):
        set_keys(kv_ref, section, slot, half, theirs_ref[i * half : (i + 1) * half, :])
    set_rows(x_ref, q_ref, section, groups[2][0], (own_ref, across_ref), late_q_ref[...])
    jobs = []
    for s in range(1, SECTIONS):
        rows, seen = slice((s - 1) * half, s * half), slice(0, s * span)
        for head, (cols, v_cols) in enumerate(head_columns(width)):

            def emit(top, total, summed, head=head, rows=rows, cols=cols):
                top_ref[head, rows, :] = top
                total_ref[head, rows, :] = total
                sum_ref[rows, cols] = summed

            queries = view(q_ref, slice(s * half, (s + 1) * half), cols)
            jobs.append((queries, [(view(kv_ref, seen, cols), view(kv_ref, seen, v_cols))], None, emit))
    attend_all(jobs)

    @pl.when(section == 0)
    def _():
        rows = slice((LAST - 1) * half, LAST * half)
        top_ref[:, rows, :] = jnp.full((width // HEAD_DIM, half, HEAD_DIM), -1e30, jnp.float32)
        total_ref[:, rows, :] = jnp.zeros((width // HEAD_DIM, half, HEAD_DIM), jnp.float32)
        sum_ref[rows, :] = jnp.zeros((half, width), jnp.float32)


def begin_first(where, groups, placed, theirs, late_q, late_parts):
    half, width = placed[2].shape[0] // SECTIONS, late_q.shape[1]
    same = [jax.ShapeDtypeStruct(p.shape, p.dtype) for p in placed]
    return pl.pallas_call(
        functools.partial(begin_kernel, groups=groups),
        out_shape=(*same, *state_shapes(LAST * half, width)),
        in_specs=[SMEM] + [VMEM] * 7,
        out_specs=(VMEM,) * 6,
        input_output_aliases={5: 0, 6: 1, 7: 2},
        compiler_params=pltpu.CompilerParams(vmem_limit_bytes=12 << 20),
        cost_estimate=pl.CostEstimate(
            flops=24 * half * 2 * half * width, bytes_accessed=2 << 20, transcendentals=0
        ),
        name="begin_first",
    )(where, theirs, late_q, *late_parts, *placed)[1:]


def finish_kernel(where, steps, *refs, groups):
    known = len(groups)
    kv_mine, kv_theirs, refs_q = split(refs, known, known, 5)[:3]
    refs = list(refs)[2 * known + 5 :]
    x_ref, q_ref, top_ref, total_ref, sum_ref = refs_q
    mods_ref, wk_ref, wv_ref, wo_ref = refs[:4]
    stepped_hbm, velocity_hbm, kv2_ref, own2_ref, next_ref = refs[4:9]
    late_ref, o_ref, v_ref, st_ref, hid_ref, out_ref, sem = refs[9:]
    local, depth = next_ref.shape
    half = 2 * local
    width = wk_ref.shape[1]
    section = where[0]

    def set_late(slot):
        for g, group in enumerate(groups):
            if slot in group:
                rows = slice(group.index(slot) * half, (group.index(slot) + 1) * half)
                late_ref[0:half, :] = kv_mine[g][rows, :]
                late_ref[half:, :] = kv_theirs[g][rows, :]

    for s in range(LAST):
        pl.when(section == s)(functools.partial(set_late, s))
    pl.when(section == LAST)(functools.partial(set_late, LAST ^ 1))

    everything = slice(None)
    jobs = []
    for head, (cols, v_cols) in enumerate(head_columns(width)):

        def emit(_, total, summed, cols=cols):
            o_ref[:, cols] = (summed / total).astype(jnp.bfloat16)

        def state(head=head, cols=cols):
            return top_ref[head], total_ref[head], sum_ref[:, cols]

        pairs = [(view(late_ref, everything, cols), view(late_ref, everything, v_cols))]
        jobs.append((view(q_ref, slice(half, SECTIONS * half), cols), pairs, state, emit))
    attend_all(jobs)
    v_ref[...] = dot(o_ref[...], wo_ref[...])
    for s in range(1, SECTIONS):
        rows = slice((s - 1) * half, s * half)
        step = steps[jnp.where(section == 0, 0, LAST)] if s == LAST else steps[s]
        stepped = (x_ref[s * half : (s + 1) * half, :] + step * v_ref[rows, :]).astype(jnp.bfloat16)
        st_ref[rows, :] = stepped
        hid_ref[rows, :] = modulate(
            stepped.astype(jnp.float32), mods_ref[s - 1 : s, depth:], mods_ref[s - 1 : s, :depth]
        )

    base = pl.multiple_of((jnp.where(section == 0, LAST, section) - 1) * half, half)
    out_ref[0] = st_ref[pl.ds(base, half), :][:local]
    out_ref[1] = v_ref[pl.ds(base, half), :][:local].astype(jnp.bfloat16)
    copies = [
        pltpu.make_async_copy(out_ref.at[0], stepped_hbm.at[0], sem.at[0]),
        pltpu.make_async_copy(out_ref.at[1], velocity_hbm.at[0], sem.at[1]),
    ]
    for c in copies:
        c.start()
    base = pl.multiple_of(jnp.minimum(section, LAST - 1) * half, half)
    own2_ref[...] = hid_ref[pl.ds(base, half), :][:local]
    next_ref[...] = st_ref[pl.ds(base, half), :][:local]
    kv2_ref[:, :width] = dot(hid_ref[...], wk_ref[...]).astype(jnp.bfloat16)
    kv2_ref[:, width:] = dot(hid_ref[...], wv_ref[...]).astype(jnp.bfloat16)
    for c in copies:
        c.wait()


def finish_first(where, steps, groups, kv_mine, kv_theirs, begun, mods, w_key, w_value, w_out):
    depth, width = w_key.shape
    half = begun[0].shape[0] // SECTIONS
    local = half // 2
    pair = jax.ShapeDtypeStruct((2, local, depth), jnp.bfloat16)
    one = jax.ShapeDtypeStruct((local, depth), jnp.bfloat16)
    args = [*kv_mine, *kv_theirs, *begun, mods, w_key, w_value, w_out]
    return pl.pallas_call(
        functools.partial(finish_kernel, groups=groups),
        out_shape=(pair, pair, jax.ShapeDtypeStruct((LAST * half, 2 * width), jnp.bfloat16), one, one),
        in_specs=[SMEM, SMEM] + [VMEM] * len(args),
        out_specs=(HBM, HBM, VMEM, VMEM, VMEM),
        scratch_shapes=[
            pltpu.VMEM((2 * half, 2 * width), jnp.bfloat16),
            pltpu.VMEM((LAST * half, width), jnp.bfloat16),
            pltpu.VMEM((LAST * half, depth), jnp.float32),
            pltpu.VMEM((LAST * half, depth), jnp.bfloat16),
            pltpu.VMEM((LAST * half, depth), jnp.bfloat16),
            pltpu.VMEM((2, local, depth), jnp.bfloat16),
            pltpu.SemaphoreType.DMA((2,)),
        ],
        compiler_params=pltpu.CompilerParams(vmem_limit_bytes=18 << 20),
        cost_estimate=pl.CostEstimate(
            flops=8 * LAST * half * depth * width, bytes_accessed=4 << 20, transcendentals=0
        ),
        name="finish_first",
    )(where, steps, *args)


def begin_second_kernel(
    where, own_ref, wq_ref, mine_ref, fresh_q_ref, fresh_mine_ref, fresh_theirs_ref,
    q_ref, top_ref, total_ref, sum_ref, *, fresh_row,
):
    local, width = q_ref.shape
    half = 2 * local
    section = where[0]

    def run(seen):
        jobs = []
        for head, (cols, v_cols) in enumerate(head_columns(width)):

            def emit(top, total, summed, head=head, cols=cols):
                top_ref[head], total_ref[head], sum_ref[:, cols] = top, total, summed

            pairs = [(view(r, rows, cols), view(r, rows, v_cols)) for r, rows in seen]
            jobs.append((view(q_ref, slice(None), cols), pairs, None, emit))
        attend_all(jobs)

    for s in range(LAST):

        @pl.when(section == s)
        def _():
            q_ref[...] = dot(own_ref[...], wq_ref[...]).astype(jnp.bfloat16)
            run([(mine_ref, slice(0, (s + 1) * half))])

    @pl.when(section == LAST)
    def _():
        fresh_rows = slice(fresh_row, fresh_row + half)
        q_ref[...] = fresh_q_ref[fresh_row : fresh_row + local, :]
        run([(mine_ref, slice(0, LAST * half)), (fresh_mine_ref, fresh_rows), (fresh_theirs_ref, fresh_rows)])


def begin_second(where, own2, w_query, mine2, fresh_q, fresh_mine, fresh_theirs, fresh_row):
    local, width = own2.shape[0], w_query.shape[1]
    return pl.pallas_call(
        functools.partial(begin_second_kernel, fresh_row=fresh_row),
        out_shape=(jax.ShapeDtypeStruct((local, width), jnp.bfloat16), *state_shapes(local, width)),
        in_specs=[SMEM] + [VMEM] * 6,
        out_specs=(VMEM,) * 4,
        compiler_params=pltpu.CompilerParams(vmem_limit_bytes=8 << 20),
        cost_estimate=pl.CostEstimate(
            flops=4 * local * own2.shape[1] * width, bytes_accessed=2 << 20, transcendentals=0
        ),
        name="begin_second",
    )(where, own2, w_query, mine2, fresh_q, fresh_mine, fresh_theirs)


def finish_second_kernel(
    where, steps, q_ref, top_ref, total_ref, sum_ref, theirs_ref, old_ref, fresh_ref, wo_ref, _s, _v,
    stepped_hbm, velocity_hbm, o_ref, x_ref, out_ref, sem,
):
    local, width = q_ref.shape
    section = where[0]

    def run(seen):
        jobs = []
        for head, (cols, v_cols) in enumerate(head_columns(width)):

            def emit(_, total, summed, cols=cols):
                o_ref[:, cols] = (summed / total).astype(jnp.bfloat16)

            def state(head=head, cols=cols):
                return top_ref[head], total_ref[head], sum_ref[:, cols]

            pairs = [(view(theirs_ref, slice(0, seen), cols), view(theirs_ref, slice(0, seen), v_cols))]
            jobs.append((view(q_ref, slice(None), cols), pairs, state, emit))
        attend_all(jobs)

    for s in range(LAST):
        reached = (section >= s) if s == LAST - 1 else (section == s)
        pl.when(reached)(functools.partial(run, (s + 1) * 2 * local))
    x_ref[...] = old_ref[...]

    @pl.when(section == LAST)
    def _():
        x_ref[...] = fresh_ref[...]

    moving = dot(o_ref[...], wo_ref[...])
    out_ref[0] = (x_ref[...].astype(jnp.float32) + steps[section] * moving).astype(jnp.bfloat16)
    out_ref[1] = moving.astype(jnp.bfloat16)
    copies = [
        pltpu.make_async_copy(out_ref.at[0], stepped_hbm.at[1], sem.at[0]),
        pltpu.make_async_copy(out_ref.at[1], velocity_hbm.at[1], sem.at[1]),
    ]
    for c in copies:
        c.start()
    for c in copies:
        c.wait()


def finish_second(where, steps, begun, theirs2, old, fresh, w_out, stepped, velocity):
    local, width = begun[0].shape
    pair = jax.ShapeDtypeStruct(stepped.shape, stepped.dtype)
    return pl.pallas_call(
        finish_second_kernel,
        out_shape=(pair, pair),
        in_specs=[SMEM, SMEM] + [VMEM] * 8 + [HBM, HBM],
        out_specs=(HBM, HBM),
        scratch_shapes=[
            pltpu.VMEM((local, width), jnp.bfloat16),
            pltpu.VMEM(old.shape, jnp.bfloat16),
            pltpu.VMEM((2, *old.shape), jnp.bfloat16),
            pltpu.SemaphoreType.DMA((2,)),
        ],
        input_output_aliases={10: 0, 11: 1},
        compiler_params=pltpu.CompilerParams(vmem_limit_bytes=8 << 20),
        cost_estimate=pl.CostEstimate(
            flops=4 * local * old.shape[1] * width, bytes_accessed=4 << 20, transcendentals=0
        ),
        name="finish_second",
    )(where, steps, *begun, theirs2, old, fresh, w_out, stepped, velocity)


def chip_body(latents, fresh_noise, levels, time_weight, w_query, w_key, w_value, w_out):
    per_section = lax.axis_size("tok") // SECTIONS
    where = (lax.axis_index("tok") // per_section).astype(jnp.int32).reshape(1)

    def needs(section, source):
        return source <= section + 1

    def from_section(block, slot):
        def move(i):
            section, within = i // per_section, i % per_section
            target = section ^ slot
            return target * per_section + within if needs(target, section) else None

        return permuted(block, "tok", move)

    def chip_swap(block):
        return permuted(block, "tok", lambda i: i ^ CORES)

    def core_swap(block):
        return permuted(block, "tok", lambda i: i ^ 1)

    def after(value, *others):
        return lax.optimization_barrier((value, *others))[0]

    embedding, steps = lax.optimization_barrier(
        (level_embedding(levels, time_weight.shape[0] // 2), level_steps(levels))
    )
    w_key, w_value, w_query, w_out, mods = fetch(
        (w_key, w_value, w_query, w_out), embedding, time_weight
    )
    weights = (w_key, w_value, w_query)

    groups = ((0, None), (1, 3), (2,))
    own = {0: latents, None: fresh_noise}
    for slot in (3, 1, 2):
        own[slot] = from_section(latents, slot)
    parts = {slot: [own[slot], chip_swap(own[slot])] for slot in (0, None, 3)}
    parts[1] = [own[1], chip_swap(own[1])]
    mine, theirs, q = {}, {}, {}

    def work(group):
        mine[group], q[group] = project(where, group, [parts[x] for x in group], mods, weights)
        theirs[group] = core_swap(mine[group])

    work(groups[0])
    own[2] = after(own[2], own[3], mine[groups[0]])
    parts[2] = [own[2], chip_swap(own[2])]
    work(groups[1])
    early = groups[:-1]
    placed = place(
        where, early, [mine[g] for g in early], [theirs[groups[0]]], [q[g] for g in early],
        [parts[x] for g in early for x in g if x is not None],
    )
    parts[2][1] = after(parts[2][1], *placed)
    work(groups[2])
    all_mine, all_theirs = [mine[g] for g in groups], [theirs[g] for g in groups]
    begun = begin_first(
        where, groups, placed, theirs[groups[1]], q[groups[2]], parts[groups[2][0]]
    )
    stepped, velocity, mine2, own2, old = finish_first(
        where, steps, groups, all_mine, all_theirs, begun, mods, w_key, w_value, w_out
    )
    theirs2 = core_swap(mine2)
    first = groups[0]
    begun = begin_second(
        where, own2, w_query, mine2, q[first], mine[first], theirs[first],
        first.index(None) * 2 * latents.shape[0],
    )
    return finish_second(where, steps, begun, theirs2, old, fresh_noise, w_out, stepped, velocity)


def solution(mesh):
    per_section = mesh.shape["tok"] // SECTIONS
    on_chips = per_section == 2 * CORES
    rows = P(("groups", "tok"), None)
    return jax.shard_map(
        chip_body if on_chips else gathered_body,
        mesh=mesh,
        in_specs=(rows, rows, P(), P(), P(), P(), P(), P()),
        out_specs=(P(None, ("groups", "tok"), None), P(None, ("groups", "tok"), None)),
        check_vma=False,
    )
```

```python
import functools
import math

import jax
import jax.numpy as jnp
from jax import lax
from jax.experimental import pallas as pl
from jax.experimental.pallas import tpu as pltpu
from jax.sharding import PartitionSpec as P


HEAD_DIM = 128
SECTIONS = 4
CORES = 2

epsilon = 1e-06


def permuted(block, axis, move):
    devices = range(lax.axis_size(axis))
    route = [(i, move(i)) for i in devices if move(i) is not None and move(i) in devices]
    return lax.ppermute(block, axis, route)


def level_embedding(levels, half_width):
    frequency = jnp.exp(-math.log(10000.0) * jnp.arange(half_width, dtype=jnp.float32) / half_width)
    angles = levels.astype(jnp.float32)[:, None] * frequency[None, :]
    return jnp.concatenate([jnp.cos(angles), jnp.sin(angles)], axis=1)


def embed_levels(levels, time_weight):
    return jnp.dot(
        level_embedding(levels, time_weight.shape[0] // 2),
        time_weight.astype(jnp.float32),
        precision=lax.Precision.HIGHEST,
    )


def level_steps(levels):
    previous = jnp.concatenate([jnp.zeros((1,), jnp.int32), levels[:-1]])
    return (previous - levels).astype(jnp.float32) / 1000.0


def gathered_body(latents, fresh_noise, levels, time_weight, w_query, w_key, w_value, w_out):
    local_rows = latents.shape[0]
    heads = w_query.shape[1] // HEAD_DIM
    per_section = lax.axis_size("tok") // SECTIONS
    span_rows = local_rows * per_section
    my_block = lax.axis_index("tok") // per_section
    section_ids = jnp.arange(SECTIONS, dtype=jnp.int32)
    mods = embed_levels(levels, time_weight)
    width = mods.shape[1] // 2
    shift_all, scale_all = mods[:, :width], mods[:, width:]
    chosen = section_ids == my_block
    shift_vec = jnp.sum(jnp.where(chosen[:, None], shift_all, 0.0), axis=0)
    scale_vec = jnp.sum(jnp.where(chosen[:, None], scale_all, 0.0), axis=0)
    step_size = jnp.sum(jnp.where(chosen, level_steps(levels), 0.0))

    def denoise_local(rows):
        rows_f = rows.astype(jnp.float32)
        normed = rows_f * lax.rsqrt(jnp.mean(rows_f * rows_f, axis=-1, keepdims=True) + epsilon)
        hidden = (normed * (1.0 + scale_vec) + shift_vec).astype(jnp.bfloat16)

        def project(weight):
            return jnp.dot(hidden, weight, preferred_element_type=jnp.float32).astype(jnp.bfloat16)

        queries = project(w_query).reshape(local_rows, heads, HEAD_DIM)
        keys = lax.all_gather(project(w_key), "tok", axis=0, tiled=True)
        values = lax.all_gather(project(w_value), "tok", axis=0, tiled=True)
        count = keys.shape[0]
        allowed = (jnp.arange(count, dtype=jnp.int32) // span_rows <= my_block)[None, None, :]
        scores = jnp.einsum(
            "rhd,phd->hrp",
            queries,
            keys.reshape(count, heads, HEAD_DIM),
            preferred_element_type=jnp.float32,
        ) / math.sqrt(HEAD_DIM)
        scores = jnp.where(allowed, scores, -1e30)
        best = jnp.max(scores, axis=-1)
        weights = jnp.where(allowed, jnp.exp(scores - best[..., None]), 0.0)
        denominator = jnp.sum(weights, axis=-1)
        summed = jnp.einsum(
            "hrp,phd->hrd",
            weights.astype(jnp.bfloat16),
            values.reshape(count, heads, HEAD_DIM),
            preferred_element_type=jnp.float32,
        )
        attended = (summed / denominator[..., None]).astype(jnp.bfloat16)
        attended = attended.transpose(1, 0, 2).reshape(local_rows, heads * HEAD_DIM)
        moving = jnp.dot(attended, w_out, preferred_element_type=jnp.float32)
        stepped = (rows_f + step_size * moving).astype(jnp.bfloat16)
        return (stepped, moving.astype(jnp.bfloat16))

    first, first_moving = denoise_local(latents)
    incoming = permuted(first, "tok", lambda i: i - per_section)
    second_input = jnp.where(my_block == SECTIONS - 1, fresh_noise, incoming)
    second, second_moving = denoise_local(second_input)
    return (jnp.stack([first, second]), jnp.stack([first_moving, second_moving]))


VMEM = pl.BlockSpec(memory_space=pltpu.VMEM)
SMEM = pl.BlockSpec(memory_space=pltpu.SMEM)
HBM = pl.BlockSpec(memory_space=pltpu.HBM)
LAST = SECTIONS - 1


def modulate(rows_f, scale_row, shift_row):
    normed = rows_f * lax.rsqrt(jnp.mean(rows_f * rows_f, axis=-1, keepdims=True) + epsilon)
    return (normed * (1.0 + scale_row) + shift_row).astype(jnp.bfloat16)


def dot(a, b):
    return jnp.dot(a, b, preferred_element_type=jnp.float32)


SHARPNESS = math.log2(math.e) / math.sqrt(HEAD_DIM)


def score(queries, pairs):
    return [
        lax.dot_general(queries(), keys(), (((1,), (1,)), ((), ())), preferred_element_type=jnp.float32)
        for keys, _ in pairs
    ]


def weigh(scores, pairs, state=None):
    top = functools.reduce(jnp.maximum, [jnp.max(s, axis=-1, keepdims=True) for s in scores])
    rows = top.shape[0]
    top = jnp.broadcast_to(top, (rows, HEAD_DIM))
    if state is not None:
        old_top, old_total, old_summed = state()
        top = jnp.maximum(top, old_top)
    total, summed = 0.0, 0.0
    for part, (_, values) in zip(scores, pairs):
        rounded = []
        sums = []
        for low in range(0, part.shape[1], HEAD_DIM):
            piece = part[:, low : low + HEAD_DIM]
            weights = jnp.exp2((piece - top[:, : piece.shape[1]]) * SHARPNESS)
            sums.append(jnp.sum(weights, axis=-1, keepdims=True) if piece.shape[1] < HEAD_DIM else weights)
            rounded.append(weights.astype(jnp.bfloat16))
        full = [w for w in sums if w.shape[1] == HEAD_DIM]
        for w in [functools.reduce(jnp.add, full)] * (len(full) > 0) + [w for w in sums if w.shape[1] < HEAD_DIM]:
            total = total + jnp.sum(w, axis=-1, keepdims=True)
        summed = summed + dot(jnp.concatenate(rounded, axis=1), values())
    total = jnp.broadcast_to(total, (rows, HEAD_DIM))
    if state is not None:
        fade = jnp.exp2((old_top - top) * SHARPNESS)
        total, summed = old_total * fade + total, old_summed * fade + summed
    return top, total, summed


AHEAD = 4


def attend_all(jobs):
    pending = [score(*job[:2]) for job in jobs[:AHEAD]]
    for i, (_, pairs, state, emit) in enumerate(jobs):
        if i + AHEAD < len(jobs):
            pending.append(score(*jobs[i + AHEAD][:2]))
        emit(*weigh(pending.pop(0), pairs, state))


def view(ref, *where):
    return lambda: ref[where]


def head_columns(width):
    for head in range(width // HEAD_DIM):
        yield slice(head * HEAD_DIM, (head + 1) * HEAD_DIM), slice(
            width + head * HEAD_DIM, width + (head + 1) * HEAD_DIM
        )


def fetch_kernel(*refs, count):
    sources, embedding_ref, time_hbm = refs[:count], refs[count], refs[count + 1]
    outs, mods_ref = refs[count + 2 : 2 * count + 2], refs[2 * count + 2]
    time_ref, sem = refs[2 * count + 3 :]
    time_copy = pltpu.make_async_copy(time_hbm, time_ref, sem.at[count])
    time_copy.start()
    copies = [pltpu.make_async_copy(sources[i], outs[i], sem.at[i]) for i in range(count)]
    for c in copies:
        c.start()
    rest = embedding_ref[...]
    modulated = None
    time_copy.wait()
    for _ in range(3):
        term = rest.astype(jnp.bfloat16)
        rest = rest - term.astype(jnp.float32)
        product = dot(term, time_ref[...])
        modulated = product if modulated is None else modulated + product
    mods_ref[...] = modulated
    for c in copies:
        c.wait()


def fetch(arrays, embedding, time_weight):
    in_hbm = [pltpu.with_memory_space_constraint(a, pltpu.HBM) for a in (*arrays, time_weight)]
    return pl.pallas_call(
        functools.partial(fetch_kernel, count=len(arrays)),
        out_shape=[jax.ShapeDtypeStruct(a.shape, a.dtype) for a in arrays]
        + [jax.ShapeDtypeStruct((embedding.shape[0], time_weight.shape[1]), jnp.float32)],
        in_specs=[HBM] * len(arrays) + [VMEM, HBM],
        out_specs=[VMEM] * (len(arrays) + 1),
        scratch_shapes=[
            pltpu.VMEM(time_weight.shape, time_weight.dtype),
            pltpu.SemaphoreType.DMA((len(arrays) + 1,)),
        ],
        compiler_params=pltpu.CompilerParams(vmem_limit_bytes=6 << 20),
        cost_estimate=pl.CostEstimate(
            flops=0, bytes_accessed=sum(a.size * 2 for a in arrays), transcendentals=0
        ),
        name="fetch",
    )(*in_hbm[:-1], embedding, in_hbm[-1])


def project_kernel(where, *refs, slots, counts):
    refs = list(refs)
    parts = [[refs.pop(0) for _ in range(n)] for n in counts]
    mods_ref, wk_ref, wv_ref, wq_ref, kv_ref, q_ref = refs
    depth, width = wk_ref.shape
    hidden = []
    for i, slot in enumerate(slots):
        rows_f = jnp.concatenate([part[...].astype(jnp.float32) for part in parts[i]])
        section = LAST if slot is None else where[0] ^ slot
        row = mods_ref[pl.ds(section, 1), :]
        hidden.append(modulate(rows_f, row[:, depth:], row[:, :depth]))
    hidden = jnp.concatenate(hidden)
    kv_ref[:, :width] = dot(hidden, wk_ref[...]).astype(jnp.bfloat16)
    kv_ref[:, width:] = dot(hidden, wv_ref[...]).astype(jnp.bfloat16)
    q_ref[...] = dot(hidden, wq_ref[...]).astype(jnp.bfloat16)


def project(where, slots, parts, mods, weights):
    args = [p for rows in parts for p in rows]
    depth, width = weights[0].shape
    rows = sum(p.shape[0] for p in args)
    return pl.pallas_call(
        functools.partial(project_kernel, slots=slots, counts=[len(p) for p in parts]),
        out_shape=(
            jax.ShapeDtypeStruct((rows, 2 * width), jnp.bfloat16),
            jax.ShapeDtypeStruct((rows, width), jnp.bfloat16),
        ),
        in_specs=[SMEM] + [VMEM] * (len(args) + 4),
        out_specs=(VMEM, VMEM),
        compiler_params=pltpu.CompilerParams(vmem_limit_bytes=12 << 20),
        cost_estimate=pl.CostEstimate(
            flops=6 * rows * depth * width, bytes_accessed=2 << 20, transcendentals=0
        ),
        name="project",
    )(where, *args, mods, *weights)


def state_shapes(rows, width):
    stat = jax.ShapeDtypeStruct((width // HEAD_DIM, rows, HEAD_DIM), jnp.float32)
    return stat, stat, jax.ShapeDtypeStruct((rows, width), jnp.float32)


def split(refs, *counts):
    refs = list(refs)
    return [[refs.pop(0) for _ in range(n)] for n in counts] + refs


def key_place(section, slot):
    source = section ^ slot
    swapped = jnp.where(section == LAST, 1 - source, source)
    return jnp.where(source > 1, source - 1, jnp.where(swapped == 1, 0, LAST))


def set_keys(kv_ref, section, slot, offset, block):
    base = key_place(section, slot) * (kv_ref.shape[0] // SECTIONS) + offset
    kv_ref[pl.ds(pl.multiple_of(base, 16), block.shape[0]), :] = block


def set_rows(x_ref, q_ref, section, slot, parts, queries):
    half = q_ref.shape[0] // SECTIONS
    base = pl.multiple_of((section ^ slot) * half, half)
    q_ref[pl.ds(base, half), :] = queries
    low = 0
    for part in parts:
        x_ref[pl.ds(pl.multiple_of(base + low, 8), part.shape[0]), :] = part[...].astype(jnp.float32)
        low += part.shape[0]


def place_kernel(where, *refs, groups, swapped):
    slots = [slot for group in groups for slot in group if slot is not None]
    kv_mine, kv_theirs, q_in, *refs = split(refs, len(groups), swapped, len(groups))
    *x_in, out = split(refs, *[2] * len(slots), 3)
    kv_ref, x_ref, q_ref = out
    half = q_ref.shape[0] // SECTIONS
    section = where[0]
    for g, group in enumerate(groups):
        for i, slot in enumerate(group):
            if slot is None:
                continue
            rows = slice(i * half, (i + 1) * half)
            set_rows(x_ref, q_ref, section, slot, x_in[slots.index(slot)], q_in[g][rows, :])
            set_keys(kv_ref, section, slot, 0, kv_mine[g][rows, :])
            if g < swapped:
                set_keys(kv_ref, section, slot, half, kv_theirs[g][rows, :])

    @pl.when(section == 0)
    def _():
        q_ref[LAST * half :, :] = q_ref[0:half, :]
        x_ref[LAST * half :, :] = x_ref[0:half, :]


def place(where, groups, kv_mine, kv_theirs, q, parts):
    local, depth = parts[0][0].shape
    half, width = 2 * local, q[0].shape[1]
    args = [*kv_mine, *kv_theirs, *q, *(p for rows in parts for p in rows)]
    return pl.pallas_call(
        functools.partial(place_kernel, groups=groups, swapped=len(kv_theirs)),
        out_shape=(
            jax.ShapeDtypeStruct((SECTIONS * 2 * half, 2 * width), jnp.bfloat16),
            jax.ShapeDtypeStruct((SECTIONS * half, depth), jnp.float32),
            jax.ShapeDtypeStruct((SECTIONS * half, width), jnp.bfloat16),
        ),
        in_specs=[SMEM] + [VMEM] * len(args),
        out_specs=(VMEM,) * 3,
        compiler_params=pltpu.CompilerParams(vmem_limit_bytes=4 << 20),
        cost_estimate=pl.CostEstimate(flops=0, bytes_accessed=4 << 20, transcendentals=0),
        name="place",
    )(where, *args)


def begin_kernel(where, theirs_ref, late_q_ref, own_ref, across_ref, kv_in, x_in, q_in,
                 kv_ref, x_ref, q_ref, top_ref, total_ref, sum_ref, *, groups):
    half = q_ref.shape[0] // SECTIONS
    span = 2 * half
    width = q_ref.shape[1]
    section = where[0]
    for i, slot in enumerate(groups[1]):
        set_keys(kv_ref, section, slot, half, theirs_ref[i * half : (i + 1) * half, :])
    set_rows(x_ref, q_ref, section, groups[2][0], (own_ref, across_ref), late_q_ref[...])
    jobs = []
    for s in range(1, SECTIONS):
        rows, seen = slice((s - 1) * half, s * half), slice(0, s * span)
        for head, (cols, v_cols) in enumerate(head_columns(width)):

            def emit(top, total, summed, head=head, rows=rows, cols=cols):
                top_ref[head, rows, :] = top
                total_ref[head, rows, :] = total
                sum_ref[rows, cols] = summed

            queries = view(q_ref, slice(s * half, (s + 1) * half), cols)
            jobs.append((queries, [(view(kv_ref, seen, cols), view(kv_ref, seen, v_cols))], None, emit))
    attend_all(jobs)

    @pl.when(section == 0)
    def _():
        rows = slice((LAST - 1) * half, LAST * half)
        top_ref[:, rows, :] = jnp.full((width // HEAD_DIM, half, HEAD_DIM), -1e30, jnp.float32)
        total_ref[:, rows, :] = jnp.zeros((width // HEAD_DIM, half, HEAD_DIM), jnp.float32)
        sum_ref[rows, :] = jnp.zeros((half, width), jnp.float32)


def begin_first(where, groups, placed, theirs, late_q, late_parts):
    half, width = placed[2].shape[0] // SECTIONS, late_q.shape[1]
    same = [jax.ShapeDtypeStruct(p.shape, p.dtype) for p in placed]
    return pl.pallas_call(
        functools.partial(begin_kernel, groups=groups),
        out_shape=(*same, *state_shapes(LAST * half, width)),
        in_specs=[SMEM] + [VMEM] * 7,
        out_specs=(VMEM,) * 6,
        input_output_aliases={5: 0, 6: 1, 7: 2},
        compiler_params=pltpu.CompilerParams(vmem_limit_bytes=12 << 20),
        cost_estimate=pl.CostEstimate(
            flops=24 * half * 2 * half * width, bytes_accessed=2 << 20, transcendentals=0
        ),
        name="begin_first",
    )(where, theirs, late_q, *late_parts, *placed)[1:]


def finish_kernel(where, steps, *refs, groups):
    known = len(groups)
    kv_mine, kv_theirs, refs_q = split(refs, known, known, 5)[:3]
    refs = list(refs)[2 * known + 5 :]
    x_ref, q_ref, top_ref, total_ref, sum_ref = refs_q
    mods_ref, wk_ref, wv_ref, wo_ref = refs[:4]
    stepped_hbm, velocity_hbm, kv2_ref, own2_ref, next_ref = refs[4:9]
    late_ref, o_ref, v_ref, st_ref, hid_ref, out_ref, sem = refs[9:]
    local, depth = next_ref.shape
    half = 2 * local
    width = wk_ref.shape[1]
    section = where[0]

    def set_late(slot):
        for g, group in enumerate(groups):
            if slot in group:
                rows = slice(group.index(slot) * half, (group.index(slot) + 1) * half)
                late_ref[0:half, :] = kv_mine[g][rows, :]
                late_ref[half:, :] = kv_theirs[g][rows, :]

    for s in range(LAST):
        pl.when(section == s)(functools.partial(set_late, s))
    pl.when(section == LAST)(functools.partial(set_late, LAST ^ 1))

    everything = slice(None)
    jobs = []
    for s in range(1, SECTIONS):
        rows = slice((s - 1) * half, s * half)
        for head, (cols, v_cols) in enumerate(head_columns(width)):

            def emit(_, total, summed, cols=cols, rows=rows):
                o_ref[rows, cols] = (summed / total).astype(jnp.bfloat16)

            def state(head=head, cols=cols, rows=rows):
                return top_ref[head, rows, :], total_ref[head, rows, :], sum_ref[rows, cols]

            pairs = [(view(late_ref, everything, cols), view(late_ref, everything, v_cols))]
            jobs.append((view(q_ref, slice(s * half, (s + 1) * half), cols), pairs, state, emit))
    attend_all(jobs)
    v_ref[...] = dot(o_ref[...], wo_ref[...])
    for s in range(1, SECTIONS):
        rows = slice((s - 1) * half, s * half)
        step = steps[jnp.where(section == 0, 0, LAST)] if s == LAST else steps[s]
        stepped = (x_ref[s * half : (s + 1) * half, :] + step * v_ref[rows, :]).astype(jnp.bfloat16)
        st_ref[rows, :] = stepped
        hid_ref[rows, :] = modulate(
            stepped.astype(jnp.float32), mods_ref[s - 1 : s, depth:], mods_ref[s - 1 : s, :depth]
        )

    base = pl.multiple_of((jnp.where(section == 0, LAST, section) - 1) * half, half)
    out_ref[0] = st_ref[pl.ds(base, half), :][:local]
    out_ref[1] = v_ref[pl.ds(base, half), :][:local].astype(jnp.bfloat16)
    copies = [
        pltpu.make_async_copy(out_ref.at[0], stepped_hbm.at[0], sem.at[0]),
        pltpu.make_async_copy(out_ref.at[1], velocity_hbm.at[0], sem.at[1]),
    ]
    for c in copies:
        c.start()
    base = pl.multiple_of(jnp.minimum(section, LAST - 1) * half, half)
    own2_ref[...] = hid_ref[pl.ds(base, half), :][:local]
    next_ref[...] = st_ref[pl.ds(base, half), :][:local]
    kv2_ref[:, :width] = dot(hid_ref[...], wk_ref[...]).astype(jnp.bfloat16)
    kv2_ref[:, width:] = dot(hid_ref[...], wv_ref[...]).astype(jnp.bfloat16)
    for c in copies:
        c.wait()


def finish_first(where, steps, groups, kv_mine, kv_theirs, begun, mods, w_key, w_value, w_out):
    depth, width = w_key.shape
    half = begun[0].shape[0] // SECTIONS
    local = half // 2
    pair = jax.ShapeDtypeStruct((2, local, depth), jnp.bfloat16)
    one = jax.ShapeDtypeStruct((local, depth), jnp.bfloat16)
    args = [*kv_mine, *kv_theirs, *begun, mods, w_key, w_value, w_out]
    return pl.pallas_call(
        functools.partial(finish_kernel, groups=groups),
        out_shape=(pair, pair, jax.ShapeDtypeStruct((LAST * half, 2 * width), jnp.bfloat16), one, one),
        in_specs=[SMEM, SMEM] + [VMEM] * len(args),
        out_specs=(HBM, HBM, VMEM, VMEM, VMEM),
        scratch_shapes=[
            pltpu.VMEM((2 * half, 2 * width), jnp.bfloat16),
            pltpu.VMEM((LAST * half, width), jnp.bfloat16),
            pltpu.VMEM((LAST * half, depth), jnp.float32),
            pltpu.VMEM((LAST * half, depth), jnp.bfloat16),
            pltpu.VMEM((LAST * half, depth), jnp.bfloat16),
            pltpu.VMEM((2, local, depth), jnp.bfloat16),
            pltpu.SemaphoreType.DMA((2,)),
        ],
        compiler_params=pltpu.CompilerParams(vmem_limit_bytes=18 << 20),
        cost_estimate=pl.CostEstimate(
            flops=8 * LAST * half * depth * width, bytes_accessed=4 << 20, transcendentals=0
        ),
        name="finish_first",
    )(where, steps, *args)


def begin_second_kernel(
    where, own_ref, wq_ref, mine_ref, fresh_q_ref, fresh_mine_ref, fresh_theirs_ref,
    q_ref, top_ref, total_ref, sum_ref, *, fresh_row,
):
    local, width = q_ref.shape
    half = 2 * local
    section = where[0]

    def run(seen):
        jobs = []
        for head, (cols, v_cols) in enumerate(head_columns(width)):

            def emit(top, total, summed, head=head, cols=cols):
                top_ref[head], total_ref[head], sum_ref[:, cols] = top, total, summed

            pairs = [(view(r, rows, cols), view(r, rows, v_cols)) for r, rows in seen]
            jobs.append((view(q_ref, slice(None), cols), pairs, None, emit))
        attend_all(jobs)

    for s in range(LAST):

        @pl.when(section == s)
        def _():
            q_ref[...] = dot(own_ref[...], wq_ref[...]).astype(jnp.bfloat16)
            run([(mine_ref, slice(0, (s + 1) * half))])

    @pl.when(section == LAST)
    def _():
        fresh_rows = slice(fresh_row, fresh_row + half)
        q_ref[...] = fresh_q_ref[fresh_row : fresh_row + local, :]
        run([(mine_ref, slice(0, LAST * half)), (fresh_mine_ref, fresh_rows), (fresh_theirs_ref, fresh_rows)])


def begin_second(where, own2, w_query, mine2, fresh_q, fresh_mine, fresh_theirs, fresh_row):
    local, width = own2.shape[0], w_query.shape[1]
    return pl.pallas_call(
        functools.partial(begin_second_kernel, fresh_row=fresh_row),
        out_shape=(jax.ShapeDtypeStruct((local, width), jnp.bfloat16), *state_shapes(local, width)),
        in_specs=[SMEM] + [VMEM] * 6,
        out_specs=(VMEM,) * 4,
        compiler_params=pltpu.CompilerParams(vmem_limit_bytes=8 << 20),
        cost_estimate=pl.CostEstimate(
            flops=4 * local * own2.shape[1] * width, bytes_accessed=2 << 20, transcendentals=0
        ),
        name="begin_second",
    )(where, own2, w_query, mine2, fresh_q, fresh_mine, fresh_theirs)


def finish_second_kernel(
    where, steps, q_ref, top_ref, total_ref, sum_ref, theirs_ref, old_ref, fresh_ref, wo_ref, _s, _v,
    stepped_hbm, velocity_hbm, o_ref, x_ref, out_ref, sem,
):
    local, width = q_ref.shape
    section = where[0]

    def run(seen):
        jobs = []
        for head, (cols, v_cols) in enumerate(head_columns(width)):

            def emit(_, total, summed, cols=cols):
                o_ref[:, cols] = (summed / total).astype(jnp.bfloat16)

            def state(head=head, cols=cols):
                return top_ref[head], total_ref[head], sum_ref[:, cols]

            pairs = [(view(theirs_ref, slice(0, seen), cols), view(theirs_ref, slice(0, seen), v_cols))]
            jobs.append((view(q_ref, slice(None), cols), pairs, state, emit))
        attend_all(jobs)

    for s in range(LAST):
        reached = (section >= s) if s == LAST - 1 else (section == s)
        pl.when(reached)(functools.partial(run, (s + 1) * 2 * local))
    x_ref[...] = old_ref[...]

    @pl.when(section == LAST)
    def _():
        x_ref[...] = fresh_ref[...]

    moving = dot(o_ref[...], wo_ref[...])
    out_ref[0] = (x_ref[...].astype(jnp.float32) + steps[section] * moving).astype(jnp.bfloat16)
    out_ref[1] = moving.astype(jnp.bfloat16)
    copies = [
        pltpu.make_async_copy(out_ref.at[0], stepped_hbm.at[1], sem.at[0]),
        pltpu.make_async_copy(out_ref.at[1], velocity_hbm.at[1], sem.at[1]),
    ]
    for c in copies:
        c.start()
    for c in copies:
        c.wait()


def finish_second(where, steps, begun, theirs2, old, fresh, w_out, stepped, velocity):
    local, width = begun[0].shape
    pair = jax.ShapeDtypeStruct(stepped.shape, stepped.dtype)
    return pl.pallas_call(
        finish_second_kernel,
        out_shape=(pair, pair),
        in_specs=[SMEM, SMEM] + [VMEM] * 8 + [HBM, HBM],
        out_specs=(HBM, HBM),
        scratch_shapes=[
            pltpu.VMEM((local, width), jnp.bfloat16),
            pltpu.VMEM(old.shape, jnp.bfloat16),
            pltpu.VMEM((2, *old.shape), jnp.bfloat16),
            pltpu.SemaphoreType.DMA((2,)),
        ],
        input_output_aliases={10: 0, 11: 1},
        compiler_params=pltpu.CompilerParams(vmem_limit_bytes=8 << 20),
        cost_estimate=pl.CostEstimate(
            flops=4 * local * old.shape[1] * width, bytes_accessed=4 << 20, transcendentals=0
        ),
        name="finish_second",
    )(where, steps, *begun, theirs2, old, fresh, w_out, stepped, velocity)


def chip_body(latents, fresh_noise, levels, time_weight, w_query, w_key, w_value, w_out):
    per_section = lax.axis_size("tok") // SECTIONS
    where = (lax.axis_index("tok") // per_section).astype(jnp.int32).reshape(1)

    def needs(section, source):
        return source <= section + 1

    def from_section(block, slot):
        def move(i):
            section, within = i // per_section, i % per_section
            target = section ^ slot
            return target * per_section + within if needs(target, section) else None

        return permuted(block, "tok", move)

    def chip_swap(block):
        return permuted(block, "tok", lambda i: i ^ CORES)

    def core_swap(block):
        return permuted(block, "tok", lambda i: i ^ 1)

    def after(value, *others):
        return lax.optimization_barrier((value, *others))[0]

    embedding, steps = lax.optimization_barrier(
        (level_embedding(levels, time_weight.shape[0] // 2), level_steps(levels))
    )
    w_key, w_value, w_query, w_out, mods = fetch(
        (w_key, w_value, w_query, w_out), embedding, time_weight
    )
    weights = (w_key, w_value, w_query)

    groups = ((0, None), (1, 3), (2,))
    own = {0: latents, None: fresh_noise}
    for slot in (3, 1, 2):
        own[slot] = from_section(latents, slot)
    parts = {slot: [own[slot], chip_swap(own[slot])] for slot in (0, None, 3)}
    parts[1] = [own[1], from_section(parts[0][1], 1)]
    mine, theirs, q = {}, {}, {}

    def work(group):
        mine[group], q[group] = project(where, group, [parts[x] for x in group], mods, weights)
        theirs[group] = core_swap(mine[group])

    work(groups[0])
    own[2] = after(own[2], own[3], mine[groups[0]])
    parts[2] = [own[2], chip_swap(own[2])]
    work(groups[1])
    early = groups[:-1]
    placed = place(
        where, early, [mine[g] for g in early], [theirs[groups[0]]], [q[g] for g in early],
        [parts[x] for g in early for x in g if x is not None],
    )
    parts[2][1] = after(parts[2][1], *placed)
    work(groups[2])
    all_mine, all_theirs = [mine[g] for g in groups], [theirs[g] for g in groups]
    begun = begin_first(
        where, groups, placed, theirs[groups[1]], q[groups[2]], parts[groups[2][0]]
    )
    stepped, velocity, mine2, own2, old = finish_first(
        where, steps, groups, all_mine, all_theirs, begun, mods, w_key, w_value, w_out
    )
    theirs2 = core_swap(mine2)
    first = groups[0]
    begun = begin_second(
        where, own2, w_query, mine2, q[first], mine[first], theirs[first],
        first.index(None) * 2 * latents.shape[0],
    )
    return finish_second(where, steps, begun, theirs2, old, fresh_noise, w_out, stepped, velocity)


def solution(mesh):
    per_section = mesh.shape["tok"] // SECTIONS
    on_chips = per_section == 2 * CORES
    rows = P(("groups", "tok"), None)
    return jax.shard_map(
        chip_body if on_chips else gathered_body,
        mesh=mesh,
        in_specs=(rows, rows, P(), P(), P(), P(), P(), P()),
        out_specs=(P(None, ("groups", "tok"), None), P(None, ("groups", "tok"), None)),
        check_vma=False,
    )
```
